32 devices in a mesh: rows: 8 (over y, x, core), cols: 4 (over z).
Axes of the slice: x: 2, y: 2, z: 4, core: 2. Of those that a mesh axis runs over, the one named last changes fastest.
Arguments:
- terminal_value: float32 [1024, 2048], P('rows', 'cols'), may hold values from -6 to 6
- density_start: float32 [1024, 2048], P('rows', 'cols'), may hold values from 0.2 to 3
- start_cells: int32 [131072], P(('rows', 'cols')), may hold values from 0 to 65535
- offsets: float32 [2, 131072], P(None, ('rows', 'cols')), may hold values from -4 to 4
- weights: float32 [131072], P(('rows', 'cols')), may hold values from 0.3 to 9
- dest_tiles: int32 [1024], P(('rows', 'cols')), may hold values from 0 to 31, as said below
- end_cells: int32 [131072], P(('rows', 'cols')), may hold values from 0 to 65535
Outputs:
- value: float32 [1024, 2048], P('rows', 'cols')
- density: float32 [1024, 2048], P('rows', 'cols')
The draws below stay inside these ranges and needn't reach their ends.
Inputs may be any that keep to these rules, and one draw needn't show every extreme that they name: `dest_tiles`: block b's tile lies in the band of the tile where b starts or in a band next to it. At most 8 blocks that start in one tile go to any one tile, and for every starting tile there is one destination tile that receives exactly 8 of its blocks.
All inputs are finite; a program needn't handle non-finite values.
Results may differ from the reference program's by a relative error of at most 0.0003.
Values sent between devices are 32-bit elements; how exact they have to be, the bound alone decides.
No kernel may reach another device: no remote copies, remote signals or barrier semaphores. Data moves between devices by JAX's collectives and lax.ppermute only.
A program may use at most 64 MiB of HBM per device.

```python
import math
import jax
import jax.numpy as jnp

TR = 128
TC = 512
BLOCK = 128
BLOCKS_DEV = 32
CAP = 8
HJB_STEPS = 4
ITERS = 2
NX = 1024
NY = 2048
AGENTS = 131072
N_ROWS = 8
N_COLS = 4


def draw_weights(key, part):
    agent = jnp.arange(AGENTS, dtype=jnp.int32)
    tile = agent // (BLOCK * BLOCKS_DEV)
    band = tile // N_COLS
    ramp = 1.0 + 2.0 * band.astype(jnp.float32) / (N_ROWS - 1)
    base = jnp.exp(jax.random.uniform(key, (AGENTS,), jnp.float32, jnp.log(0.5), jnp.log(2.0)))
    return (base * ramp).astype(jnp.float32)


def draw_dest_tiles(key, part):
    tile_list = N_ROWS * N_COLS
    choices_count = 3 * N_COLS
    agent_tokens = choices_count * CAP
    random_keys = jax.random.split(jax.random.fold_in(key, 7), 5)
    device = jnp.arange(tile_list, dtype=jnp.int32)
    band = device // N_COLS
    main_band = jnp.clip(band + jax.random.randint(random_keys[0], (tile_list,), -1, 2), 0, N_ROWS - 1)
    main_col = jax.random.randint(random_keys[1], (tile_list,), 0, N_COLS)
    main_pick = (main_band - band + 1) * N_COLS + main_col
    token = jnp.arange(agent_tokens, dtype=jnp.int32)
    pick = token // CAP
    cand_band = band[:, None] + pick[None, :] // N_COLS - 1
    cand_col = jnp.broadcast_to(pick[None, :] % N_COLS, (tile_list, agent_tokens))
    valid = (cand_band >= 0) & (cand_band < N_ROWS)
    candidate_tile = jnp.clip(cand_band, 0, N_ROWS - 1) * N_COLS + cand_col
    preference = jax.random.randint(random_keys[2], (tile_list,), 0, 3)
    reward_extra = preference[candidate_tile] * 400
    tile_rating = jax.random.randint(random_keys[3], (tile_list, agent_tokens), 0, 1024) - reward_extra
    tile_rating = jnp.where(pick[None, :] == main_pick[:, None], -2000, tile_rating)
    tile_rating = jnp.where(valid, tile_rating, 4096)
    tile_rating = (tile_rating + 4096) * agent_tokens + token[None, :]
    order = jnp.argsort(tile_rating, axis=1)[:, :BLOCKS_DEV]
    chosen = jnp.take_along_axis(candidate_tile, order, axis=1)
    mixing = jax.random.randint(random_keys[4], (tile_list, BLOCKS_DEV), 0, 1 << 20) * BLOCKS_DEV
    mixing = mixing + jnp.arange(BLOCKS_DEV, dtype=jnp.int32)[None, :]
    shuffle = jnp.argsort(mixing, axis=1)
    chosen = jnp.take_along_axis(chosen, shuffle, axis=1)
    return chosen.reshape(-1).astype(jnp.int32)


def touch_ends(result, stream_key, smallest, high):
    longest = result.shape.index(max(result.shape))
    spots = []
    for shift in (0, 1):
        where = [jax.random.randint(jax.random.fold_in(stream_key, axis), (), 0, length) for axis, length in enumerate(result.shape)]
        where[longest] = (where[longest] + shift) % result.shape[longest]
        spots.append(tuple(where))
    return result.at[spots[0]].set(smallest).at[spots[1]].set(high)


def block_scale(rng, dims, cuts, low, top_value):
    loudness, own = 1.0, jax.random.fold_in(rng, 6)
    for axis_at, shards_of in cuts:
        steps = jnp.exp(jax.random.uniform(jax.random.fold_in(own, axis_at), (shards_of,), jnp.float32, low / len(cuts), top_value / len(cuts)))
        loudness = loudness * jnp.repeat(steps, dims[axis_at] // shards_of).reshape([-1 if axis == axis_at else 1 for axis in range(len(dims))])
    return loudness


def normal_values(own_key, extent, width, bound, shards=(), kind=jnp.bfloat16):
    array = width * jax.random.normal(own_key, extent, jnp.float32)
    if shards:
        array = array * block_scale(own_key, extent, shards, -0.22, 0.18)
    return jnp.clip(array, -bound, bound).astype(kind)


def setup_inputs(seed: int = 0) -> dict:
    key_list = jax.random.split(jax.random.key(seed), 8)
    return {
        "terminal_value": normal_values(key_list[0], (NX, NY), 1.0, 6.0, ((0, 8), (1, 4)), jnp.float32),
        "density_start": jnp.clip(jnp.exp(math.log(3.0) - 2.7080502 * jax.random.uniform(key_list[1], (NX, NY), jnp.float32) ** block_scale(key_list[1], (NX, NY), ((0, 8), (1, 4)), -0.2, 0.2)), 0.2, 3.0),
        "start_cells": touch_ends(jax.random.randint(key_list[2], (AGENTS,), 0, TR * TC), jax.random.fold_in(key_list[2], 1), 0, (TR * TC) - 1).astype(jnp.int32),
        "offsets": normal_values(key_list[3], (2, AGENTS), 1.0, 4.0, ((1, 32),), jnp.float32),
        "weights": draw_weights(jax.random.fold_in(key_list[7], 71), 0),
        "dest_tiles": draw_dest_tiles(jax.random.fold_in(key_list[7], 71), 0),
        "end_cells": touch_ends(jax.random.randint(key_list[6], (AGENTS,), 0, TR * TC), jax.random.fold_in(key_list[6], 1), 0, (TR * TC) - 1).astype(jnp.int32),
    }


def hjb_step(value, density):
    padded = jnp.pad(value, 1)
    up = padded[:-2, 1:-1]
    down = padded[2:, 1:-1]
    left = padded[1:-1, :-2]
    right = padded[1:-1, 2:]
    back_x = jnp.maximum(value - up, 0.0)
    fore_x = jnp.minimum(down - value, 0.0)
    back_y = jnp.maximum(value - left, 0.0)
    fore_y = jnp.minimum(right - value, 0.0)
    square_x = jnp.maximum(back_x * back_x, fore_x * fore_x)
    square_y = jnp.maximum(back_y * back_y, fore_y * fore_y)
    spread = up + down + left + right - 4.0 * value
    return value + 0.25 * (0.5 * spread - 0.5 * (square_x + square_y) + 0.5 * density)


def reference(terminal_value, density_start, start_cells, offsets, weights, dest_tiles, end_cells):
    per_tile = BLOCK * BLOCKS_DEV
    agent = jnp.arange(AGENTS, dtype=jnp.int32)
    source = agent // per_tile
    row_start = (source // N_COLS) * TR + start_cells // TC
    col_start = (source % N_COLS) * TC + start_cells % TC
    target = jnp.repeat(dest_tiles, BLOCK)
    row_end = (target // N_COLS) * TR + end_cells // TC
    col_end = (target % N_COLS) * TC + end_cells % TC
    row_next = jnp.minimum(row_end + 1, NX - 1).astype(jnp.int32)
    col_next = jnp.minimum(col_end + 1, NY - 1).astype(jnp.int32)
    frac_x = 0.5 + 0.45 * jnp.tanh(offsets[0])
    frac_y = 0.5 + 0.45 * jnp.tanh(offsets[1])
    total = jnp.sum(weights)
    density = density_start
    value = terminal_value
    for outer in range(ITERS):
        value = terminal_value
        for inner in range(HJB_STEPS):
            value = hjb_step(value, density)
        padded = jnp.pad(value, 1)
        corner_a = padded[row_start + 1, col_start + 1]
        corner_b = padded[row_start + 2, col_start + 1]
        corner_c = padded[row_start + 1, col_start + 2]
        corner_d = padded[row_start + 2, col_start + 2]
        grad_x = (1.0 - frac_y) * (corner_b - corner_a) + frac_y * (corner_d - corner_c)
        grad_y = (1.0 - frac_x) * (corner_c - corner_a) + frac_x * (corner_d - corner_b)
        moved_x = 0.5 + 0.45 * jnp.tanh(offsets[0] - grad_x)
        moved_y = 0.5 + 0.45 * jnp.tanh(offsets[1] - grad_y)
        deposit = jnp.zeros((NX, NY), jnp.float32)
        deposit = deposit.at[row_end, col_end].add(weights * (1.0 - moved_x) * (1.0 - moved_y))
        deposit = deposit.at[row_next, col_end].add(weights * moved_x * (1.0 - moved_y))
        deposit = deposit.at[row_end, col_next].add(weights * (1.0 - moved_x) * moved_y)
        deposit = deposit.at[row_next, col_next].add(weights * moved_x * moved_y)
        fresh = deposit * (NX * NY / total)
        density = 0.5 * density + 0.5 * fresh
    return value, density
```

```python
import functools
import jax
import jax.numpy as jnp
from jax import lax
from jax.experimental import pallas as pl
from jax.experimental.pallas import tpu as pltpu
from jax.sharding import PartitionSpec as P

HJB_STEPS = 4
ITERS = 2
F32, BF16, I32 = jnp.float32, jnp.bfloat16, jnp.int32

PAD = 16
EDGE = 8
GROUP = 8


def swap_pairs(count):
    first = [(i, i ^ 1) for i in range(count)]
    second = [(i, ((i + 1) ^ 1) - 1) for i in range(1, count - 1)]
    return first, second


def swap_both(first, second, axis):
    pairs_a, pairs_b = swap_pairs(lax.axis_size(axis))
    return lax.ppermute(first, axis, pairs_a), lax.ppermute(second, axis, pairs_b)


def xor_permute(value, axis, bit):
    return lax.ppermute(value, axis, [(i, i ^ bit) for i in range(lax.axis_size(axis))])


def vmem_call(kernel, out_shape, n_in, scratch=(), smem_in=()):
    in_specs = [
        pl.BlockSpec(memory_space=pltpu.SMEM if i in smem_in else pltpu.VMEM) for i in range(n_in)
    ]
    return pl.pallas_call(
        kernel,
        out_shape=out_shape,
        in_specs=in_specs,
        out_specs=jax.tree.map(lambda _: pl.BlockSpec(memory_space=pltpu.VMEM), out_shape),
        scratch_shapes=list(scratch),
    )


def shape(*dims, dtype=F32):
    return jax.ShapeDtypeStruct(dims, dtype)


def flipped(block):
    rows = block.shape[0]
    width = -(-rows // 128) * 128
    if width > rows:
        block = jnp.concatenate([block, jnp.zeros((width - rows, 128), F32)], axis=0)
    parts = [block[i : i + 128].T for i in range(0, width, 128)]
    return jnp.concatenate(parts, axis=1)


def unflipped(block, rows):
    parts = [block[:, i : i + 128].T for i in range(0, block.shape[1], 128)]
    return jnp.concatenate(parts, axis=0)[:rows]


def pick(flag, one, other):
    return jnp.where(flag, one, other)


def start_mid_kernel(rows, cols, u_ref, m_ref, a_ref, b_ref, ue_ref, me_ref, ca_ref, cb_ref):
    row_even = lax.axis_index("rows") % 2 == 0
    col_even = lax.axis_index("cols") % 2 == 0
    for index, (src, dst) in enumerate(((u_ref, ue_ref), (m_ref, me_ref))):
        dst[...] = jnp.zeros(dst.shape, F32)
        dst[PAD : PAD + rows, 0:cols] = src[...]
        part = slice(index * EDGE, (index + 1) * EDGE)
        north = pick(row_even, b_ref[part, :], a_ref[part, :])
        south = pick(row_even, a_ref[part, :], b_ref[part, :])
        dst[PAD - EDGE : PAD, 0:cols] = north
        dst[PAD + rows : PAD + rows + EDGE, 0:cols] = south
        west_going = flipped(dst[:, 0:128])[0:EDGE]
        east_going = flipped(dst[:, cols - 128 : cols])[128 - EDGE : 128]
        ca_ref[part, :] = pick(col_even, east_going, west_going)
        cb_ref[part, :] = pick(col_even, west_going, east_going)


def side_tile(left, right, width):
    return jnp.concatenate([right, jnp.zeros((128 - 2 * EDGE, width), F32), left], axis=0)


def hjb_sweep(rows, cols, ua, ub, m):
    wide = cols + 128
    n_rows, n_cols = lax.axis_size("rows"), lax.axis_size("cols")
    lane = lax.broadcasted_iota(I32, (8, wide), 1)
    col = jnp.where(lane < cols + 64, lane, lane - wide) + lax.axis_index("cols") * cols
    col_ok = (col >= 0) & (col < cols * n_cols)
    sub = lax.broadcasted_iota(I32, (8, wide), 0)
    row_first = lax.axis_index("rows") * rows
    src, dst = ua, ub
    for step in range(HJB_STEPS):
        for i in range(PAD - 8, PAD + rows + 8, 8):
            value = src[i : i + 8, :]
            up = src[i - 1 : i + 7, :]
            down = src[i + 1 : i + 9, :]
            left = pltpu.roll(value, 1, 1)
            right = pltpu.roll(value, wide - 1, 1)
            back_x = jnp.maximum(value - up, 0.0)
            fore_x = jnp.minimum(down - value, 0.0)
            back_y = jnp.maximum(value - left, 0.0)
            fore_y = jnp.minimum(right - value, 0.0)
            square_x = jnp.maximum(back_x * back_x, fore_x * fore_x)
            square_y = jnp.maximum(back_y * back_y, fore_y * fore_y)
            spread = up + down + left + right - 4.0 * value
            update = 0.5 * spread - 0.5 * (square_x + square_y) + 0.5 * m[i : i + 8, :]
            ok = col_ok
            if i < PAD or i >= PAD + rows:
                row = sub + (row_first + (i - PAD))
                ok = ok & (row >= 0) & (row < rows * n_rows)
            dst[i : i + 8, :] = jnp.where(ok, value + 0.25 * update, 0.0)
        src, dst = dst, src
    return src


def split(value):
    high = value.astype(BF16)
    return high, (value - high.astype(F32)).astype(BF16)


def fill_tables(rows, cols, u, tab):
    wide = cols + 128
    for i in range(0, rows, 16):
        here = u[PAD + i : PAD + i + 16, :]
        below = u[PAD + i + 1 : PAD + i + 17, :]
        d_x = below - here
        d_y = pltpu.roll(here, wide - 1, 1) - here
        d_xy = pltpu.roll(d_x, wide - 1, 1) - d_x
        for index, table in enumerate((d_x, d_y, d_xy)):
            high, low = split(table[:, 0:cols])
            tab[index * rows + i : index * rows + i + 16, :] = high
            tab[(3 + index) * rows + i : (3 + index) * rows + i + 16, :] = low


def sample_moves(
    rows, cols, blocks, cap, first, tab, starts, offs, wts, ends, dest, buf, slot_row, counter
):
    n_cols = lax.axis_size("cols")
    my_row, my_col = lax.axis_index("rows"), lax.axis_index("cols")
    kinds = 4 if first else 2
    part_rows = 3 * kinds * cap + (EDGE if first else 0)
    buf[...] = jnp.zeros(buf.shape, F32)
    for i in range(3 * n_cols):
        counter[i] = 0
    for b in range(blocks):
        tile = dest[b]
        band, column = tile // n_cols, tile % n_cols
        section = jnp.where(band == my_row, 0, jnp.where(band == (my_row ^ 1), 1, 2))
        distance = column ^ my_col
        rank = counter[distance * 3 + section]
        counter[distance * 3 + section] = rank + 1
        slot_row[b] = distance * part_rows + section * (kinds * cap) + rank

    col_iota = lax.broadcasted_iota(I32, (cols, 256), 0)
    row_iota = lax.broadcasted_iota(I32, (rows, 256), 0)

    def step(j, carry):
        def pair(ref):
            return jnp.concatenate([ref[pl.ds(2 * j, 1), :], ref[pl.ds(2 * j + 1, 1), :]], axis=1)

        cell = pair(starts)
        row, col = cell // cols, cell % cols
        lanes = pl.ds(pl.multiple_of(j * 256, 256), 256)
        off_x = offs[0:1, lanes]
        off_y = offs[1:2, lanes]
        hot = jnp.where(col_iota == col, 1.0, 0.0).astype(BF16)
        lines = jnp.dot(tab[...], hot, preferred_element_type=F32)
        row_hit = row_iota == row
        found = []
        for index in range(3):
            line = (
                lines[index * rows : (index + 1) * rows]
                + lines[(3 + index) * rows : (4 + index) * rows]
            )
            found.append(jnp.sum(jnp.where(row_hit, line, 0.0), axis=0, keepdims=True))
        d_x, d_y, d_xy = found
        frac_x = 0.5 + 0.45 * jnp.tanh(off_x)
        frac_y = 0.5 + 0.45 * jnp.tanh(off_y)
        moved_x = 0.5 + 0.45 * jnp.tanh(off_x - (d_x + frac_y * d_xy))
        moved_y = 0.5 + 0.45 * jnp.tanh(off_y - (d_y + frac_x * d_xy))
        out = [moved_x, moved_y]
        if first:
            out += [pair(wts), (pair(ends) + 1).astype(F32)]
        for half in range(2):
            base = slot_row[2 * j + half]
            for q, value in enumerate(out):
                buf[pl.ds(base + q * cap, 1), :] = value[:, half * 128 : (half + 1) * 128]
        return carry

    lax.fori_loop(0, blocks // 2, step, 0)


def first_kernel(
    rows, cols, blocks, cap, n_cols, *refs
):
    (ue_in, me_in, ra_ref, rb_ref, starts, offs, wts, ends, dest) = refs[:9]
    outs = refs[9 : 9 + n_cols]
    ue_ref, me_ref = refs[9 + n_cols : 11 + n_cols]
    ua, ub, tab, buf, slot_row, counter = refs[11 + n_cols :]
    col_even = lax.axis_index("cols") % 2 == 0
    tall = ue_in.shape[0]
    width = ra_ref.shape[1]
    for index, (src, dst) in enumerate(((ue_in, ue_ref), (me_in, me_ref))):
        part = slice(index * EDGE, (index + 1) * EDGE)
        west = pick(col_even, rb_ref[part, :], ra_ref[part, :])
        east = pick(col_even, ra_ref[part, :], rb_ref[part, :])
        dst[:, 0:cols] = src[:, 0:cols]
        dst[:, cols : cols + 128] = unflipped(side_tile(west, east, width), tall)
    ua[...] = ue_ref[...]
    ub[...] = jnp.zeros(ub.shape, F32)
    u = hjb_sweep(rows, cols, ua, ub, me_ref)
    fill_tables(rows, cols, u, tab)
    sample_moves(
        rows, cols, blocks, cap, True, tab, starts, offs, wts, ends, dest, buf, slot_row, counter
    )
    part_rows = 12 * cap + EDGE
    total = jnp.sum(jnp.sum(wts[...], axis=0, keepdims=True), axis=1, keepdims=True)
    for k in range(n_cols):
        outs[k][0 : part_rows - EDGE, :] = buf[k * part_rows : (k + 1) * part_rows - EDGE, :]
        outs[k][part_rows - EDGE :, :] = jnp.broadcast_to(total, (EDGE, 128))


def again_kernel(rows, cols, blocks, cap, n_cols, *refs):
    (ue_ref, m_in, d_ref, ra_ref, rb_ref, total_ref, starts, offs, dest) = refs[:9]
    outs = refs[9 : 9 + n_cols]
    value_ref, density_ref = refs[9 + n_cols : 11 + n_cols]
    ua, ub, m, tab, buf, slot_row, counter = refs[11 + n_cols :]
    col_even = lax.axis_index("cols") % 2 == 0
    n_rows = lax.axis_size("rows")
    tall = ue_ref.shape[0]
    width = ra_ref.shape[1]
    half_scale = 0.5 * ((rows * cols * n_rows * n_cols) / total_ref[0:1, 0:1])
    west = pick(col_even, rb_ref[...], ra_ref[...])
    east = pick(col_even, ra_ref[...], rb_ref[...])
    side = unflipped(side_tile(west[0:EDGE], east[0:EDGE], width), tall)
    pushed = unflipped(
        jnp.concatenate([west[EDGE : 2 * EDGE], jnp.zeros((128 - EDGE, width), F32)], axis=0), tall
    )
    m[:, 0:128] = 0.5 * m_in[:, 0:128] + half_scale * (d_ref[:, 0:128] + pushed)
    m[:, 128:cols] = 0.5 * m_in[:, 128:cols] + half_scale * d_ref[:, 128:cols]
    m[:, cols : cols + 128] = 0.5 * m_in[:, cols : cols + 128] + half_scale * (
        d_ref[:, cols : cols + 128] + side
    )
    density_ref[...] = m[PAD : PAD + rows, 0:cols]
    ua[...] = ue_ref[...]
    ub[...] = jnp.zeros(ub.shape, F32)
    u = hjb_sweep(rows, cols, ua, ub, m)
    value_ref[...] = u[PAD : PAD + rows, 0:cols]
    fill_tables(rows, cols, u, tab)
    sample_moves(
        rows, cols, blocks, cap, False, tab, starts, offs, None, None, dest, buf, slot_row, counter
    )
    part_rows = 6 * cap
    for k in range(n_cols):
        outs[k][...] = buf[k * part_rows : (k + 1) * part_rows, :]


def deposit_grid(rows, cols, cap, chunks, moves, masses, acc, lhs, rhs, slots, grid):
    counts = []
    for q in range(chunks):
        cells = masses[(2 * q + 1) * cap : (2 * q + 2) * cap, :]
        counts.append(jnp.sum(jnp.where(cells > 0.5, 1.0, 0.0)).astype(I32) // 128)
    base = jnp.int32(0)
    for q in range(chunks):
        for rank in range(cap):
            slots[base + rank] = 2 * q * cap + rank
        base = base + counts[q]
    for rank in range(GROUP):
        slots[base + rank] = 2 * chunks * cap
    acc[...] = jnp.zeros(acc.shape, F32)
    row_iota = lax.broadcasted_iota(I32, (rows, 128), 0)
    spill_iota = lax.broadcasted_iota(I32, (16, 128), 0)
    col_iota = lax.broadcasted_iota(I32, (cols, 128), 0)

    def step(g, carry):
        for t in range(GROUP):
            at = slots[g * GROUP + t]
            move_x = moves[pl.ds(at, 1), :]
            move_y = moves[pl.ds(at + cap, 1), :]
            mass = masses[pl.ds(at, 1), :]
            cell = masses[pl.ds(at + cap, 1), :].astype(I32) - 1
            row, col = cell // cols, cell % cols
            stay, go = mass * (1.0 - move_x), mass * move_x
            parts = []
            for factor in (1.0 - move_y, move_y):
                parts.append((split(stay * factor), split(go * factor)))
            lanes = slice(t * 128, (t + 1) * 128)
            here, next_row = row_iota == row, row_iota == row + 1
            last = row == rows - 1
            spill = jnp.zeros((16, 128), F32)
            for side in range(2):
                (stay_pair, go_pair) = parts[side]
                for level in range(2):
                    index = 2 * side + level
                    first, second = stay_pair[level].astype(F32), go_pair[level].astype(F32)
                    lhs[index * rows : (index + 1) * rows, lanes] = jnp.where(
                        here, first, jnp.where(next_row, second, 0.0)
                    ).astype(BF16)
                    spill = jnp.where((spill_iota == index) & last, second, spill)
            lhs[4 * rows : 4 * rows + 16, lanes] = spill.astype(BF16)
            rhs[:, lanes] = jnp.where(col_iota == col, 1.0, 0.0).astype(BF16)
        acc[...] += lax.dot_general(
            lhs[...], rhs[...], (((1,), (1,)), ((), ())), preferred_element_type=F32
        )
        return carry

    lax.fori_loop(0, (base + GROUP - 1) // GROUP, step, 0)

    wide = cols + 128
    lane = lax.broadcasted_iota(I32, (8, wide), 1)

    def join(stay, pushed):
        blank = jnp.zeros((8, 128), F32)
        stay = jnp.concatenate([stay, blank], axis=1)
        pushed = jnp.concatenate([pushed, blank], axis=1)
        return stay + pltpu.roll(pushed, 1, 1)

    for i in range(0, rows, 8):
        grid[i : i + 8, :] = join(
            acc[i : i + 8, :] + acc[rows + i : rows + i + 8, :],
            acc[2 * rows + i : 2 * rows + i + 8, :] + acc[3 * rows + i : 3 * rows + i + 8, :],
        )
    below = acc[4 * rows : 4 * rows + 8, :]
    sub = lax.broadcasted_iota(I32, (8, cols), 0)
    stay = jnp.sum(jnp.where(sub < 2, below, 0.0), axis=0, keepdims=True)
    pushed = jnp.sum(jnp.where((sub >= 2) & (sub < 4), below, 0.0), axis=0, keepdims=True)
    first = lax.broadcasted_iota(I32, (8, cols), 0) == 0
    spilled = join(jnp.where(first, stay, 0.0), jnp.where(first, pushed, 0.0))
    grid[rows : rows + 8, :] = spilled

    @pl.when(lax.axis_index("rows") == lax.axis_size("rows") - 1)
    def _():
        tail = grid[rows - 8 : rows, :]
        sub8 = lax.broadcasted_iota(I32, (8, wide), 0)
        spill_row = jnp.broadcast_to(grid[rows : rows + 1, :], (8, wide))
        grid[rows - 8 : rows, :] = tail + jnp.where(sub8 == 7, spill_row, 0.0)
        grid[rows : rows + 8, :] = jnp.zeros((8, wide), F32)

    @pl.when(lax.axis_index("cols") == lax.axis_size("cols") - 1)
    def _():
        for i in range(0, rows + 8, 8):
            line = grid[i : i + 8, :]
            moved = jnp.where(lane == cols - 1, pltpu.roll(line, wide - 1, 1), 0.0)
            grid[i : i + 8, :] = jnp.where(lane < cols, line + moved, 0.0)


def gather_parts(cap, n_cols, kinds, pieces, ra_ref, rb_ref, groups):
    step = kinds * cap
    for dst, offset in groups:
        size = 2 * cap
        for k in range(n_cols):
            dst[k * size : (k + 1) * size, :] = pieces[k][offset : offset + size, :]
            for index, other in ((1, ra_ref), (2, rb_ref)):
                at = (index * n_cols + k) * size
                dst[at : at + size, :] = other[k * step + offset : k * step + offset + size, :]


def first_deposit_kernel(rows, cols, cap, n_cols, *refs):
    pieces = refs[:n_cols]
    ra_ref, rb_ref = refs[n_cols : n_cols + 2]
    grid, sa_ref, sb_ref, masses = refs[n_cols + 2 : n_cols + 6]
    moves, acc, lhs, rhs, slots = refs[n_cols + 6 :]
    chunks = 3 * n_cols
    gather_parts(
        cap, n_cols, 4, pieces, ra_ref, rb_ref, ((moves, 0), (masses, 2 * cap))
    )
    for ref in (moves, masses):
        ref[2 * cap * chunks :, :] = jnp.zeros((2 * cap, 128), F32)
    deposit_grid(rows, cols, cap, chunks, moves, masses, acc, lhs, rhs, slots, grid)
    row_even = lax.axis_index("rows") % 2 == 0
    south_going = grid[rows - 7 : rows + 1, :]
    north_going = grid[0:8, :]
    sa_ref[...] = pick(row_even, south_going, north_going)
    sb_ref[...] = pick(row_even, north_going, south_going)


def last_deposit_kernel(rows, cols, cap, n_cols, *refs):
    pieces = refs[:n_cols]
    ra_ref, rb_ref, masses = refs[n_cols : n_cols + 3]
    grid, row_ref, col_ref, corner_ref = refs[n_cols + 3 : n_cols + 7]
    moves, acc, lhs, rhs, slots = refs[n_cols + 7 :]
    chunks = 3 * n_cols
    gather_parts(cap, n_cols, 2, pieces, ra_ref, rb_ref, ((moves, 0),))
    moves[2 * cap * chunks :, :] = jnp.zeros((2 * cap, 128), F32)
    deposit_grid(rows, cols, cap, chunks, moves, masses, acc, lhs, rhs, slots, grid)
    row_ref[...] = grid[rows : rows + 8, 0:cols]
    corner_ref[...] = grid[rows : rows + 8, cols : cols + 128]
    col_ref[...] = flipped(grid[0:rows, cols : cols + 128])[0:8]


def edge_mid_kernel(rows, cols, g_ref, a_ref, b_ref, d_ref, ca_ref, cb_ref):
    row_even = lax.axis_index("rows") % 2 == 0
    col_even = lax.axis_index("cols") % 2 == 0
    wide = cols + 128
    north = pick(row_even, b_ref[...], a_ref[...])
    south = pick(row_even, a_ref[...], b_ref[...])
    d_ref[0:PAD, :] = jnp.zeros((PAD, wide), F32)
    d_ref[PAD : PAD + rows, :] = g_ref[0:rows, :]
    d_ref[PAD + rows : PAD + rows + 8, :] = south + g_ref[rows : rows + 8, :]
    d_ref[PAD + rows + 8 :, :] = jnp.zeros((d_ref.shape[0] - PAD - rows - 8, wide), F32)
    d_ref[PAD - 7 : PAD + 1, :] = d_ref[PAD - 7 : PAD + 1, :] + north
    west_going = flipped(d_ref[:, 0:128])[0:EDGE]
    east_going = flipped(d_ref[:, cols - 128 : cols])[128 - EDGE : 128]
    spilled = flipped(d_ref[:, cols : cols + 128])[0:EDGE]
    ca_ref[0:EDGE, :] = pick(col_even, east_going, west_going)
    cb_ref[0:EDGE, :] = pick(col_even, west_going, east_going)
    ca_ref[EDGE:, :] = pick(col_even, spilled, 0.0)
    cb_ref[EDGE:, :] = pick(col_even, 0.0, spilled)


def final_kernel(rows, cols, g_ref, m_ref, row_in, col_in, corner_in, total_ref, out_ref):
    n_rows, n_cols = lax.axis_size("rows"), lax.axis_size("cols")
    half_scale = 0.5 * ((rows * cols * n_rows * n_cols) / total_ref[0:1, 0:1])
    out_ref[...] = 0.5 * m_ref[...] + half_scale * g_ref[0:rows, 0:cols]
    out_ref[0:8, :] = out_ref[0:8, :] + half_scale * row_in[...]
    out_ref[0:8, 0:128] = out_ref[0:8, 0:128] + half_scale * corner_in[...]
    beside = jnp.concatenate([col_in[...], jnp.zeros((120, col_in.shape[1]), F32)], axis=0)
    out_ref[:, 0:128] = out_ref[:, 0:128] + half_scale * unflipped(beside, rows)


def exchange_columns(outs):
    n_cols = len(outs)
    return [outs[0]] + [xor_permute(outs[k], "cols", k) for k in range(1, n_cols)]


def exchange_rows(pieces, kinds, cap, extra=None):
    step = kinds * cap
    first = [piece[step : 2 * step] for piece in pieces]
    second = [piece[2 * step : 3 * step] for piece in pieces]
    if extra is not None:
        first.append(extra)
    return swap_both(jnp.concatenate(first), jnp.concatenate(second), "rows")


def body(terminal_value, density_start, start_cells, offsets, weights, dest_tiles, end_cells):
    rows, cols = terminal_value.shape
    n_rows, n_cols = lax.axis_size("rows"), lax.axis_size("cols")
    blocks = dest_tiles.shape[0]
    cap = blocks // 4
    chunks = 3 * n_cols
    wide, tall = cols + 128, rows + 2 * PAD
    flat = -(-tall // 128) * 128
    starts = start_cells.reshape(blocks, 128)
    wts = weights.reshape(blocks, 128)
    ends = end_cells.reshape(blocks, 128)
    row_even = lax.axis_index("rows") % 2 == 0

    south_going = jnp.concatenate([terminal_value[rows - EDGE :], density_start[rows - EDGE :]])
    north_going = jnp.concatenate([terminal_value[:EDGE], density_start[:EDGE]])
    ra, rb = swap_both(
        jnp.where(row_even, south_going, north_going),
        jnp.where(row_even, north_going, south_going),
        "rows",
    )
    ue, me, ca, cb = vmem_call(
        functools.partial(start_mid_kernel, rows, cols),
        (shape(tall, wide), shape(tall, wide), shape(2 * EDGE, flat), shape(2 * EDGE, flat)),
        4,
    )(terminal_value, density_start, ra, rb)
    ca, cb = swap_both(ca, cb, "cols")
    sweep_scratch = [
        pltpu.VMEM((tall, wide), F32),
        pltpu.VMEM((tall, wide), F32),
    ]

    def sample_scratch(part_rows):
        return [
            pltpu.VMEM((6 * rows, cols), BF16),
            pltpu.VMEM((n_cols * part_rows, 128), F32),
            pltpu.SMEM((blocks,), I32),
            pltpu.SMEM((chunks,), I32),
        ]

    deposit_scratch = [
        pltpu.VMEM((2 * cap * (chunks + 1), 128), F32),
        pltpu.VMEM((4 * rows + 16, cols), F32),
        pltpu.VMEM((4 * rows + 16, GROUP * 128), BF16),
        pltpu.VMEM((cols, GROUP * 128), BF16),
        pltpu.SMEM((chunks * cap + GROUP,), I32),
    ]
    part_rows = 12 * cap + EDGE
    *outs, ue, me = vmem_call(
        functools.partial(first_kernel, rows, cols, blocks, cap, n_cols),
        tuple([shape(part_rows, 128)] * n_cols + [shape(tall, wide)] * 2),
        9,
        sweep_scratch + sample_scratch(part_rows),
        smem_in=(8,),
    )(ue, me, ca, cb, starts, offsets, wts, ends, dest_tiles)
    pieces = exchange_columns(outs)
    total = sum(piece[part_rows - EDGE :] for piece in pieces)
    ra, rb = exchange_rows(pieces, 4, cap, total)
    total = total + ra[4 * n_cols * cap :]
    bit = 2
    while bit < n_rows:
        total = total + xor_permute(total, "rows", bit)
        bit *= 2
    grid, ea, eb, masses = vmem_call(
        functools.partial(first_deposit_kernel, rows, cols, cap, n_cols),
        (
            shape(rows + 8, wide),
            shape(8, wide),
            shape(8, wide),
            shape(2 * cap * (chunks + 1), 128),
        ),
        n_cols + 2,
        deposit_scratch,
    )(*pieces, ra, rb)
    ea, eb = swap_both(ea, eb, "rows")
    deposit, ca, cb = vmem_call(
        functools.partial(edge_mid_kernel, rows, cols),
        (shape(tall, wide), shape(2 * EDGE, flat), shape(2 * EDGE, flat)),
        3,
    )(grid, ea, eb)
    ca, cb = swap_both(ca, cb, "cols")
    part_rows = 6 * cap
    *outs, value, density = vmem_call(
        functools.partial(again_kernel, rows, cols, blocks, cap, n_cols),
        tuple([shape(part_rows, 128)] * n_cols + [shape(rows, cols)] * 2),
        9,
        sweep_scratch + [pltpu.VMEM((tall, wide), F32)] + sample_scratch(part_rows),
        smem_in=(8,),
    )(ue, me, deposit, ca, cb, total, starts, offsets, dest_tiles)
    pieces = exchange_columns(outs)
    ra, rb = exchange_rows(pieces, 2, cap)
    grid, below, beside, corner = vmem_call(
        functools.partial(last_deposit_kernel, rows, cols, cap, n_cols),
        (shape(rows + 8, wide), shape(8, cols), shape(8, rows), shape(8, 128)),
        n_cols + 3,
        deposit_scratch,
    )(*pieces, ra, rb, masses)
    below = lax.ppermute(below, "rows", [(i, i + 1) for i in range(n_rows - 1)])
    beside = lax.ppermute(beside, "cols", [(i, i + 1) for i in range(n_cols - 1)])
    corner = lax.ppermute(
        corner,
        ("rows", "cols"),
        [
            (r * n_cols + c, (r + 1) * n_cols + c + 1)
            for r in range(n_rows - 1)
            for c in range(n_cols - 1)
        ],
    )
    density = vmem_call(functools.partial(final_kernel, rows, cols), shape(rows, cols), 6)(
        grid, density, below, beside, corner, total
    )
    return (value, density)


def solution(mesh):
    in_specs = (
        P("rows", "cols"),
        P("rows", "cols"),
        P(("rows", "cols")),
        P(None, ("rows", "cols")),
        P(("rows", "cols")),
        P(("rows", "cols")),
        P(("rows", "cols")),
    )
    out_specs = (P("rows", "cols"), P("rows", "cols"))
    return jax.shard_map(body, mesh=mesh, in_specs=in_specs, out_specs=out_specs, check_vma=False)
```

```python
import functools
import jax
import jax.numpy as jnp
from jax import lax
from jax.experimental import pallas as pl
from jax.experimental.pallas import tpu as pltpu
from jax.sharding import PartitionSpec as P

HJB_STEPS = 4
ITERS = 2
F32, BF16, I32 = jnp.float32, jnp.bfloat16, jnp.int32

PAD = 16
EDGE = 8
GROUP = 8
UNROLL = 4
VMEM_LIMIT = 24 * 1024 * 1024


def swap_pairs(count):
    first = [(i, i ^ 1) for i in range(count)]
    second = [(i, ((i + 1) ^ 1) - 1) for i in range(1, count - 1)]
    return first, second


def swap_both(first, second, axis):
    pairs_a, pairs_b = swap_pairs(lax.axis_size(axis))
    return lax.ppermute(first, axis, pairs_a), lax.ppermute(second, axis, pairs_b)


def xor_permute(value, axis, bit):
    return lax.ppermute(value, axis, [(i, i ^ bit) for i in range(lax.axis_size(axis))])


def vmem_call(kernel, out_shape, n_in, scratch=(), smem_in=(), keep=()):
    def spec(smem):
        return pl.BlockSpec(memory_space=pltpu.SMEM if smem else pltpu.VMEM)

    results = [
        leaf if i in keep else pltpu.VMEM(leaf.shape, leaf.dtype)
        for i, leaf in enumerate(out_shape)
    ]
    call = pl.pallas_call(
        kernel,
        out_shape=results,
        in_specs=[spec(i in smem_in) for i in range(n_in)],
        out_specs=[spec(False) for _ in results],
        scratch_shapes=list(scratch),
        compiler_params=pltpu.CompilerParams(vmem_limit_bytes=VMEM_LIMIT),
    )

    def run(*operands):
        return call(
            *[
                x if i in smem_in else pltpu.with_memory_space_constraint(x, pltpu.VMEM)
                for i, x in enumerate(operands)
            ]
        )

    return run


def shape(*dims, dtype=F32):
    return jax.ShapeDtypeStruct(dims, dtype)


def flipped(block):
    rows = block.shape[0]
    width = -(-rows // 128) * 128
    if width > rows:
        block = jnp.concatenate([block, jnp.zeros((width - rows, 128), F32)], axis=0)
    parts = [block[i : i + 128].T for i in range(0, width, 128)]
    return jnp.concatenate(parts, axis=1)


def unflipped(block, rows):
    parts = [block[:, i : i + 128].T for i in range(0, block.shape[1], 128)]
    return jnp.concatenate(parts, axis=0)[:rows]


def row_col(cell, cols):
    if cols & (cols - 1) == 0:
        return cell >> (cols.bit_length() - 1), cell & (cols - 1)
    return cell // cols, cell % cols


def pick(flag, one, other):
    return jnp.where(flag, one, other)


def start_mid_kernel(rows, cols, u_ref, m_ref, a_ref, b_ref, ue_ref, me_ref, ca_ref, cb_ref):
    row_even = lax.axis_index("rows") % 2 == 0
    col_even = lax.axis_index("cols") % 2 == 0
    for index, (src, dst) in enumerate(((u_ref, ue_ref), (m_ref, me_ref))):
        dst[...] = jnp.zeros(dst.shape, F32)
        dst[PAD : PAD + rows, 0:cols] = src[...]
        part = slice(index * EDGE, (index + 1) * EDGE)
        north = pick(row_even, b_ref[part, :], a_ref[part, :])
        south = pick(row_even, a_ref[part, :], b_ref[part, :])
        dst[PAD - EDGE : PAD, 0:cols] = north
        dst[PAD + rows : PAD + rows + EDGE, 0:cols] = south
        west_going = flipped(dst[:, 0:128])[0:EDGE]
        east_going = flipped(dst[:, cols - 128 : cols])[128 - EDGE : 128]
        ca_ref[part, :] = pick(col_even, east_going, west_going)
        cb_ref[part, :] = pick(col_even, west_going, east_going)


def side_tile(left, right, width):
    return jnp.concatenate([right, jnp.zeros((128 - 2 * EDGE, width), F32), left], axis=0)


def hjb_sweep(rows, cols, ua, ub, m):
    wide = cols + 128
    tiles = wide // 128
    n_rows, n_cols = lax.axis_size("rows"), lax.axis_size("cols")
    sub = lax.broadcasted_iota(I32, (8, 128), 0)
    lane = lax.broadcasted_iota(I32, (8, 128), 1)
    top, bottom, first, last = sub == 0, sub == 7, lane == 0, lane == 127
    row_first = lax.axis_index("rows") * rows
    col = jnp.where(lane < 64, cols + lane, lane - 128) + lax.axis_index("cols") * cols
    side_ok = (col >= 0) & (col < cols * n_cols)
    src, dst = ua, ub

    def strip(i):
        return [src[i : i + 8, t * 128 : (t + 1) * 128] for t in range(tiles)]

    for step in range(HJB_STEPS):
        start, stop = PAD - 8, PAD + rows + 8
        here = strip(start)
        fell = [pltpu.roll(x, 1, 0) for x in here]
        rose = [pltpu.roll(x, 7, 0) for x in here]
        fell_before = fell
        for i in range(start, stop, 8):
            if i + 8 < stop:
                after = strip(i + 8)
                rose_after = [pltpu.roll(x, 7, 0) for x in after]
                fell_after = [pltpu.roll(x, 1, 0) for x in after]
            else:
                after, rose_after, fell_after = here, rose, fell
            row_ok = None
            if i < PAD or i >= PAD + rows:
                row = sub + (row_first + (i - PAD))
                row_ok = (row >= 0) & (row < rows * n_rows)
            went = [pltpu.roll(x, 1, 1) for x in here]
            came = [pltpu.roll(x, 127, 1) for x in here]
            for t in range(tiles):
                value = here[t]
                up = jnp.where(top, fell_before[t], fell[t])
                down = jnp.where(bottom, rose_after[t], rose[t])
                left = jnp.where(first, went[t - 1], went[t])
                right = jnp.where(last, came[(t + 1) % tiles], came[t])
                slope_x = jnp.maximum(value - jnp.minimum(up, down), 0.0)
                slope_y = jnp.maximum(value - jnp.minimum(left, right), 0.0)
                around = (up + down) + (left + right) + m[i : i + 8, t * 128 : (t + 1) * 128]
                new = 0.5 * value + 0.125 * (around - (slope_x * slope_x + slope_y * slope_y))
                ok = row_ok
                if t == tiles - 1:
                    ok = side_ok if ok is None else ok & side_ok
                dst[i : i + 8, t * 128 : (t + 1) * 128] = (
                    new if ok is None else jnp.where(ok, new, 0.0)
                )
            here, fell_before, fell, rose = after, fell, fell_after, rose_after
        src, dst = dst, src
    return src


def split(value):
    high = value.astype(BF16)
    return high, (value - high.astype(F32)).astype(BF16)


def lane_pick(value, index):
    dims = lax.GatherDimensionNumbers(
        offset_dims=(),
        collapsed_slice_dims=(1,),
        start_index_map=(1,),
        operand_batching_dims=(0,),
        start_indices_batching_dims=(0,),
    )
    return lax.gather(
        value, index[..., None], dims, (1, 1), mode=lax.GatherScatterMode.PROMISE_IN_BOUNDS
    )


def table_height(rows):
    return rows + 16


def fill_tables(rows, cols, u, tabs, halo):
    high_rows = table_height(rows)
    lane = lax.broadcasted_iota(I32, (8, 128), 1)
    lower = lane < 64
    for i in range(0, high_rows, 16):
        for parity in range(2):
            index = (2 * lane + parity) & 127
            for t in range(cols // 256):
                halves = []
                for j in range(2):
                    at = PAD + i + 8 * j
                    one = u[at : at + 8, 2 * t * 128 : (2 * t + 1) * 128]
                    two = u[at : at + 8, (2 * t + 1) * 128 : (2 * t + 2) * 128]
                    halves.append(
                        jnp.where(lower, lane_pick(one, index), lane_pick(two, index))
                    )
                high, low = split(jnp.concatenate(halves, axis=0))
                tabs[parity][i : i + 16, t * 128 : (t + 1) * 128] = high
                tabs[parity][high_rows + i : high_rows + i + 16, t * 128 : (t + 1) * 128] = low
        halo[i : i + 16, :] = jnp.broadcast_to(
            u[PAD + i : PAD + i + 16, cols : cols + 1], (16, 128)
        )


def sample_moves(
    rows, cols, blocks, cap, first, tabs, halo, starts, offs, wts, ends, dest, buf, slot_row, counter
):
    n_cols = lax.axis_size("cols")
    my_row, my_col = lax.axis_index("rows"), lax.axis_index("cols")
    kinds = 4 if first else 2
    part_rows = 3 * kinds * cap + (EDGE if first else 0)
    buf[...] = jnp.zeros(buf.shape, F32)
    for i in range(3 * n_cols):
        counter[i] = 0
    for b in range(blocks):
        tile = dest[b]
        band, column = tile // n_cols, tile % n_cols
        section = jnp.where(band == my_row, 0, jnp.where(band == (my_row ^ 1), 1, 2))
        distance = column ^ my_col
        rank = counter[distance * 3 + section]
        counter[distance * 3 + section] = rank + 1
        slot_row[b] = distance * part_rows + section * (kinds * cap) + rank

    high_rows = table_height(rows)
    pair_iota = lax.broadcasted_iota(I32, (cols // 2, 256), 0)
    row_iota = lax.broadcasted_iota(I32, (high_rows, 256), 0)

    def step(j, carry):
        def pair(ref):
            return jnp.concatenate([ref[pl.ds(2 * j, 1), :], ref[pl.ds(2 * j + 1, 1), :]], axis=1)

        row, col = row_col(pair(starts), cols)
        lanes = pl.ds(pl.multiple_of(j * 256, 256), 256)
        off_x = offs[0:1, lanes]
        off_y = offs[1:2, lanes]
        odd = (col & 1) == 1
        line = []
        for tab, place in ((tabs[0], (col + 1) >> 1), (tabs[1], col >> 1)):
            hot = jnp.where(pair_iota == place, 1.0, 0.0).astype(BF16)
            both = jnp.dot(tab[...], hot, preferred_element_type=F32)
            line.append(both[0:high_rows] + both[high_rows:])
        beyond = jnp.concatenate([halo[...]] * 2, axis=1)
        even_line = line[0] + jnp.where(col == cols - 1, beyond, 0.0)
        step_y = line[1] - even_line
        frac_x = 0.5 + 0.45 * jnp.tanh(off_x)
        frac_y = 0.5 + 0.45 * jnp.tanh(off_y)
        mixed = even_line + jnp.where(odd, 1.0 - frac_y, frac_y) * step_y
        here, below = row_iota == row, row_iota == row + 1
        grad_x = jnp.sum(
            jnp.where(below, mixed, jnp.where(here, -mixed, 0.0)), axis=0, keepdims=True
        )
        grad_y = jnp.sum(
            step_y * jnp.where(here, 1.0 - frac_x, jnp.where(below, frac_x, 0.0)),
            axis=0,
            keepdims=True,
        )
        grad_y = jnp.where(odd, -grad_y, grad_y)
        moved_x = 0.5 + 0.45 * jnp.tanh(off_x - grad_x)
        moved_y = 0.5 + 0.45 * jnp.tanh(off_y - grad_y)
        out = [moved_x, moved_y]
        if first:
            out += [pair(wts), (pair(ends) + 1).astype(F32)]
        for half in range(2):
            base = slot_row[2 * j + half]
            for q, value in enumerate(out):
                buf[pl.ds(base + q * cap, 1), :] = value[:, half * 128 : (half + 1) * 128]
        return carry

    lax.fori_loop(0, blocks // 2, step, 0, unroll=UNROLL)


def first_kernel(
    rows, cols, blocks, cap, n_cols, *refs
):
    (ue_in, me_in, ra_ref, rb_ref, starts, offs, wts, ends, dest) = refs[:9]
    outs = refs[9 : 9 + n_cols]
    ue_ref, me_ref = refs[9 + n_cols : 11 + n_cols]
    ua, ub, tab_even, tab_odd, halo, buf, slot_row, counter = refs[11 + n_cols :]
    col_even = lax.axis_index("cols") % 2 == 0
    tall = ue_in.shape[0]
    width = ra_ref.shape[1]
    for index, (src, dst) in enumerate(((ue_in, ue_ref), (me_in, me_ref))):
        part = slice(index * EDGE, (index + 1) * EDGE)
        west = pick(col_even, rb_ref[part, :], ra_ref[part, :])
        east = pick(col_even, ra_ref[part, :], rb_ref[part, :])
        dst[:, 0:cols] = src[:, 0:cols]
        dst[:, cols : cols + 128] = unflipped(side_tile(west, east, width), tall)
    ua[...] = ue_ref[...]
    ub[...] = jnp.zeros(ub.shape, F32)
    u = hjb_sweep(rows, cols, ua, ub, me_ref)
    tabs = (tab_even, tab_odd)
    fill_tables(rows, cols, u, tabs, halo)
    sample_moves(
        rows, cols, blocks, cap, True, tabs, halo, starts, offs, wts, ends, dest, buf, slot_row, counter
    )
    part_rows = 12 * cap + EDGE
    total = jnp.sum(jnp.sum(wts[...], axis=0, keepdims=True), axis=1, keepdims=True)
    for k in range(n_cols):
        outs[k][0 : part_rows - EDGE, :] = buf[k * part_rows : (k + 1) * part_rows - EDGE, :]
        outs[k][part_rows - EDGE :, :] = jnp.broadcast_to(total, (EDGE, 128))


def again_kernel(rows, cols, blocks, cap, n_cols, *refs):
    (ue_ref, m_in, d_ref, ra_ref, rb_ref, total_ref, starts, offs, dest) = refs[:9]
    outs = refs[9 : 9 + n_cols]
    value_ref, density_ref = refs[9 + n_cols : 11 + n_cols]
    ua, ub, m, tab_even, tab_odd, halo, buf, slot_row, counter = refs[11 + n_cols :]
    col_even = lax.axis_index("cols") % 2 == 0
    n_rows = lax.axis_size("rows")
    tall = ue_ref.shape[0]
    width = ra_ref.shape[1]
    half_scale = 0.5 * ((rows * cols * n_rows * n_cols) / total_ref[0:1, 0:1])
    west = pick(col_even, rb_ref[...], ra_ref[...])
    east = pick(col_even, ra_ref[...], rb_ref[...])
    side = unflipped(side_tile(west[0:EDGE], east[0:EDGE], width), tall)
    pushed = unflipped(
        jnp.concatenate([west[EDGE : 2 * EDGE], jnp.zeros((128 - EDGE, width), F32)], axis=0), tall
    )
    m[:, 0:128] = 0.5 * m_in[:, 0:128] + half_scale * (d_ref[:, 0:128] + pushed)
    m[:, 128:cols] = 0.5 * m_in[:, 128:cols] + half_scale * d_ref[:, 128:cols]
    m[:, cols : cols + 128] = 0.5 * m_in[:, cols : cols + 128] + half_scale * (
        d_ref[:, cols : cols + 128] + side
    )
    density_ref[...] = m[PAD : PAD + rows, 0:cols]
    ua[...] = ue_ref[...]
    ub[...] = jnp.zeros(ub.shape, F32)
    u = hjb_sweep(rows, cols, ua, ub, m)
    value_ref[...] = u[PAD : PAD + rows, 0:cols]
    tabs = (tab_even, tab_odd)
    fill_tables(rows, cols, u, tabs, halo)
    sample_moves(
        rows, cols, blocks, cap, False, tabs, halo, starts, offs, None, None, dest, buf, slot_row, counter
    )
    part_rows = 6 * cap
    for k in range(n_cols):
        outs[k][...] = buf[k * part_rows : (k + 1) * part_rows, :]


def deposit_grid(rows, cols, cap, chunks, moves, masses, scratch, grid):
    acc, lhs, rhs, beside, slots = scratch
    counts = []
    for q in range(chunks):
        cells = masses[(2 * q + 1) * cap : (2 * q + 2) * cap, :]
        counts.append(jnp.sum(jnp.where(cells > 0.5, 1.0, 0.0)).astype(I32) // 128)
    base = jnp.int32(0)
    for q in range(chunks):
        for rank in range(cap):
            slots[base + rank] = 2 * q * cap + rank
        base = base + counts[q]
    for rank in range(GROUP):
        slots[base + rank] = 2 * chunks * cap
    acc[...] = jnp.zeros(acc.shape, F32)
    beside[...] = jnp.zeros(beside.shape, F32)
    row_iota = lax.broadcasted_iota(I32, (rows, 128), 0)
    spill_iota = lax.broadcasted_iota(I32, (16, 128), 0)
    pair_iota = lax.broadcasted_iota(I32, (cols // 2, 128), 0)
    corner_iota = lax.broadcasted_iota(I32, (8, 128), 0)

    def step(g, carry):
        for t in range(GROUP):
            at = slots[g * GROUP + t]
            move_x = moves[pl.ds(at, 1), :]
            move_y = moves[pl.ds(at + cap, 1), :]
            mass = masses[pl.ds(at, 1), :]
            row, col = row_col(masses[pl.ds(at + cap, 1), :].astype(I32) - 1, cols)
            odd = (col & 1) == 1
            stay, go = mass * (1.0 - move_x), mass * move_x
            lanes = slice(t * 128, (t + 1) * 128)
            here, next_row = row_iota == row, row_iota == row + 1
            last = row == rows - 1
            edge = col == cols - 1
            for parity, place in ((0, (col + 1) >> 1), (1, col >> 1)):
                share = jnp.where(odd == (parity == 1), 1.0 - move_y, move_y)
                first, second = stay * share, go * share
                spill = jnp.zeros((16, 128), F32)
                for level, (one, two) in enumerate(zip(split(first), split(second))):
                    one, two = one.astype(F32), two.astype(F32)
                    lhs[parity, level * rows : (level + 1) * rows, lanes] = jnp.where(
                        here, one, jnp.where(next_row, two, 0.0)
                    ).astype(BF16)
                    spill = jnp.where((spill_iota == level) & last, two, spill)
                lhs[parity, 2 * rows : 2 * rows + 16, lanes] = spill.astype(BF16)
                rhs[parity, :, lanes] = jnp.where(pair_iota == place, 1.0, 0.0).astype(BF16)
                if parity == 0:
                    first, second = jnp.where(edge, first, 0.0), jnp.where(edge, second, 0.0)
                    beside[0:rows, :] += jnp.where(here, first, jnp.where(next_row, second, 0.0))
                    beside[rows : rows + 8, :] += jnp.where((corner_iota == 0) & last, second, 0.0)
        for parity in range(2):
            acc[parity] += lax.dot_general(
                lhs[parity], rhs[parity], (((1,), (1,)), ((), ())), preferred_element_type=F32
            )
        return carry

    lax.fori_loop(0, (base + GROUP - 1) // GROUP, step, 0)

    wide = cols + 128
    lane = lax.broadcasted_iota(I32, (8, wide), 1)
    lane1 = lax.broadcasted_iota(I32, (8, 128), 1)
    odd_lane = (lane1 & 1) == 1
    half = lane1 >> 1

    def weave(i, even, odd):
        for t in range(cols // 128):
            index = half + 64 * (t % 2)
            at = slice((t // 2) * 128, (t // 2 + 1) * 128)
            grid[i : i + 8, t * 128 : (t + 1) * 128] = jnp.where(
                odd_lane, lane_pick(odd[:, at], index), lane_pick(even[:, at], index)
            )
        right = jnp.sum(beside[i : i + 8, :], axis=1, keepdims=True)
        grid[i : i + 8, cols:wide] = jnp.where(lane1 == 0, right, 0.0)

    for i in range(0, rows, 8):
        weave(i, *[acc[p, i : i + 8, :] + acc[p, rows + i : rows + i + 8, :] for p in range(2)])
    sub = lax.broadcasted_iota(I32, (8, cols // 2), 0)
    below = []
    for p in range(2):
        spill = acc[p, 2 * rows : 2 * rows + 8, :]
        total = jnp.sum(jnp.where(sub < 2, spill, 0.0), axis=0, keepdims=True)
        below.append(jnp.where(sub == 0, total, 0.0))
    weave(rows, *below)

    @pl.when(lax.axis_index("rows") == lax.axis_size("rows") - 1)
    def _():
        tail = grid[rows - 8 : rows, :]
        sub8 = lax.broadcasted_iota(I32, (8, wide), 0)
        spill_row = jnp.broadcast_to(grid[rows : rows + 1, :], (8, wide))
        grid[rows - 8 : rows, :] = tail + jnp.where(sub8 == 7, spill_row, 0.0)
        grid[rows : rows + 8, :] = jnp.zeros((8, wide), F32)

    @pl.when(lax.axis_index("cols") == lax.axis_size("cols") - 1)
    def _():
        for i in range(0, rows + 8, 8):
            line = grid[i : i + 8, :]
            moved = jnp.where(lane == cols - 1, pltpu.roll(line, wide - 1, 1), 0.0)
            grid[i : i + 8, :] = jnp.where(lane < cols, line + moved, 0.0)


def gather_parts(cap, n_cols, kinds, pieces, ra_ref, rb_ref, groups):
    step = kinds * cap
    for dst, offset in groups:
        size = 2 * cap
        for k in range(n_cols):
            dst[k * size : (k + 1) * size, :] = pieces[k][offset : offset + size, :]
            for index, other in ((1, ra_ref), (2, rb_ref)):
                at = (index * n_cols + k) * size
                dst[at : at + size, :] = other[k * step + offset : k * step + offset + size, :]


def first_deposit_kernel(rows, cols, cap, n_cols, *refs):
    pieces = refs[:n_cols]
    ra_ref, rb_ref = refs[n_cols : n_cols + 2]
    grid, sa_ref, sb_ref, masses = refs[n_cols + 2 : n_cols + 6]
    moves, *scratch = refs[n_cols + 6 :]
    chunks = 3 * n_cols
    gather_parts(
        cap, n_cols, 4, pieces, ra_ref, rb_ref, ((moves, 0), (masses, 2 * cap))
    )
    for ref in (moves, masses):
        ref[2 * cap * chunks :, :] = jnp.zeros((2 * cap, 128), F32)
    deposit_grid(rows, cols, cap, chunks, moves, masses, scratch, grid)
    row_even = lax.axis_index("rows") % 2 == 0
    south_going = grid[rows - 7 : rows + 1, :]
    north_going = grid[0:8, :]
    sa_ref[...] = pick(row_even, south_going, north_going)
    sb_ref[...] = pick(row_even, north_going, south_going)


def last_deposit_kernel(rows, cols, cap, n_cols, *refs):
    pieces = refs[:n_cols]
    ra_ref, rb_ref, masses = refs[n_cols : n_cols + 3]
    grid, row_ref, col_ref, corner_ref = refs[n_cols + 3 : n_cols + 7]
    moves, *scratch = refs[n_cols + 7 :]
    chunks = 3 * n_cols
    gather_parts(cap, n_cols, 2, pieces, ra_ref, rb_ref, ((moves, 0),))
    moves[2 * cap * chunks :, :] = jnp.zeros((2 * cap, 128), F32)
    deposit_grid(rows, cols, cap, chunks, moves, masses, scratch, grid)
    row_ref[...] = grid[rows : rows + 8, 0:cols]
    corner_ref[...] = grid[rows : rows + 8, cols : cols + 128]
    col_ref[...] = flipped(grid[0:rows, cols : cols + 128])[0:8]


def edge_mid_kernel(rows, cols, g_ref, a_ref, b_ref, d_ref, ca_ref, cb_ref):
    row_even = lax.axis_index("rows") % 2 == 0
    col_even = lax.axis_index("cols") % 2 == 0
    wide = cols + 128
    north = pick(row_even, b_ref[...], a_ref[...])
    south = pick(row_even, a_ref[...], b_ref[...])
    d_ref[0:PAD, :] = jnp.zeros((PAD, wide), F32)
    d_ref[PAD : PAD + rows, :] = g_ref[0:rows, :]
    d_ref[PAD + rows : PAD + rows + 8, :] = south + g_ref[rows : rows + 8, :]
    d_ref[PAD + rows + 8 :, :] = jnp.zeros((d_ref.shape[0] - PAD - rows - 8, wide), F32)
    d_ref[PAD - 7 : PAD + 1, :] = d_ref[PAD - 7 : PAD + 1, :] + north
    west_going = flipped(d_ref[:, 0:128])[0:EDGE]
    east_going = flipped(d_ref[:, cols - 128 : cols])[128 - EDGE : 128]
    spilled = flipped(d_ref[:, cols : cols + 128])[0:EDGE]
    ca_ref[0:EDGE, :] = pick(col_even, east_going, west_going)
    cb_ref[0:EDGE, :] = pick(col_even, west_going, east_going)
    ca_ref[EDGE:, :] = pick(col_even, spilled, 0.0)
    cb_ref[EDGE:, :] = pick(col_even, 0.0, spilled)


def final_kernel(rows, cols, g_ref, m_ref, row_in, col_in, corner_in, total_ref, out_ref):
    n_rows, n_cols = lax.axis_size("rows"), lax.axis_size("cols")
    half_scale = 0.5 * ((rows * cols * n_rows * n_cols) / total_ref[0:1, 0:1])
    out_ref[...] = 0.5 * m_ref[...] + half_scale * g_ref[0:rows, 0:cols]
    out_ref[0:8, :] = out_ref[0:8, :] + half_scale * row_in[...]
    out_ref[0:8, 0:128] = out_ref[0:8, 0:128] + half_scale * corner_in[...]
    beside = jnp.concatenate([col_in[...], jnp.zeros((120, col_in.shape[1]), F32)], axis=0)
    out_ref[:, 0:128] = out_ref[:, 0:128] + half_scale * unflipped(beside, rows)


def exchange_columns(outs):
    n_cols = len(outs)
    return [outs[0]] + [xor_permute(outs[k], "cols", k) for k in range(1, n_cols)]


def exchange_rows(pieces, kinds, cap, extra=None):
    step = kinds * cap
    first = [piece[step : 2 * step] for piece in pieces]
    second = [piece[2 * step : 3 * step] for piece in pieces]
    if extra is not None:
        first.append(extra)
    return swap_both(jnp.concatenate(first), jnp.concatenate(second), "rows")


def body(terminal_value, density_start, start_cells, offsets, weights, dest_tiles, end_cells):
    rows, cols = terminal_value.shape
    n_rows, n_cols = lax.axis_size("rows"), lax.axis_size("cols")
    blocks = dest_tiles.shape[0]
    cap = blocks // 4
    chunks = 3 * n_cols
    wide, tall = cols + 128, rows + 2 * PAD
    flat = -(-tall // 128) * 128
    starts = start_cells.reshape(blocks, 128)
    wts = weights.reshape(blocks, 128)
    ends = end_cells.reshape(blocks, 128)
    row_even = lax.axis_index("rows") % 2 == 0

    south_going = jnp.concatenate([terminal_value[rows - EDGE :], density_start[rows - EDGE :]])
    north_going = jnp.concatenate([terminal_value[:EDGE], density_start[:EDGE]])
    ra, rb = swap_both(
        jnp.where(row_even, south_going, north_going),
        jnp.where(row_even, north_going, south_going),
        "rows",
    )
    ue, me, ca, cb = vmem_call(
        functools.partial(start_mid_kernel, rows, cols),
        (shape(tall, wide), shape(tall, wide), shape(2 * EDGE, flat), shape(2 * EDGE, flat)),
        4,
    )(terminal_value, density_start, ra, rb)
    ca, cb = swap_both(ca, cb, "cols")
    sweep_scratch = [
        pltpu.VMEM((tall, wide), F32),
        pltpu.VMEM((tall, wide), F32),
    ]

    def sample_scratch(part_rows):
        return [
            pltpu.VMEM((2 * table_height(rows), cols // 2), BF16),
            pltpu.VMEM((2 * table_height(rows), cols // 2), BF16),
            pltpu.VMEM((table_height(rows), 128), F32),
            pltpu.VMEM((n_cols * part_rows, 128), F32),
            pltpu.SMEM((blocks,), I32),
            pltpu.SMEM((chunks,), I32),
        ]

    deposit_scratch = [
        pltpu.VMEM((2 * cap * (chunks + 1), 128), F32),
        pltpu.VMEM((2, 2 * rows + 16, cols // 2), F32),
        pltpu.VMEM((2, 2 * rows + 16, GROUP * 128), BF16),
        pltpu.VMEM((2, cols // 2, GROUP * 128), BF16),
        pltpu.VMEM((rows + 8, 128), F32),
        pltpu.SMEM((chunks * cap + GROUP,), I32),
    ]
    part_rows = 12 * cap + EDGE
    *outs, ue, me = vmem_call(
        functools.partial(first_kernel, rows, cols, blocks, cap, n_cols),
        tuple([shape(part_rows, 128)] * n_cols + [shape(tall, wide)] * 2),
        9,
        sweep_scratch + sample_scratch(part_rows),
        smem_in=(8,),
    )(ue, me, ca, cb, starts, offsets, wts, ends, dest_tiles)
    pieces = exchange_columns(outs)
    total = sum(piece[part_rows - EDGE :] for piece in pieces)
    ra, rb = exchange_rows(pieces, 4, cap, total)
    total = total + ra[4 * n_cols * cap :]
    bit = 2
    while bit < n_rows:
        total = total + xor_permute(total, "rows", bit)
        bit *= 2
    grid, ea, eb, masses = vmem_call(
        functools.partial(first_deposit_kernel, rows, cols, cap, n_cols),
        (
            shape(rows + 8, wide),
            shape(8, wide),
            shape(8, wide),
            shape(2 * cap * (chunks + 1), 128),
        ),
        n_cols + 2,
        deposit_scratch,
    )(*pieces, ra, rb)
    ea, eb = swap_both(ea, eb, "rows")
    deposit, ca, cb = vmem_call(
        functools.partial(edge_mid_kernel, rows, cols),
        (shape(tall, wide), shape(2 * EDGE, flat), shape(2 * EDGE, flat)),
        3,
    )(grid, ea, eb)
    ca, cb = swap_both(ca, cb, "cols")
    part_rows = 6 * cap
    *outs, value, density = vmem_call(
        functools.partial(again_kernel, rows, cols, blocks, cap, n_cols),
        tuple([shape(part_rows, 128)] * n_cols + [shape(rows, cols)] * 2),
        9,
        sweep_scratch + [pltpu.VMEM((tall, wide), F32)] + sample_scratch(part_rows),
        smem_in=(8,),
    )(ue, me, deposit, ca, cb, total, starts, offsets, dest_tiles)
    pieces = exchange_columns(outs)
    ra, rb = exchange_rows(pieces, 2, cap)
    grid, below, beside, corner = vmem_call(
        functools.partial(last_deposit_kernel, rows, cols, cap, n_cols),
        (shape(rows + 8, wide), shape(8, cols), shape(8, rows), shape(8, 128)),
        n_cols + 3,
        deposit_scratch,
    )(*pieces, ra, rb, masses)
    below = lax.ppermute(below, "rows", [(i, i + 1) for i in range(n_rows - 1)])
    beside = lax.ppermute(beside, "cols", [(i, i + 1) for i in range(n_cols - 1)])
    corner = lax.ppermute(
        corner,
        ("rows", "cols"),
        [
            (r * n_cols + c, (r + 1) * n_cols + c + 1)
            for r in range(n_rows - 1)
            for c in range(n_cols - 1)
        ],
    )
    (density,) = vmem_call(
        functools.partial(final_kernel, rows, cols), (shape(rows, cols),), 6, keep=(0,)
    )(grid, density, below, beside, corner, total)
    return (value, density)


def solution(mesh):
    in_specs = (
        P("rows", "cols"),
        P("rows", "cols"),
        P(("rows", "cols")),
        P(None, ("rows", "cols")),
        P(("rows", "cols")),
        P(("rows", "cols")),
        P(("rows", "cols")),
    )
    out_specs = (P("rows", "cols"), P("rows", "cols"))
    return jax.shard_map(body, mesh=mesh, in_specs=in_specs, out_specs=out_specs, check_vma=False)
```

```python
import functools
import jax
import jax.numpy as jnp
from jax import lax
from jax.experimental import pallas as pl
from jax.experimental.pallas import tpu as pltpu
from jax.sharding import PartitionSpec as P

HJB_STEPS = 4
ITERS = 2
F32, BF16, I32 = jnp.float32, jnp.bfloat16, jnp.int32

PAD = 16
EDGE = 8
GROUP = 4
UNROLL = 4
VMEM_LIMIT = 24 * 1024 * 1024


def swap_pairs(count):
    first = [(i, i ^ 1) for i in range(count)]
    second = [(i, ((i + 1) ^ 1) - 1) for i in range(1, count - 1)]
    return first, second


def swap_both(first, second, axis):
    pairs_a, pairs_b = swap_pairs(lax.axis_size(axis))
    return lax.ppermute(first, axis, pairs_a), lax.ppermute(second, axis, pairs_b)


def xor_permute(value, axis, bit):
    return lax.ppermute(value, axis, [(i, i ^ bit) for i in range(lax.axis_size(axis))])


def vmem_call(kernel, out_shape, n_in, scratch=(), hbm_in=(), hbm_out=(), keep=()):
    def spec(in_hbm):
        return pl.BlockSpec(memory_space=pltpu.HBM if in_hbm else pltpu.VMEM)

    results = [
        leaf if i in keep or i in hbm_out else pltpu.VMEM(leaf.shape, leaf.dtype)
        for i, leaf in enumerate(out_shape)
    ]
    call = pl.pallas_call(
        kernel,
        out_shape=results,
        in_specs=[spec(i in hbm_in) for i in range(n_in)],
        out_specs=[spec(i in hbm_out) for i in range(len(results))],
        scratch_shapes=list(scratch),
        compiler_params=pltpu.CompilerParams(vmem_limit_bytes=VMEM_LIMIT),
    )

    def run(*operands):
        return call(
            *[
                pltpu.with_memory_space_constraint(x, pltpu.HBM if i in hbm_in else pltpu.VMEM)
                for i, x in enumerate(operands)
            ]
        )

    return run


def shape(*dims, dtype=F32):
    return jax.ShapeDtypeStruct(dims, dtype)


def flipped(block):
    rows = block.shape[0]
    width = -(-rows // 128) * 128
    if width > rows:
        block = jnp.concatenate([block, jnp.zeros((width - rows, 128), F32)], axis=0)
    parts = [block[i : i + 128].T for i in range(0, width, 128)]
    return jnp.concatenate(parts, axis=1)


def unflipped(block, rows):
    parts = [block[:, i : i + 128].T for i in range(0, block.shape[1], 128)]
    return jnp.concatenate(parts, axis=0)[:rows]


def row_col(cell, cols):
    if cols & (cols - 1) == 0:
        return cell >> (cols.bit_length() - 1), cell & (cols - 1)
    return cell // cols, cell % cols


def pick(flag, one, other):
    return jnp.where(flag, one, other)


def start_kernel(rows, count, *refs):
    sources, copies = refs[:count], refs[count : 2 * count]
    sa_ref, sb_ref, sum_ref, sems = refs[2 * count :]
    moves = [
        pltpu.make_async_copy(src, dst, sems.at[i])
        for i, (src, dst) in enumerate(zip(sources, copies))
    ]
    for move in moves:
        move.start()
    for move in moves:
        move.wait()
    u_ref, m_ref, wts = copies[:3]
    row_even = lax.axis_index("rows") % 2 == 0
    for index, ref in enumerate((u_ref, m_ref)):
        part = slice(index * EDGE, (index + 1) * EDGE)
        south_going, north_going = ref[rows - EDGE : rows, :], ref[0:EDGE, :]
        sa_ref[part, :] = pick(row_even, south_going, north_going)
        sb_ref[part, :] = pick(row_even, north_going, south_going)
    total = jnp.sum(jnp.sum(wts[...], axis=0, keepdims=True), axis=1, keepdims=True)
    sum_ref[...] = jnp.broadcast_to(total, sum_ref.shape)


def start_mid_kernel(
    rows, cols, u_ref, m_ref, a_ref, b_ref, w_ref, v_ref, ue_ref, me_ref, ca_ref, cb_ref, sum_ref
):
    sum_ref[...] = w_ref[...] + v_ref[...]
    row_even = lax.axis_index("rows") % 2 == 0
    col_even = lax.axis_index("cols") % 2 == 0
    for index, (src, dst) in enumerate(((u_ref, ue_ref), (m_ref, me_ref))):
        dst[...] = jnp.zeros(dst.shape, F32)
        dst[PAD : PAD + rows, 0:cols] = src[...]
        part = slice(index * EDGE, (index + 1) * EDGE)
        north = pick(row_even, b_ref[part, :], a_ref[part, :])
        south = pick(row_even, a_ref[part, :], b_ref[part, :])
        dst[PAD - EDGE : PAD, 0:cols] = north
        dst[PAD + rows : PAD + rows + EDGE, 0:cols] = south
        west_going = flipped(dst[:, 0:128])[0:EDGE]
        east_going = flipped(dst[:, cols - 128 : cols])[128 - EDGE : 128]
        ca_ref[part, :] = pick(col_even, east_going, west_going)
        cb_ref[part, :] = pick(col_even, west_going, east_going)


def side_tile(left, right, width):
    return jnp.concatenate([right, jnp.zeros((128 - 2 * EDGE, width), F32), left], axis=0)


def hjb_sweep(rows, cols, ua, ub, m):
    wide = cols + 128
    tiles = wide // 128
    n_rows, n_cols = lax.axis_size("rows"), lax.axis_size("cols")
    sub = lax.broadcasted_iota(I32, (8, 128), 0)
    lane = lax.broadcasted_iota(I32, (8, 128), 1)
    top, bottom, first, last = sub == 0, sub == 7, lane == 0, lane == 127
    row_first = lax.axis_index("rows") * rows
    col = jnp.where(lane < 64, cols + lane, lane - 128) + lax.axis_index("cols") * cols
    side_ok = (col >= 0) & (col < cols * n_cols)
    src, dst = ua, ub

    def strip(i):
        return [src[i : i + 8, t * 128 : (t + 1) * 128] for t in range(tiles)]

    for step in range(HJB_STEPS):
        start, stop = PAD - 8, PAD + rows + 8
        here = strip(start)
        fell = [pltpu.roll(x, 1, 0) for x in here]
        rose = [pltpu.roll(x, 7, 0) for x in here]
        fell_before = fell
        for i in range(start, stop, 8):
            if i + 8 < stop:
                after = strip(i + 8)
                rose_after = [pltpu.roll(x, 7, 0) for x in after]
                fell_after = [pltpu.roll(x, 1, 0) for x in after]
            else:
                after, rose_after, fell_after = here, rose, fell
            row_ok = None
            if i < PAD or i >= PAD + rows:
                row = sub + (row_first + (i - PAD))
                row_ok = (row >= 0) & (row < rows * n_rows)
            went = [pltpu.roll(x, 1, 1) for x in here]
            came = [pltpu.roll(x, 127, 1) for x in here]
            for t in range(tiles):
                value = here[t]
                up = jnp.where(top, fell_before[t], fell[t])
                down = jnp.where(bottom, rose_after[t], rose[t])
                left = jnp.where(first, went[t - 1], went[t])
                right = jnp.where(last, came[(t + 1) % tiles], came[t])
                slope_x = jnp.maximum(value - jnp.minimum(up, down), 0.0)
                slope_y = jnp.maximum(value - jnp.minimum(left, right), 0.0)
                around = (up + down) + (left + right) + m[i : i + 8, t * 128 : (t + 1) * 128]
                new = 0.5 * value + 0.125 * (around - (slope_x * slope_x + slope_y * slope_y))
                ok = row_ok
                if t == tiles - 1:
                    ok = side_ok if ok is None else ok & side_ok
                dst[i : i + 8, t * 128 : (t + 1) * 128] = (
                    new if ok is None else jnp.where(ok, new, 0.0)
                )
            here, fell_before, fell, rose = after, fell, fell_after, rose_after
        src, dst = dst, src
    return src


def split(value):
    high = value.astype(BF16)
    return high, (value - high.astype(F32)).astype(BF16)


def lane_pick(value, index):
    dims = lax.GatherDimensionNumbers(
        offset_dims=(),
        collapsed_slice_dims=(1,),
        start_index_map=(1,),
        operand_batching_dims=(0,),
        start_indices_batching_dims=(0,),
    )
    return lax.gather(
        value, index[..., None], dims, (1, 1), mode=lax.GatherScatterMode.PROMISE_IN_BOUNDS
    )


def table_height(rows):
    return rows + 16


def fill_tables(rows, cols, u, tabs, halo):
    high_rows = table_height(rows)
    lane = lax.broadcasted_iota(I32, (8, 128), 1)
    lower = lane < 64
    for i in range(0, high_rows, 16):
        for parity in range(2):
            index = (2 * lane + parity) & 127
            for t in range(cols // 256):
                halves = []
                for j in range(2):
                    at = PAD + i + 8 * j
                    one = u[at : at + 8, 2 * t * 128 : (2 * t + 1) * 128]
                    two = u[at : at + 8, (2 * t + 1) * 128 : (2 * t + 2) * 128]
                    halves.append(
                        jnp.where(lower, lane_pick(one, index), lane_pick(two, index))
                    )
                high, low = split(jnp.concatenate(halves, axis=0))
                tabs[parity][i : i + 16, t * 128 : (t + 1) * 128] = high
                tabs[parity][high_rows + i : high_rows + i + 16, t * 128 : (t + 1) * 128] = low
        halo[i : i + 16, :] = jnp.broadcast_to(
            u[PAD + i : PAD + i + 16, cols : cols + 1], (16, 128)
        )


def sample_moves(
    rows, cols, blocks, cap, first, tabs, halo, starts, offs, wts, ends, dest, buf, slot_row,
    corner_row, counter
):
    n_cols = lax.axis_size("cols")
    my_row, my_col = lax.axis_index("rows"), lax.axis_index("cols")
    n_rows = lax.axis_size("rows")
    kinds = 4 if first else 2
    part_rows = 3 * kinds * cap + EDGE
    spare_row = n_cols * part_rows
    buf[...] = jnp.zeros(buf.shape, F32)
    for i in range(3 * n_cols):
        counter[i] = 0
    for b in range(blocks):
        tile = dest[b]
        band, column = tile // n_cols, tile % n_cols
        section = jnp.where(band == my_row, 0, jnp.where(band == (my_row ^ 1), 1, 2))
        distance = column ^ my_col
        rank = counter[distance * 3 + section]
        counter[distance * 3 + section] = rank + 1
        slot_row[b] = distance * part_rows + section * (kinds * cap) + rank
        if not first:
            goes = (band < n_rows - 1) & (column < n_cols - 1)
            row = ((column + 1) ^ my_col) * part_rows + 3 * kinds * cap + section
            corner_row[b] = jnp.where(goes, row, spare_row)

    high_rows = table_height(rows)
    pair_iota = lax.broadcasted_iota(I32, (cols // 2, 256), 0)
    row_iota = lax.broadcasted_iota(I32, (high_rows, 256), 0)

    def step(j, carry):
        def pair(ref):
            return jnp.concatenate([ref[pl.ds(2 * j, 1), :], ref[pl.ds(2 * j + 1, 1), :]], axis=1)

        row, col = row_col(pair(starts), cols)
        lanes = pl.ds(pl.multiple_of(j * 256, 256), 256)
        off_x = offs[0:1, lanes]
        off_y = offs[1:2, lanes]
        odd = (col & 1) == 1
        line = []
        for tab, place in ((tabs[0], (col + 1) >> 1), (tabs[1], col >> 1)):
            hot = jnp.where(pair_iota == place, 1.0, 0.0).astype(BF16)
            both = jnp.dot(tab[...], hot, preferred_element_type=F32)
            line.append(both[0:high_rows] + both[high_rows:])
        beyond = jnp.concatenate([halo[...]] * 2, axis=1)
        even_line = line[0] + jnp.where(col == cols - 1, beyond, 0.0)
        step_y = line[1] - even_line
        frac_x = 0.5 + 0.45 * jnp.tanh(off_x)
        frac_y = 0.5 + 0.45 * jnp.tanh(off_y)
        mixed = even_line + jnp.where(odd, 1.0 - frac_y, frac_y) * step_y
        here, below = row_iota == row, row_iota == row + 1
        grad_x = jnp.sum(
            jnp.where(below, mixed, jnp.where(here, -mixed, 0.0)), axis=0, keepdims=True
        )
        grad_y = jnp.sum(
            step_y * jnp.where(here, 1.0 - frac_x, jnp.where(below, frac_x, 0.0)),
            axis=0,
            keepdims=True,
        )
        grad_y = jnp.where(odd, -grad_y, grad_y)
        moved_x = 0.5 + 0.45 * jnp.tanh(off_x - grad_x)
        moved_y = 0.5 + 0.45 * jnp.tanh(off_y - grad_y)
        out = [moved_x, moved_y]
        if first:
            out += [pair(wts), (pair(ends) + 1).astype(F32)]
        else:
            corner = jnp.where(pair(ends) == rows * cols - 1, pair(wts) * moved_x * moved_y, 0.0)
        for half in range(2):
            if not first:
                buf[pl.ds(corner_row[2 * j + half], 1), :] += corner[:, half * 128 : (half + 1) * 128]
            base = slot_row[2 * j + half]
            for q, value in enumerate(out):
                buf[pl.ds(base + q * cap, 1), :] = value[:, half * 128 : (half + 1) * 128]
        return carry

    lax.fori_loop(0, blocks // 2, step, 0, unroll=UNROLL)


def first_kernel(
    rows, cols, blocks, cap, n_cols, *refs
):
    (ue_in, me_in, ra_ref, rb_ref, w_ref, v_ref, starts, offs, wts, ends, dest_hbm) = refs[:11]
    outs = refs[11 : 11 + n_cols]
    ue_ref, me_ref = refs[11 + n_cols : 13 + n_cols]
    ua, ub, tab_even, tab_odd, halo, buf, slot_row, corner_row, counter, dest, sem = refs[13 + n_cols :]
    fetch = pltpu.make_async_copy(dest_hbm, dest, sem)
    fetch.start()
    col_even = lax.axis_index("cols") % 2 == 0
    tall = ue_in.shape[0]
    width = ra_ref.shape[1]
    for index, (src, dst) in enumerate(((ue_in, ue_ref), (me_in, me_ref))):
        part = slice(index * EDGE, (index + 1) * EDGE)
        west = pick(col_even, rb_ref[part, :], ra_ref[part, :])
        east = pick(col_even, ra_ref[part, :], rb_ref[part, :])
        dst[:, 0:cols] = src[:, 0:cols]
        dst[:, cols : cols + 128] = unflipped(side_tile(west, east, width), tall)
    ua[...] = ue_ref[...]
    ub[...] = jnp.zeros(ub.shape, F32)
    u = hjb_sweep(rows, cols, ua, ub, me_ref)
    tabs = (tab_even, tab_odd)
    fill_tables(rows, cols, u, tabs, halo)
    fetch.wait()
    sample_moves(
        rows, cols, blocks, cap, True, tabs, halo, starts, offs, wts, ends, dest, buf, slot_row,
        corner_row, counter,
    )
    part_rows = 12 * cap + EDGE
    for k in range(n_cols):
        outs[k][0 : part_rows - EDGE, :] = buf[k * part_rows : (k + 1) * part_rows - EDGE, :]
        outs[k][part_rows - EDGE :, :] = w_ref[...] + v_ref[...]


def again_kernel(rows, cols, blocks, cap, n_cols, *refs):
    (ue_ref, m_in, d_ref, ra_ref, rb_ref, total_ref) = refs[:6]
    (starts, offs, wts, ends, dest_hbm) = refs[6:11]
    outs = refs[11 : 11 + n_cols]
    value_hbm, density_ref = refs[11 + n_cols : 13 + n_cols]
    (ua, ub, m, tab_even, tab_odd, halo, buf, slot_row, corner_row, counter, dest, sem, value_sem) = (
        refs[13 + n_cols :]
    )
    fetch = pltpu.make_async_copy(dest_hbm, dest, sem)
    fetch.start()
    col_even = lax.axis_index("cols") % 2 == 0
    n_rows = lax.axis_size("rows")
    tall = ue_ref.shape[0]
    width = ra_ref.shape[1]
    half_scale = 0.5 * ((rows * cols * n_rows * n_cols) / total_ref[0:1, 0:1])
    west = pick(col_even, rb_ref[...], ra_ref[...])
    east = pick(col_even, ra_ref[...], rb_ref[...])
    side = unflipped(side_tile(west[0:EDGE], east[0:EDGE], width), tall)
    pushed = unflipped(
        jnp.concatenate([west[EDGE : 2 * EDGE], jnp.zeros((128 - EDGE, width), F32)], axis=0), tall
    )
    m[:, 0:128] = 0.5 * m_in[:, 0:128] + half_scale * (d_ref[:, 0:128] + pushed)
    m[:, 128:cols] = 0.5 * m_in[:, 128:cols] + half_scale * d_ref[:, 128:cols]
    m[:, cols : cols + 128] = 0.5 * m_in[:, cols : cols + 128] + half_scale * (
        d_ref[:, cols : cols + 128] + side
    )
    density_ref[...] = m[PAD : PAD + rows, 0:cols]
    ua[...] = ue_ref[...]
    ub[...] = jnp.zeros(ub.shape, F32)
    u = hjb_sweep(rows, cols, ua, ub, m)
    leave = pltpu.make_async_copy(u.at[PAD : PAD + rows, 0:cols], value_hbm, value_sem)
    leave.start()
    tabs = (tab_even, tab_odd)
    fill_tables(rows, cols, u, tabs, halo)
    fetch.wait()
    sample_moves(
        rows, cols, blocks, cap, False, tabs, halo, starts, offs, wts, ends, dest, buf, slot_row,
        corner_row, counter,
    )
    part_rows = 6 * cap + EDGE
    for k in range(n_cols):
        outs[k][...] = buf[k * part_rows : (k + 1) * part_rows, :]
    leave.wait()


def deposit_blocks(rows, cols, cap, chunks, moves, masses, scratch, slots):
    acc, beside, lhs_a, rhs_a, lhs_b, rhs_b = scratch
    counts = []
    for q in range(chunks):
        cells = masses[(2 * q + 1) * cap : (2 * q + 2) * cap, :]
        counts.append(jnp.sum(jnp.where(cells > 0.5, 1.0, 0.0)).astype(I32) // 128)
    base = jnp.int32(0)
    for q in range(chunks):
        for rank in range(cap):
            slots[base + rank] = 2 * q * cap + rank
        base = base + counts[q]
    for rank in range(2 * GROUP):
        slots[base + rank] = 2 * chunks * cap
    lhs_b[...] = jnp.zeros(lhs_b.shape, BF16)
    rhs_b[...] = jnp.zeros(rhs_b.shape, BF16)
    high_rows = table_height(rows)
    sub16 = lax.broadcasted_iota(I32, (16, 128), 0)
    sub8 = lax.broadcasted_iota(I32, (8, 128), 0)
    one16, zero16 = jnp.ones((16, 128), BF16), jnp.zeros((16, 128), BF16)

    def relative(line, sub):
        return jnp.broadcast_to(line, sub.shape) - sub

    def build(first_slot, lhs, rhs):
        edges = []
        for t in range(GROUP):
            at = slots[first_slot + t]
            move_x = moves[pl.ds(at, 1), :]
            move_y = moves[pl.ds(at + cap, 1), :]
            mass = masses[pl.ds(at, 1), :]
            row, col = row_col(masses[pl.ds(at + cap, 1), :].astype(I32) - 1, cols)
            odd = (col & 1) == 1
            stay, go = mass * (1.0 - move_x), mass * move_x
            row_at = relative(row, sub16).astype(jnp.int16)
            values = []
            for parity in range(2):
                share = jnp.where(odd == (parity == 1), 1.0 - move_y, move_y)
                first, second = stay * share, go * share
                if parity == 0:
                    edge_row = jnp.where(col == cols - 1, row, -2)
                    edges.append((relative(edge_row, sub8), first, second))
                for one, two in zip(split(first), split(second)):
                    values.append(
                        [jnp.broadcast_to(x.astype(F32), (16, 128)).astype(BF16) for x in (one, two)]
                    )
            for i in range(high_rows // 16):
                here, below = row_at == 16 * i, row_at == 16 * i - 1
                for index, (one, two) in enumerate(values):
                    at_row = (index % 2) * high_rows + 16 * i
                    lhs[index // 2, t, at_row : at_row + 16, :] = jnp.where(
                        here, one, jnp.where(below, two, zero16)
                    )
            for parity, place in ((0, (col + 1) >> 1), (1, col >> 1)):
                place_at = relative(place, sub16).astype(jnp.int16)
                for i in range(cols // 32):
                    rhs[parity, t, 16 * i : 16 * i + 16, :] = jnp.where(
                        place_at == 16 * i, one16, zero16
                    )
        for i in range(rows // 8 + 1):
            total = beside[8 * i : 8 * i + 8, :]
            for row_at, first, second in edges:
                total = total + jnp.where(
                    row_at == 8 * i, first, jnp.where(row_at == 8 * i - 1, second, 0.0)
                )
            beside[8 * i : 8 * i + 8, :] = total

    def multiply(lhs, rhs):
        for parity in range(2):
            one, two = [
                jnp.concatenate([ref[parity, t] for t in range(GROUP)], axis=1) for ref in (lhs, rhs)
            ]
            acc[parity] += lax.dot_general(
                one, two, (((1,), (1,)), ((), ())), preferred_element_type=F32
            )

    def step(g, carry):
        multiply(lhs_b, rhs_b)
        build(2 * g * GROUP, lhs_a, rhs_a)
        multiply(lhs_a, rhs_a)
        build((2 * g + 1) * GROUP, lhs_b, rhs_b)
        return carry

    lax.fori_loop(0, (base + 2 * GROUP - 1) // (2 * GROUP), step, 0)
    multiply(lhs_b, rhs_b)


def finish_grid(rows, cols, acc, beside, grid):
    high_rows = table_height(rows)
    wide = cols + 128
    lane = lax.broadcasted_iota(I32, (8, wide), 1)
    lane1 = lax.broadcasted_iota(I32, (8, 128), 1)
    odd_lane = (lane1 & 1) == 1
    half = lane1 >> 1

    def weave(i, even, odd):
        for t in range(cols // 128):
            index = half + 64 * (t % 2)
            at = slice((t // 2) * 128, (t // 2 + 1) * 128)
            grid[i : i + 8, t * 128 : (t + 1) * 128] = jnp.where(
                odd_lane, lane_pick(odd[:, at], index), lane_pick(even[:, at], index)
            )
        right = jnp.sum(beside[i : i + 8, :], axis=1, keepdims=True)
        grid[i : i + 8, cols:wide] = jnp.where(lane1 == 0, right, 0.0)

    for i in range(0, rows + 8, 8):
        weave(
            i,
            *[acc[p, i : i + 8, :] + acc[p, high_rows + i : high_rows + i + 8, :] for p in range(2)],
        )

    @pl.when(lax.axis_index("rows") == lax.axis_size("rows") - 1)
    def _():
        tail = grid[rows - 8 : rows, :]
        sub8 = lax.broadcasted_iota(I32, (8, wide), 0)
        spill_row = jnp.broadcast_to(grid[rows : rows + 1, :], (8, wide))
        grid[rows - 8 : rows, :] = tail + jnp.where(sub8 == 7, spill_row, 0.0)
        grid[rows : rows + 8, :] = jnp.zeros((8, wide), F32)

    @pl.when(lax.axis_index("cols") == lax.axis_size("cols") - 1)
    def _():
        for i in range(0, rows + 8, 8):
            line = grid[i : i + 8, :]
            moved = jnp.where(lane == cols - 1, pltpu.roll(line, wide - 1, 1), 0.0)
            grid[i : i + 8, :] = jnp.where(lane < cols, line + moved, 0.0)


def own_deposit_kernel(rows, cols, cap, n_cols, first, *refs):
    pieces, refs = refs[:n_cols], refs[n_cols:]
    if first:
        acc_out, beside_out, masses, moves, *scratch, slots = refs
    else:
        masses, acc_out, beside_out, moves, *scratch, slots = refs
    size = 2 * cap
    for k in range(n_cols):
        moves[k * size : (k + 1) * size, :] = pieces[k][0:size, :]
        if first:
            masses[k * size : (k + 1) * size, :] = pieces[k][size : 2 * size, :]
    for ref in (moves, masses) if first else (moves,):
        ref[n_cols * size :, :] = jnp.zeros((size, 128), F32)
    acc_out[...] = jnp.zeros(acc_out.shape, F32)
    beside_out[...] = jnp.zeros(beside_out.shape, F32)
    deposit_blocks(
        rows, cols, cap, n_cols, moves, masses, (acc_out, beside_out, *scratch), slots
    )


def other_deposit(rows, cols, cap, n_cols, first, came, acc_in, beside_in, masses, grid, scratch):
    moves, acc, beside, *rest, slots = scratch
    size = 2 * cap
    step = 2 * size if first else size
    for index, ref in enumerate(came):
        for k in range(n_cols):
            at = (index * n_cols + k) * size
            moves[at : at + size, :] = ref[k * step : k * step + size, :]
            if first:
                masses[at : at + size, :] = ref[k * step + size : (k + 1) * step, :]
    for ref in (moves, masses) if first else (moves,):
        ref[2 * n_cols * size :, :] = jnp.zeros((size, 128), F32)
    acc[...] = acc_in[...]
    beside[...] = beside_in[...]
    deposit_blocks(
        rows, cols, cap, 2 * n_cols, moves, masses, (acc, beside, *rest), slots
    )
    finish_grid(rows, cols, acc, beside, grid)


def first_deposit_kernel(rows, cols, cap, n_cols, *refs):
    ra_ref, rb_ref, acc_in, beside_in, total_in = refs[:5]
    grid, sa_ref, sb_ref, masses, total = refs[5:10]
    other_deposit(
        rows, cols, cap, n_cols, True, (ra_ref, rb_ref), acc_in, beside_in, masses, grid, refs[10:]
    )
    total[...] = total_in[...] + ra_ref[4 * cap * n_cols :, :]
    row_even = lax.axis_index("rows") % 2 == 0
    south_going = grid[rows - 7 : rows + 1, :]
    north_going = grid[0:8, :]
    sa_ref[...] = pick(row_even, south_going, north_going)
    sb_ref[...] = pick(row_even, north_going, south_going)


def last_deposit_kernel(rows, cols, cap, n_cols, *refs):
    ra_ref, rb_ref, acc_in, beside_in, masses, corner_ref = refs[:6]
    grid, row_ref, col_ref = refs[6:9]
    other_deposit(
        rows, cols, cap, n_cols, False, (ra_ref, rb_ref), acc_in, beside_in, masses, grid, refs[9:]
    )
    tail = 2 * cap * n_cols
    corner = corner_ref[0:1, :] + ra_ref[tail + 1 : tail + 2, :] + rb_ref[tail + 2 : tail + 3, :]
    corner = jnp.sum(corner, axis=1, keepdims=True)
    place = lax.broadcasted_iota(I32, (8, 128), 0) + lax.broadcasted_iota(I32, (8, 128), 1)
    row_ref[...] = grid[rows : rows + 8, 0:cols]
    row_ref[:, 0:128] = row_ref[:, 0:128] + jnp.where(place == 0, corner, 0.0)
    col_ref[...] = flipped(grid[0:rows, cols : cols + 128])[0:8]


def edge_mid_kernel(rows, cols, g_ref, a_ref, b_ref, d_ref, ca_ref, cb_ref):
    row_even = lax.axis_index("rows") % 2 == 0
    col_even = lax.axis_index("cols") % 2 == 0
    wide = cols + 128
    north = pick(row_even, b_ref[...], a_ref[...])
    south = pick(row_even, a_ref[...], b_ref[...])
    d_ref[0:PAD, :] = jnp.zeros((PAD, wide), F32)
    d_ref[PAD : PAD + rows, :] = g_ref[0:rows, :]
    d_ref[PAD + rows : PAD + rows + 8, :] = south + g_ref[rows : rows + 8, :]
    d_ref[PAD + rows + 8 :, :] = jnp.zeros((d_ref.shape[0] - PAD - rows - 8, wide), F32)
    d_ref[PAD - 7 : PAD + 1, :] = d_ref[PAD - 7 : PAD + 1, :] + north
    west_going = flipped(d_ref[:, 0:128])[0:EDGE]
    east_going = flipped(d_ref[:, cols - 128 : cols])[128 - EDGE : 128]
    spilled = flipped(d_ref[:, cols : cols + 128])[0:EDGE]
    ca_ref[0:EDGE, :] = pick(col_even, east_going, west_going)
    cb_ref[0:EDGE, :] = pick(col_even, west_going, east_going)
    ca_ref[EDGE:, :] = pick(col_even, spilled, 0.0)
    cb_ref[EDGE:, :] = pick(col_even, 0.0, spilled)


def final_kernel(rows, cols, g_ref, m_ref, row_in, col_in, total_ref, out_ref):
    n_rows, n_cols = lax.axis_size("rows"), lax.axis_size("cols")
    half_scale = 0.5 * ((rows * cols * n_rows * n_cols) / total_ref[0:1, 0:1])
    out_ref[...] = 0.5 * m_ref[...] + half_scale * g_ref[0:rows, 0:cols]
    out_ref[0:8, :] = out_ref[0:8, :] + half_scale * row_in[...]
    beside = jnp.concatenate([col_in[...], jnp.zeros((120, col_in.shape[1]), F32)], axis=0)
    out_ref[:, 0:128] = out_ref[:, 0:128] + half_scale * unflipped(beside, rows)


def exchange_columns(outs):
    came = {k: xor_permute(outs[k], "cols", k) for k in range(len(outs) - 1, 0, -1)}
    return [outs[0]] + [came[k] for k in range(1, len(outs))]


def exchange_rows(pieces, kinds, cap, extra_first, extra_second=None):
    step = kinds * cap
    first = [piece[step : 2 * step] for piece in pieces] + [extra_first]
    second = [piece[2 * step : 3 * step] for piece in pieces]
    if extra_second is not None:
        second.append(extra_second)
    return swap_both(jnp.concatenate(first), jnp.concatenate(second), "rows")


def body(terminal_value, density_start, start_cells, offsets, weights, dest_tiles, end_cells):
    rows, cols = terminal_value.shape
    n_rows, n_cols = lax.axis_size("rows"), lax.axis_size("cols")
    blocks = dest_tiles.shape[0]
    cap = blocks // 4
    chunks = 3 * n_cols
    wide, tall = cols + 128, rows + 2 * PAD
    flat = -(-tall // 128) * 128
    starts = start_cells.reshape(blocks, 128)
    wts = weights.reshape(blocks, 128)
    ends = end_cells.reshape(blocks, 128)
    arrays = (terminal_value, density_start, wts, starts, offsets, ends)
    *arrays, sa, sb, total = vmem_call(
        functools.partial(start_kernel, rows, len(arrays)),
        (
            *[shape(*x.shape, dtype=x.dtype) for x in arrays],
            shape(2 * EDGE, cols),
            shape(2 * EDGE, cols),
            shape(EDGE, 128),
        ),
        len(arrays),
        [pltpu.SemaphoreType.DMA((len(arrays),))],
        hbm_in=range(len(arrays)),
    )(*arrays)
    terminal_value, density_start, wts, starts, offsets, ends = arrays
    bits = [1 << i for i in range(1, n_rows.bit_length() - 1)]
    ra, rb = swap_both(sa, sb, "rows")
    more = xor_permute(total, "rows", bits[0])
    ue, me, ca, cb, total = vmem_call(
        functools.partial(start_mid_kernel, rows, cols),
        (
            shape(tall, wide),
            shape(tall, wide),
            shape(2 * EDGE, flat),
            shape(2 * EDGE, flat),
            shape(EDGE, 128),
        ),
        6,
    )(terminal_value, density_start, ra, rb, total, more)
    ca, cb = swap_both(ca, cb, "cols")
    for bit in bits[1:-1]:
        total = total + xor_permute(total, "rows", bit)
    more = xor_permute(total, "rows", bits[-1])
    sweep_scratch = [
        pltpu.VMEM((tall, wide), F32),
        pltpu.VMEM((tall, wide), F32),
    ]

    def sample_scratch(part_rows):
        return [
            pltpu.VMEM((2 * table_height(rows), cols // 2), BF16),
            pltpu.VMEM((2 * table_height(rows), cols // 2), BF16),
            pltpu.VMEM((table_height(rows), 128), F32),
            pltpu.VMEM((n_cols * part_rows + EDGE, 128), F32),
            pltpu.SMEM((blocks,), I32),
            pltpu.SMEM((blocks,), I32),
            pltpu.SMEM((chunks,), I32),
            pltpu.SMEM((blocks,), I32),
            pltpu.SemaphoreType.DMA(()),
        ]

    high_rows = table_height(rows)
    acc_shape = (2, 2 * high_rows, cols // 2)
    beside_shape = (rows + 8, 128)
    product_scratch = [
        pltpu.VMEM((2, GROUP, 2 * high_rows, 128), BF16),
        pltpu.VMEM((2, GROUP, cols // 2, 128), BF16),
    ] * 2

    def part_rows_of(chunk_count):
        return 2 * cap * (chunk_count + 1)

    own_scratch = [
        pltpu.VMEM((part_rows_of(n_cols), 128), F32),
        *product_scratch,
        pltpu.SMEM((n_cols * cap + 2 * GROUP,), I32),
    ]
    other_scratch = [
        pltpu.VMEM((part_rows_of(2 * n_cols), 128), F32),
        pltpu.VMEM(acc_shape, F32),
        pltpu.VMEM(beside_shape, F32),
        *product_scratch,
        pltpu.SMEM((2 * n_cols * cap + 2 * GROUP,), I32),
    ]
    carried = (shape(*acc_shape), shape(*beside_shape))
    part_rows = 12 * cap + EDGE
    *outs, ue, me = vmem_call(
        functools.partial(first_kernel, rows, cols, blocks, cap, n_cols),
        tuple([shape(part_rows, 128)] * n_cols + [shape(tall, wide)] * 2),
        11,
        sweep_scratch + sample_scratch(part_rows),
        hbm_in=(10,),
    )(ue, me, ca, cb, total, more, starts, offsets, wts, ends, dest_tiles)
    pieces = exchange_columns(outs)
    total = sum(piece[part_rows - EDGE :] for piece in pieces)
    ra, rb = exchange_rows(pieces, 4, cap, total)
    acc, beside, own_masses = vmem_call(
        functools.partial(own_deposit_kernel, rows, cols, cap, n_cols, True),
        (*carried, shape(part_rows_of(n_cols), 128)),
        n_cols,
        own_scratch,
    )(*pieces)
    grid, ea, eb, masses, total = vmem_call(
        functools.partial(first_deposit_kernel, rows, cols, cap, n_cols),
        (
            shape(rows + 8, wide),
            shape(8, wide),
            shape(8, wide),
            shape(part_rows_of(2 * n_cols), 128),
            shape(EDGE, 128),
        ),
        5,
        other_scratch,
    )(ra, rb, acc, beside, total)
    ea, eb = swap_both(ea, eb, "rows")
    deposit, ca, cb = vmem_call(
        functools.partial(edge_mid_kernel, rows, cols),
        (shape(tall, wide), shape(2 * EDGE, flat), shape(2 * EDGE, flat)),
        3,
    )(grid, ea, eb)
    ca, cb = swap_both(ca, cb, "cols")
    part_rows = 6 * cap + EDGE
    *outs, value, density = vmem_call(
        functools.partial(again_kernel, rows, cols, blocks, cap, n_cols),
        tuple([shape(part_rows, 128)] * n_cols + [shape(rows, cols)] * 2),
        11,
        sweep_scratch
        + [pltpu.VMEM((tall, wide), F32)]
        + sample_scratch(part_rows)
        + [pltpu.SemaphoreType.DMA(())],
        hbm_in=(10,),
        hbm_out=(n_cols,),
    )(ue, me, deposit, ca, cb, total, starts, offsets, wts, ends, dest_tiles)
    pieces = exchange_columns(outs)
    corner = sum(piece[part_rows - EDGE :] for piece in pieces)
    ra, rb = exchange_rows(pieces, 2, cap, corner, corner)
    acc, beside = vmem_call(
        functools.partial(own_deposit_kernel, rows, cols, cap, n_cols, False),
        carried,
        n_cols + 1,
        own_scratch,
    )(*pieces, own_masses)
    grid, below, beside = vmem_call(
        functools.partial(last_deposit_kernel, rows, cols, cap, n_cols),
        (shape(rows + 8, wide), shape(8, cols), shape(8, rows)),
        6,
        other_scratch,
    )(ra, rb, acc, beside, masses, corner)
    below = lax.ppermute(below, "rows", [(i, i + 1) for i in range(n_rows - 1)])
    beside = lax.ppermute(beside, "cols", [(i, i + 1) for i in range(n_cols - 1)])
    (density,) = vmem_call(
        functools.partial(final_kernel, rows, cols), (shape(rows, cols),), 5, keep=(0,)
    )(grid, density, below, beside, total)
    return (value, density)


def solution(mesh):
    in_specs = (
        P("rows", "cols"),
        P("rows", "cols"),
        P(("rows", "cols")),
        P(None, ("rows", "cols")),
        P(("rows", "cols")),
        P(("rows", "cols")),
        P(("rows", "cols")),
    )
    out_specs = (P("rows", "cols"), P("rows", "cols"))
    return jax.shard_map(body, mesh=mesh, in_specs=in_specs, out_specs=out_specs, check_vma=False)
```

```python
import functools
import jax
import jax.numpy as jnp
from jax import lax
from jax.experimental import pallas as pl
from jax.experimental.pallas import tpu as pltpu
from jax.sharding import PartitionSpec as P

HJB_STEPS = 4
ITERS = 2
F32, BF16, I32 = jnp.float32, jnp.bfloat16, jnp.int32

PAD = 16
EDGE = 8
GROUP = 4
UNROLL = 4
VMEM_LIMIT = 24 * 1024 * 1024


def swap_pairs(count):
    first = [(i, i ^ 1) for i in range(count)]
    second = [(i, ((i + 1) ^ 1) - 1) for i in range(1, count - 1)]
    return first, second


def swap_both(first, second, axis):
    pairs_a, pairs_b = swap_pairs(lax.axis_size(axis))
    return lax.ppermute(first, axis, pairs_a), lax.ppermute(second, axis, pairs_b)


def xor_permute(value, axis, bit):
    return lax.ppermute(value, axis, [(i, i ^ bit) for i in range(lax.axis_size(axis))])


def vmem_call(kernel, out_shape, n_in, scratch=(), hbm_in=(), hbm_out=(), keep=()):
    def spec(in_hbm):
        return pl.BlockSpec(memory_space=pltpu.HBM if in_hbm else pltpu.VMEM)

    results = [
        leaf if i in keep or i in hbm_out else pltpu.VMEM(leaf.shape, leaf.dtype)
        for i, leaf in enumerate(out_shape)
    ]
    call = pl.pallas_call(
        kernel,
        out_shape=results,
        in_specs=[spec(i in hbm_in) for i in range(n_in)],
        out_specs=[spec(i in hbm_out) for i in range(len(results))],
        scratch_shapes=list(scratch),
        compiler_params=pltpu.CompilerParams(vmem_limit_bytes=VMEM_LIMIT),
    )

    def run(*operands):
        return call(
            *[
                pltpu.with_memory_space_constraint(x, pltpu.HBM if i in hbm_in else pltpu.VMEM)
                for i, x in enumerate(operands)
            ]
        )

    return run


def shape(*dims, dtype=F32):
    return jax.ShapeDtypeStruct(dims, dtype)


def flipped(block):
    rows = block.shape[0]
    width = -(-rows // 128) * 128
    if width > rows:
        block = jnp.concatenate([block, jnp.zeros((width - rows, 128), F32)], axis=0)
    parts = [block[i : i + 128].T for i in range(0, width, 128)]
    return jnp.concatenate(parts, axis=1)


def unflipped(block, rows):
    parts = [block[:, i : i + 128].T for i in range(0, block.shape[1], 128)]
    return jnp.concatenate(parts, axis=0)[:rows]


def row_col(cell, cols):
    if cols & (cols - 1) == 0:
        return cell >> (cols.bit_length() - 1), cell & (cols - 1)
    return cell // cols, cell % cols


def pick(flag, one, other):
    return jnp.where(flag, one, other)


def start_kernel(rows, count, *refs):
    sources, copies = refs[:count], refs[count : 2 * count]
    sa_ref, sb_ref, sum_ref, sems = refs[2 * count :]
    moves = [
        pltpu.make_async_copy(src, dst, sems.at[i])
        for i, (src, dst) in enumerate(zip(sources, copies))
    ]
    for move in moves:
        move.start()
    for move in moves:
        move.wait()
    u_ref, m_ref, wts = copies[:3]
    row_even = lax.axis_index("rows") % 2 == 0
    for index, ref in enumerate((u_ref, m_ref)):
        part = slice(index * EDGE, (index + 1) * EDGE)
        south_going, north_going = ref[rows - EDGE : rows, :], ref[0:EDGE, :]
        sa_ref[part, :] = pick(row_even, south_going, north_going)
        sb_ref[part, :] = pick(row_even, north_going, south_going)
    total = jnp.sum(jnp.sum(wts[...], axis=0, keepdims=True), axis=1, keepdims=True)
    sum_ref[...] = jnp.broadcast_to(total, sum_ref.shape)


def start_mid_kernel(
    rows, cols, u_ref, m_ref, a_ref, b_ref, w_ref, v_ref, ue_ref, me_ref, ca_ref, cb_ref, sum_ref
):
    sum_ref[...] = w_ref[...] + v_ref[...]
    row_even = lax.axis_index("rows") % 2 == 0
    col_even = lax.axis_index("cols") % 2 == 0
    for index, (src, dst) in enumerate(((u_ref, ue_ref), (m_ref, me_ref))):
        dst[...] = jnp.zeros(dst.shape, F32)
        dst[PAD : PAD + rows, 0:cols] = src[...]
        part = slice(index * EDGE, (index + 1) * EDGE)
        north = pick(row_even, b_ref[part, :], a_ref[part, :])
        south = pick(row_even, a_ref[part, :], b_ref[part, :])
        dst[PAD - EDGE : PAD, 0:cols] = north
        dst[PAD + rows : PAD + rows + EDGE, 0:cols] = south
        west_going = flipped(dst[:, 0:128])[0:EDGE]
        east_going = flipped(dst[:, cols - 128 : cols])[128 - EDGE : 128]
        ca_ref[part, :] = pick(col_even, east_going, west_going)
        cb_ref[part, :] = pick(col_even, west_going, east_going)


def side_tile(left, right, width):
    return jnp.concatenate([right, jnp.zeros((128 - 2 * EDGE, width), F32), left], axis=0)


def hjb_sweep(rows, cols, ua, ub, m):
    wide = cols + 128
    tiles = wide // 128
    n_rows, n_cols = lax.axis_size("rows"), lax.axis_size("cols")
    sub = lax.broadcasted_iota(I32, (8, 128), 0)
    lane = lax.broadcasted_iota(I32, (8, 128), 1)
    top, bottom, first, last = sub == 0, sub == 7, lane == 0, lane == 127
    row_first = lax.axis_index("rows") * rows
    col = jnp.where(lane < 64, cols + lane, lane - 128) + lax.axis_index("cols") * cols
    side_ok = (col >= 0) & (col < cols * n_cols)
    src, dst = ua, ub

    def strip(i):
        return [src[i : i + 8, t * 128 : (t + 1) * 128] for t in range(tiles)]

    for step in range(HJB_STEPS):
        start, stop = PAD - 8, PAD + rows + 8
        here = strip(start)
        fell = [pltpu.roll(x, 1, 0) for x in here]
        rose = [pltpu.roll(x, 7, 0) for x in here]
        fell_before = fell
        for i in range(start, stop, 8):
            if i + 8 < stop:
                after = strip(i + 8)
                rose_after = [pltpu.roll(x, 7, 0) for x in after]
                fell_after = [pltpu.roll(x, 1, 0) for x in after]
            else:
                after, rose_after, fell_after = here, rose, fell
            row_ok = None
            if i < PAD or i >= PAD + rows:
                row = sub + (row_first + (i - PAD))
                row_ok = (row >= 0) & (row < rows * n_rows)
            went = [pltpu.roll(x, 1, 1) for x in here]
            came = [pltpu.roll(x, 127, 1) for x in here]
            for t in range(tiles):
                value = here[t]
                up = jnp.where(top, fell_before[t], fell[t])
                down = jnp.where(bottom, rose_after[t], rose[t])
                left = jnp.where(first, went[t - 1], went[t])
                right = jnp.where(last, came[(t + 1) % tiles], came[t])
                slope_x = jnp.maximum(value - jnp.minimum(up, down), 0.0)
                slope_y = jnp.maximum(value - jnp.minimum(left, right), 0.0)
                around = (up + down) + (left + right) + m[i : i + 8, t * 128 : (t + 1) * 128]
                new = 0.5 * value + 0.125 * (around - (slope_x * slope_x + slope_y * slope_y))
                ok = row_ok
                if t == tiles - 1:
                    ok = side_ok if ok is None else ok & side_ok
                dst[i : i + 8, t * 128 : (t + 1) * 128] = (
                    new if ok is None else jnp.where(ok, new, 0.0)
                )
            here, fell_before, fell, rose = after, fell, fell_after, rose_after
        src, dst = dst, src
    return src


def split(value):
    high = value.astype(BF16)
    return high, (value - high.astype(F32)).astype(BF16)


def lane_pick(value, index):
    dims = lax.GatherDimensionNumbers(
        offset_dims=(),
        collapsed_slice_dims=(1,),
        start_index_map=(1,),
        operand_batching_dims=(0,),
        start_indices_batching_dims=(0,),
    )
    return lax.gather(
        value, index[..., None], dims, (1, 1), mode=lax.GatherScatterMode.PROMISE_IN_BOUNDS
    )


def table_height(rows):
    return rows + 16


def fill_tables(rows, cols, u, tabs, halo):
    high_rows = table_height(rows)
    lane = lax.broadcasted_iota(I32, (8, 128), 1)
    lower = lane < 64
    for i in range(0, high_rows, 16):
        for parity in range(2):
            index = (2 * lane + parity) & 127
            for t in range(cols // 256):
                halves = []
                for j in range(2):
                    at = PAD + i + 8 * j
                    one = u[at : at + 8, 2 * t * 128 : (2 * t + 1) * 128]
                    two = u[at : at + 8, (2 * t + 1) * 128 : (2 * t + 2) * 128]
                    halves.append(
                        jnp.where(lower, lane_pick(one, index), lane_pick(two, index))
                    )
                high, low = split(jnp.concatenate(halves, axis=0))
                tabs[parity][i : i + 16, t * 128 : (t + 1) * 128] = high
                tabs[parity][high_rows + i : high_rows + i + 16, t * 128 : (t + 1) * 128] = low
        halo[i : i + 16, :] = jnp.broadcast_to(
            u[PAD + i : PAD + i + 16, cols : cols + 1], (16, 128)
        )


def sample_moves(
    rows, cols, blocks, cap, first, tabs, halo, starts, offs, wts, ends, dest, buf, slot_row,
    corner_row, counter
):
    n_cols = lax.axis_size("cols")
    my_row, my_col = lax.axis_index("rows"), lax.axis_index("cols")
    n_rows = lax.axis_size("rows")
    kinds = 4 if first else 2
    part_rows = 3 * kinds * cap + EDGE
    spare_row = n_cols * part_rows
    buf[...] = jnp.zeros(buf.shape, F32)
    for i in range(3 * n_cols):
        counter[i] = 0
    for b in range(blocks):
        tile = dest[b]
        band, column = tile // n_cols, tile % n_cols
        section = jnp.where(band == my_row, 0, jnp.where(band == (my_row ^ 1), 1, 2))
        distance = column ^ my_col
        rank = counter[distance * 3 + section]
        counter[distance * 3 + section] = rank + 1
        slot_row[b] = distance * part_rows + section * (kinds * cap) + rank
        if not first:
            goes = (band < n_rows - 1) & (column < n_cols - 1)
            row = ((column + 1) ^ my_col) * part_rows + 3 * kinds * cap + section
            corner_row[b] = jnp.where(goes, row, spare_row)

    high_rows = table_height(rows)
    sub16 = lax.broadcasted_iota(I32, (16, 256), 0)
    sub8 = lax.broadcasted_iota(I32, (8, 256), 0)
    one16, zero16 = jnp.ones((16, 256), BF16), jnp.zeros((16, 256), BF16)

    def step(j, carry):
        def pair(ref):
            return jnp.concatenate([ref[pl.ds(2 * j, 1), :], ref[pl.ds(2 * j + 1, 1), :]], axis=1)

        row, col = row_col(pair(starts), cols)
        lanes = pl.ds(pl.multiple_of(j * 256, 256), 256)
        off_x = offs[0:1, lanes]
        off_y = offs[1:2, lanes]
        odd = (col & 1) == 1
        line = []
        for tab, place in ((tabs[0], (col + 1) >> 1), (tabs[1], col >> 1)):
            at = (jnp.broadcast_to(place, (16, 256)) - sub16).astype(jnp.int16)
            hot = [jnp.where(at == 16 * i, one16, zero16) for i in range(cols // 32)]
            line.append(
                jnp.dot(tab[...], jnp.concatenate(hot, axis=0), preferred_element_type=F32)
            )
        frac_x = 0.5 + 0.45 * jnp.tanh(off_x)
        frac_y = 0.5 + 0.45 * jnp.tanh(off_y)
        blend = jnp.where(odd, 1.0 - frac_y, frac_y)
        edge = jnp.broadcast_to(col == cols - 1, (8, 256))
        row_at = jnp.broadcast_to(row, (8, 256)) - sub8
        near, far = jnp.broadcast_to(1.0 - frac_x, (8, 256)), jnp.broadcast_to(frac_x, (8, 256))
        sum_x, sum_y = jnp.zeros((8, 256), F32), jnp.zeros((8, 256), F32)
        for i in range(0, rows + 8, 8):
            even, odds = [
                both[i : i + 8] + both[high_rows + i : high_rows + i + 8] for both in line
            ]
            beyond = jnp.concatenate([halo[i : i + 8, :]] * 2, axis=1)
            even = jnp.where(edge, beyond, even)
            step_y = odds - even
            mixed = even + blend * step_y
            here, below = row_at == i, row_at == i - 1
            sum_x = sum_x + jnp.where(below, mixed, jnp.where(here, -mixed, 0.0))
            sum_y = sum_y + step_y * jnp.where(here, near, jnp.where(below, far, 0.0))
        grad_x = jnp.sum(sum_x, axis=0, keepdims=True)
        grad_y = jnp.sum(sum_y, axis=0, keepdims=True)
        grad_y = jnp.where(odd, -grad_y, grad_y)
        moved_x = 0.5 + 0.45 * jnp.tanh(off_x - grad_x)
        moved_y = 0.5 + 0.45 * jnp.tanh(off_y - grad_y)
        out = [moved_x, moved_y]
        if first:
            out += [pair(wts), (pair(ends) + 1).astype(F32)]
        else:
            corner = jnp.where(pair(ends) == rows * cols - 1, pair(wts) * moved_x * moved_y, 0.0)
        for half in range(2):
            if not first:
                buf[pl.ds(corner_row[2 * j + half], 1), :] += corner[:, half * 128 : (half + 1) * 128]
            base = slot_row[2 * j + half]
            for q, value in enumerate(out):
                buf[pl.ds(base + q * cap, 1), :] = value[:, half * 128 : (half + 1) * 128]
        return carry

    lax.fori_loop(0, blocks // 2, step, 0, unroll=UNROLL)


def first_kernel(
    rows, cols, blocks, cap, n_cols, *refs
):
    (ue_in, me_in, ra_ref, rb_ref, w_ref, v_ref, starts, offs, wts, ends, dest_hbm) = refs[:11]
    outs = refs[11 : 11 + n_cols]
    ue_ref, me_ref = refs[11 + n_cols : 13 + n_cols]
    ua, ub, tab_even, tab_odd, halo, buf, slot_row, corner_row, counter, dest, sem = refs[13 + n_cols :]
    fetch = pltpu.make_async_copy(dest_hbm, dest, sem)
    fetch.start()
    col_even = lax.axis_index("cols") % 2 == 0
    tall = ue_in.shape[0]
    width = ra_ref.shape[1]
    for index, (src, dst) in enumerate(((ue_in, ue_ref), (me_in, me_ref))):
        part = slice(index * EDGE, (index + 1) * EDGE)
        west = pick(col_even, rb_ref[part, :], ra_ref[part, :])
        east = pick(col_even, ra_ref[part, :], rb_ref[part, :])
        dst[:, 0:cols] = src[:, 0:cols]
        dst[:, cols : cols + 128] = unflipped(side_tile(west, east, width), tall)
    ua[...] = ue_ref[...]
    ub[...] = jnp.zeros(ub.shape, F32)
    u = hjb_sweep(rows, cols, ua, ub, me_ref)
    tabs = (tab_even, tab_odd)
    fill_tables(rows, cols, u, tabs, halo)
    fetch.wait()
    sample_moves(
        rows, cols, blocks, cap, True, tabs, halo, starts, offs, wts, ends, dest, buf, slot_row,
        corner_row, counter,
    )
    part_rows = 12 * cap + EDGE
    for k in range(n_cols):
        out = outs[(n_cols - k) % n_cols]
        out[0 : part_rows - EDGE, :] = buf[k * part_rows : (k + 1) * part_rows - EDGE, :]
        out[part_rows - EDGE :, :] = w_ref[...] + v_ref[...]


def again_kernel(rows, cols, blocks, cap, n_cols, *refs):
    (ue_ref, m_in, d_ref, ra_ref, rb_ref, total_ref) = refs[:6]
    (starts, offs, wts, ends, dest_hbm) = refs[6:11]
    outs = refs[11 : 11 + n_cols]
    value_hbm, density_ref = refs[11 + n_cols : 13 + n_cols]
    (ua, ub, m, tab_even, tab_odd, halo, buf, slot_row, corner_row, counter, dest, sem, value_sem) = (
        refs[13 + n_cols :]
    )
    fetch = pltpu.make_async_copy(dest_hbm, dest, sem)
    fetch.start()
    col_even = lax.axis_index("cols") % 2 == 0
    n_rows = lax.axis_size("rows")
    tall = ue_ref.shape[0]
    width = ra_ref.shape[1]
    half_scale = 0.5 * ((rows * cols * n_rows * n_cols) / total_ref[0:1, 0:1])
    west = pick(col_even, rb_ref[...], ra_ref[...])
    east = pick(col_even, ra_ref[...], rb_ref[...])
    side = unflipped(side_tile(west[0:EDGE], east[0:EDGE], width), tall)
    pushed = unflipped(
        jnp.concatenate([west[EDGE : 2 * EDGE], jnp.zeros((128 - EDGE, width), F32)], axis=0), tall
    )
    m[:, 0:128] = 0.5 * m_in[:, 0:128] + half_scale * (d_ref[:, 0:128] + pushed)
    m[:, 128:cols] = 0.5 * m_in[:, 128:cols] + half_scale * d_ref[:, 128:cols]
    m[:, cols : cols + 128] = 0.5 * m_in[:, cols : cols + 128] + half_scale * (
        d_ref[:, cols : cols + 128] + side
    )
    density_ref[...] = m[PAD : PAD + rows, 0:cols]
    ua[...] = ue_ref[...]
    ub[...] = jnp.zeros(ub.shape, F32)
    u = hjb_sweep(rows, cols, ua, ub, m)
    leave = pltpu.make_async_copy(u.at[PAD : PAD + rows, 0:cols], value_hbm, value_sem)
    leave.start()
    tabs = (tab_even, tab_odd)
    fill_tables(rows, cols, u, tabs, halo)
    fetch.wait()
    sample_moves(
        rows, cols, blocks, cap, False, tabs, halo, starts, offs, wts, ends, dest, buf, slot_row,
        corner_row, counter,
    )
    part_rows = 6 * cap + EDGE
    for k in range(n_cols):
        outs[(n_cols - k) % n_cols][...] = buf[k * part_rows : (k + 1) * part_rows, :]
    leave.wait()


def deposit_blocks(rows, cols, cap, chunks, moves, masses, scratch, slots):
    acc, beside = scratch
    counts = []
    for q in range(chunks):
        cells = masses[(2 * q + 1) * cap : (2 * q + 2) * cap, :]
        counts.append(jnp.sum(jnp.where(cells > 0.5, 1.0, 0.0)).astype(I32) // 128)
    base = jnp.int32(0)
    for q in range(chunks):
        for rank in range(cap):
            slots[base + rank] = 2 * q * cap + rank
        base = base + counts[q]
    for rank in range(2 * GROUP):
        slots[base + rank] = 2 * chunks * cap
    high_rows = table_height(rows)
    sub16 = lax.broadcasted_iota(I32, (16, 128), 0)
    sub8 = lax.broadcasted_iota(I32, (8, 128), 0)
    one16, zero16 = jnp.ones((16, 128), BF16), jnp.zeros((16, 128), BF16)

    def relative(line, sub):
        return jnp.broadcast_to(line, sub.shape) - sub

    def build(first_slot):
        edges, left, right = [], ([], []), ([], [])
        for t in range(GROUP):
            at = slots[first_slot + t]
            move_x = moves[pl.ds(at, 1), :]
            move_y = moves[pl.ds(at + cap, 1), :]
            mass = masses[pl.ds(at, 1), :]
            row, col = row_col(masses[pl.ds(at + cap, 1), :].astype(I32) - 1, cols)
            odd = (col & 1) == 1
            stay, go = mass * (1.0 - move_x), mass * move_x
            row_at = relative(row, sub16).astype(jnp.int16)
            values = []
            for parity in range(2):
                share = jnp.where(odd == (parity == 1), 1.0 - move_y, move_y)
                first, second = stay * share, go * share
                if parity == 0:
                    edge_row = jnp.where(col == cols - 1, row, -2)
                    edges.append((relative(edge_row, sub8), first, second))
                for one, two in zip(split(first), split(second)):
                    values.append(
                        [jnp.broadcast_to(x.astype(F32), (16, 128)).astype(BF16) for x in (one, two)]
                    )
            tiles = [[], [], [], []]
            for i in range(high_rows // 16):
                here, below = row_at == 16 * i, row_at == 16 * i - 1
                for index, (one, two) in enumerate(values):
                    tiles[index].append(jnp.where(here, one, jnp.where(below, two, zero16)))
            for parity in range(2):
                left[parity].append(
                    jnp.concatenate(tiles[2 * parity] + tiles[2 * parity + 1], axis=0)
                )
            for parity, place in ((0, (col + 1) >> 1), (1, col >> 1)):
                place_at = relative(place, sub16).astype(jnp.int16)
                hot = [jnp.where(place_at == 16 * i, one16, zero16) for i in range(cols // 32)]
                right[parity].append(jnp.concatenate(hot, axis=0))
        for i in range(rows // 8 + 1):
            total = beside[8 * i : 8 * i + 8, :]
            for row_at, first, second in edges:
                total = total + jnp.where(
                    row_at == 8 * i, first, jnp.where(row_at == 8 * i - 1, second, 0.0)
                )
            beside[8 * i : 8 * i + 8, :] = total
        for parity in range(2):
            acc[parity] += lax.dot_general(
                jnp.concatenate(left[parity], axis=1),
                jnp.concatenate(right[parity], axis=1),
                (((1,), (1,)), ((), ())),
                preferred_element_type=F32,
            )

    def step(g, carry):
        for part in range(2):
            build((2 * g + part) * GROUP)
        return carry

    lax.fori_loop(0, (base + 2 * GROUP - 1) // (2 * GROUP), step, 0)


def finish_grid(rows, cols, acc, beside, grid):
    high_rows = table_height(rows)
    wide = cols + 128
    lane = lax.broadcasted_iota(I32, (8, wide), 1)
    lane1 = lax.broadcasted_iota(I32, (8, 128), 1)
    odd_lane = (lane1 & 1) == 1
    half = lane1 >> 1

    def weave(i, even, odd):
        for t in range(cols // 128):
            index = half + 64 * (t % 2)
            at = slice((t // 2) * 128, (t // 2 + 1) * 128)
            grid[i : i + 8, t * 128 : (t + 1) * 128] = jnp.where(
                odd_lane, lane_pick(odd[:, at], index), lane_pick(even[:, at], index)
            )
        right = jnp.sum(beside[i : i + 8, :], axis=1, keepdims=True)
        grid[i : i + 8, cols:wide] = jnp.where(lane1 == 0, right, 0.0)

    for i in range(0, rows + 8, 8):
        weave(
            i,
            *[acc[p, i : i + 8, :] + acc[p, high_rows + i : high_rows + i + 8, :] for p in range(2)],
        )

    @pl.when(lax.axis_index("rows") == lax.axis_size("rows") - 1)
    def _():
        tail = grid[rows - 8 : rows, :]
        sub8 = lax.broadcasted_iota(I32, (8, wide), 0)
        spill_row = jnp.broadcast_to(grid[rows : rows + 1, :], (8, wide))
        grid[rows - 8 : rows, :] = tail + jnp.where(sub8 == 7, spill_row, 0.0)
        grid[rows : rows + 8, :] = jnp.zeros((8, wide), F32)

    @pl.when(lax.axis_index("cols") == lax.axis_size("cols") - 1)
    def _():
        for i in range(0, rows + 8, 8):
            line = grid[i : i + 8, :]
            moved = jnp.where(lane == cols - 1, pltpu.roll(line, wide - 1, 1), 0.0)
            grid[i : i + 8, :] = jnp.where(lane < cols, line + moved, 0.0)


def own_deposit_kernel(rows, cols, cap, n_cols, first, *refs):
    pieces, refs = refs[:n_cols], refs[n_cols:]
    if first:
        acc_out, beside_out, masses, moves, *scratch, slots = refs
    else:
        masses, acc_out, beside_out, moves, *scratch, slots = refs
    size = 2 * cap
    for k in range(n_cols):
        moves[k * size : (k + 1) * size, :] = pieces[k][0:size, :]
        if first:
            masses[k * size : (k + 1) * size, :] = pieces[k][size : 2 * size, :]
    for ref in (moves, masses) if first else (moves,):
        ref[n_cols * size :, :] = jnp.zeros((size, 128), F32)
    acc_out[...] = jnp.zeros(acc_out.shape, F32)
    beside_out[...] = jnp.zeros(beside_out.shape, F32)
    deposit_blocks(
        rows, cols, cap, n_cols, moves, masses, (acc_out, beside_out, *scratch), slots
    )


def other_deposit(rows, cols, cap, n_cols, first, came, acc_in, beside_in, masses, grid, scratch):
    moves, acc, beside, *rest, slots = scratch
    size = 2 * cap
    step = 2 * size if first else size
    for index, ref in enumerate(came):
        for k in range(n_cols):
            at = (index * n_cols + k) * size
            moves[at : at + size, :] = ref[k * step : k * step + size, :]
            if first:
                masses[at : at + size, :] = ref[k * step + size : (k + 1) * step, :]
    for ref in (moves, masses) if first else (moves,):
        ref[2 * n_cols * size :, :] = jnp.zeros((size, 128), F32)
    acc[...] = acc_in[...]
    beside[...] = beside_in[...]
    deposit_blocks(
        rows, cols, cap, 2 * n_cols, moves, masses, (acc, beside, *rest), slots
    )
    finish_grid(rows, cols, acc, beside, grid)


def first_deposit_kernel(rows, cols, cap, n_cols, *refs):
    ra_ref, rb_ref, acc_in, beside_in, total_in = refs[:5]
    grid, sa_ref, sb_ref, masses, total = refs[5:10]
    other_deposit(
        rows, cols, cap, n_cols, True, (ra_ref, rb_ref), acc_in, beside_in, masses, grid, refs[10:]
    )
    total[...] = total_in[...] + ra_ref[4 * cap * n_cols :, :]
    row_even = lax.axis_index("rows") % 2 == 0
    south_going = grid[rows - 7 : rows + 1, :]
    north_going = grid[0:8, :]
    sa_ref[...] = pick(row_even, south_going, north_going)
    sb_ref[...] = pick(row_even, north_going, south_going)


def last_deposit_kernel(rows, cols, cap, n_cols, *refs):
    ra_ref, rb_ref, acc_in, beside_in, masses, corner_ref = refs[:6]
    grid, row_ref, col_ref = refs[6:9]
    other_deposit(
        rows, cols, cap, n_cols, False, (ra_ref, rb_ref), acc_in, beside_in, masses, grid, refs[9:]
    )
    tail = 2 * cap * n_cols
    corner = corner_ref[0:1, :] + ra_ref[tail + 1 : tail + 2, :] + rb_ref[tail + 2 : tail + 3, :]
    corner = jnp.sum(corner, axis=1, keepdims=True)
    place = lax.broadcasted_iota(I32, (8, 128), 0) + lax.broadcasted_iota(I32, (8, 128), 1)
    row_ref[...] = grid[rows : rows + 8, 0:cols]
    row_ref[:, 0:128] = row_ref[:, 0:128] + jnp.where(place == 0, corner, 0.0)
    col_ref[...] = flipped(grid[0:rows, cols : cols + 128])[0:8]


def edge_mid_kernel(rows, cols, g_ref, a_ref, b_ref, d_ref, ca_ref, cb_ref):
    row_even = lax.axis_index("rows") % 2 == 0
    col_even = lax.axis_index("cols") % 2 == 0
    wide = cols + 128
    north = pick(row_even, b_ref[...], a_ref[...])
    south = pick(row_even, a_ref[...], b_ref[...])
    d_ref[0:PAD, :] = jnp.zeros((PAD, wide), F32)
    d_ref[PAD : PAD + rows, :] = g_ref[0:rows, :]
    d_ref[PAD + rows : PAD + rows + 8, :] = south + g_ref[rows : rows + 8, :]
    d_ref[PAD + rows + 8 :, :] = jnp.zeros((d_ref.shape[0] - PAD - rows - 8, wide), F32)
    d_ref[PAD - 7 : PAD + 1, :] = d_ref[PAD - 7 : PAD + 1, :] + north
    west_going = flipped(d_ref[:, 0:128])[0:EDGE]
    east_going = flipped(d_ref[:, cols - 128 : cols])[128 - EDGE : 128]
    spilled = flipped(d_ref[:, cols : cols + 128])[0:EDGE]
    ca_ref[0:EDGE, :] = pick(col_even, east_going, west_going)
    cb_ref[0:EDGE, :] = pick(col_even, west_going, east_going)
    ca_ref[EDGE:, :] = pick(col_even, spilled, 0.0)
    cb_ref[EDGE:, :] = pick(col_even, 0.0, spilled)


def final_kernel(rows, cols, g_ref, m_ref, row_in, col_in, total_ref, out_ref):
    n_rows, n_cols = lax.axis_size("rows"), lax.axis_size("cols")
    half_scale = 0.5 * ((rows * cols * n_rows * n_cols) / total_ref[0:1, 0:1])
    out_ref[...] = 0.5 * m_ref[...] + half_scale * g_ref[0:rows, 0:cols]
    out_ref[0:8, :] = out_ref[0:8, :] + half_scale * row_in[...]
    beside = jnp.concatenate([col_in[...], jnp.zeros((120, col_in.shape[1]), F32)], axis=0)
    out_ref[:, 0:128] = out_ref[:, 0:128] + half_scale * unflipped(beside, rows)


def exchange_columns(outs):
    came = [xor_permute(part, "cols", len(outs) - i) for i, part in enumerate(outs) if i > 0]
    return [outs[0]] + came


def exchange_rows(pieces, kinds, cap, extra_first, extra_second=None):
    step = kinds * cap
    first = [piece[step : 2 * step] for piece in pieces] + [extra_first]
    second = [piece[2 * step : 3 * step] for piece in pieces]
    if extra_second is not None:
        second.append(extra_second)
    return swap_both(jnp.concatenate(first), jnp.concatenate(second), "rows")


def body(terminal_value, density_start, start_cells, offsets, weights, dest_tiles, end_cells):
    rows, cols = terminal_value.shape
    n_rows, n_cols = lax.axis_size("rows"), lax.axis_size("cols")
    blocks = dest_tiles.shape[0]
    cap = blocks // 4
    chunks = 3 * n_cols
    wide, tall = cols + 128, rows + 2 * PAD
    flat = -(-tall // 128) * 128
    starts = start_cells.reshape(blocks, 128)
    wts = weights.reshape(blocks, 128)
    ends = end_cells.reshape(blocks, 128)
    arrays = (terminal_value, density_start, wts, starts, offsets, ends)
    *arrays, sa, sb, total = vmem_call(
        functools.partial(start_kernel, rows, len(arrays)),
        (
            *[shape(*x.shape, dtype=x.dtype) for x in arrays],
            shape(2 * EDGE, cols),
            shape(2 * EDGE, cols),
            shape(EDGE, 128),
        ),
        len(arrays),
        [pltpu.SemaphoreType.DMA((len(arrays),))],
        hbm_in=range(len(arrays)),
    )(*arrays)
    terminal_value, density_start, wts, starts, offsets, ends = arrays
    bits = [1 << i for i in range(1, n_rows.bit_length() - 1)]
    ra, rb = swap_both(sa, sb, "rows")
    more = xor_permute(total, "rows", bits[0])
    ue, me, ca, cb, total = vmem_call(
        functools.partial(start_mid_kernel, rows, cols),
        (
            shape(tall, wide),
            shape(tall, wide),
            shape(2 * EDGE, flat),
            shape(2 * EDGE, flat),
            shape(EDGE, 128),
        ),
        6,
    )(terminal_value, density_start, ra, rb, total, more)
    ca, cb = swap_both(ca, cb, "cols")
    for bit in bits[1:-1]:
        total = total + xor_permute(total, "rows", bit)
    more = xor_permute(total, "rows", bits[-1])
    sweep_scratch = [
        pltpu.VMEM((tall, wide), F32),
        pltpu.VMEM((tall, wide), F32),
    ]

    def sample_scratch(part_rows):
        return [
            pltpu.VMEM((2 * table_height(rows), cols // 2), BF16),
            pltpu.VMEM((2 * table_height(rows), cols // 2), BF16),
            pltpu.VMEM((table_height(rows), 128), F32),
            pltpu.VMEM((n_cols * part_rows + EDGE, 128), F32),
            pltpu.SMEM((blocks,), I32),
            pltpu.SMEM((blocks,), I32),
            pltpu.SMEM((chunks,), I32),
            pltpu.SMEM((blocks,), I32),
            pltpu.SemaphoreType.DMA(()),
        ]

    high_rows = table_height(rows)
    acc_shape = (2, 2 * high_rows, cols // 2)
    beside_shape = (rows + 8, 128)

    def part_rows_of(chunk_count):
        return 2 * cap * (chunk_count + 1)

    own_scratch = [
        pltpu.VMEM((part_rows_of(n_cols), 128), F32),
        pltpu.SMEM((n_cols * cap + 2 * GROUP,), I32),
    ]
    other_scratch = [
        pltpu.VMEM((part_rows_of(2 * n_cols), 128), F32),
        pltpu.VMEM(acc_shape, F32),
        pltpu.VMEM(beside_shape, F32),
        pltpu.SMEM((2 * n_cols * cap + 2 * GROUP,), I32),
    ]
    carried = (shape(*acc_shape), shape(*beside_shape))
    part_rows = 12 * cap + EDGE
    *outs, ue, me = vmem_call(
        functools.partial(first_kernel, rows, cols, blocks, cap, n_cols),
        tuple([shape(part_rows, 128)] * n_cols + [shape(tall, wide)] * 2),
        11,
        sweep_scratch + sample_scratch(part_rows),
        hbm_in=(10,),
    )(ue, me, ca, cb, total, more, starts, offsets, wts, ends, dest_tiles)
    pieces = exchange_columns(outs)
    total = sum(piece[part_rows - EDGE :] for piece in pieces)
    ra, rb = exchange_rows(pieces, 4, cap, total)
    acc, beside, own_masses = vmem_call(
        functools.partial(own_deposit_kernel, rows, cols, cap, n_cols, True),
        (*carried, shape(part_rows_of(n_cols), 128)),
        n_cols,
        own_scratch,
    )(*pieces)
    grid, ea, eb, masses, total = vmem_call(
        functools.partial(first_deposit_kernel, rows, cols, cap, n_cols),
        (
            shape(rows + 8, wide),
            shape(8, wide),
            shape(8, wide),
            shape(part_rows_of(2 * n_cols), 128),
            shape(EDGE, 128),
        ),
        5,
        other_scratch,
    )(ra, rb, acc, beside, total)
    ea, eb = swap_both(ea, eb, "rows")
    deposit, ca, cb = vmem_call(
        functools.partial(edge_mid_kernel, rows, cols),
        (shape(tall, wide), shape(2 * EDGE, flat), shape(2 * EDGE, flat)),
        3,
    )(grid, ea, eb)
    ca, cb = swap_both(ca, cb, "cols")
    part_rows = 6 * cap + EDGE
    *outs, value, density = vmem_call(
        functools.partial(again_kernel, rows, cols, blocks, cap, n_cols),
        tuple([shape(part_rows, 128)] * n_cols + [shape(rows, cols)] * 2),
        11,
        sweep_scratch
        + [pltpu.VMEM((tall, wide), F32)]
        + sample_scratch(part_rows)
        + [pltpu.SemaphoreType.DMA(())],
        hbm_in=(10,),
        hbm_out=(n_cols,),
    )(ue, me, deposit, ca, cb, total, starts, offsets, wts, ends, dest_tiles)
    pieces = exchange_columns(outs)
    corner = sum(piece[part_rows - EDGE :] for piece in pieces)
    ra, rb = exchange_rows(pieces, 2, cap, corner, corner)
    acc, beside = vmem_call(
        functools.partial(own_deposit_kernel, rows, cols, cap, n_cols, False),
        carried,
        n_cols + 1,
        own_scratch,
    )(*pieces, own_masses)
    grid, below, beside = vmem_call(
        functools.partial(last_deposit_kernel, rows, cols, cap, n_cols),
        (shape(rows + 8, wide), shape(8, cols), shape(8, rows)),
        6,
        other_scratch,
    )(ra, rb, acc, beside, masses, corner)
    below = lax.ppermute(below, "rows", [(i, i + 1) for i in range(n_rows - 1)])
    beside = lax.ppermute(beside, "cols", [(i, i + 1) for i in range(n_cols - 1)])
    (density,) = vmem_call(
        functools.partial(final_kernel, rows, cols), (shape(rows, cols),), 5, keep=(0,)
    )(grid, density, below, beside, total)
    return (value, density)


def solution(mesh):
    in_specs = (
        P("rows", "cols"),
        P("rows", "cols"),
        P(("rows", "cols")),
        P(None, ("rows", "cols")),
        P(("rows", "cols")),
        P(("rows", "cols")),
        P(("rows", "cols")),
    )
    out_specs = (P("rows", "cols"), P("rows", "cols"))
    return jax.shard_map(body, mesh=mesh, in_specs=in_specs, out_specs=out_specs, check_vma=False)
```

```python
import functools
import jax
import jax.numpy as jnp
from jax import lax
from jax.experimental import pallas as pl
from jax.experimental.pallas import tpu as pltpu
from jax.sharding import PartitionSpec as P

HJB_STEPS = 4
ITERS = 2
F32, BF16, I32 = jnp.float32, jnp.bfloat16, jnp.int32

PAD = 16
EDGE = 8
GROUP = 4
UNROLL = 4
VMEM_LIMIT = 24 * 1024 * 1024


def swap_pairs(count):
    first = [(i, i ^ 1) for i in range(count)]
    second = [(i, ((i + 1) ^ 1) - 1) for i in range(1, count - 1)]
    return first, second


def swap_both(first, second, axis):
    pairs_a, pairs_b = swap_pairs(lax.axis_size(axis))
    return lax.ppermute(first, axis, pairs_a), lax.ppermute(second, axis, pairs_b)


def xor_permute(value, axis, bit):
    return lax.ppermute(value, axis, [(i, i ^ bit) for i in range(lax.axis_size(axis))])


def vmem_call(kernel, out_shape, n_in, scratch=(), hbm_in=(), hbm_out=(), keep=()):
    def spec(in_hbm):
        return pl.BlockSpec(memory_space=pltpu.HBM if in_hbm else pltpu.VMEM)

    results = [
        leaf if i in keep or i in hbm_out else pltpu.VMEM(leaf.shape, leaf.dtype)
        for i, leaf in enumerate(out_shape)
    ]
    call = pl.pallas_call(
        kernel,
        out_shape=results,
        in_specs=[spec(i in hbm_in) for i in range(n_in)],
        out_specs=[spec(i in hbm_out) for i in range(len(results))],
        scratch_shapes=list(scratch),
        compiler_params=pltpu.CompilerParams(vmem_limit_bytes=VMEM_LIMIT),
    )

    def run(*operands):
        return call(
            *[
                pltpu.with_memory_space_constraint(x, pltpu.HBM if i in hbm_in else pltpu.VMEM)
                for i, x in enumerate(operands)
            ]
        )

    return run


def shape(*dims, dtype=F32):
    return jax.ShapeDtypeStruct(dims, dtype)


def flipped(block):
    rows = block.shape[0]
    width = -(-rows // 128) * 128
    if width > rows:
        block = jnp.concatenate([block, jnp.zeros((width - rows, 128), F32)], axis=0)
    parts = [block[i : i + 128].T for i in range(0, width, 128)]
    return jnp.concatenate(parts, axis=1)


def unflipped(block, rows):
    parts = [block[:, i : i + 128].T for i in range(0, block.shape[1], 128)]
    return jnp.concatenate(parts, axis=0)[:rows]


def row_col(cell, cols):
    if cols & (cols - 1) == 0:
        return cell >> (cols.bit_length() - 1), cell & (cols - 1)
    return cell // cols, cell % cols


def pick(flag, one, other):
    return jnp.where(flag, one, other)


def start_kernel(rows, count, *refs):
    sources, copies = refs[:count], refs[count : 2 * count]
    sa_ref, sb_ref, sems = refs[2 * count :]
    moves = [
        pltpu.make_async_copy(src, dst, sems.at[i])
        for i, (src, dst) in enumerate(zip(sources, copies))
    ]
    for move in moves:
        move.start()
    for move in moves:
        move.wait()
    u_ref, m_ref, wts = copies[:3]
    row_even = lax.axis_index("rows") % 2 == 0
    for index, ref in enumerate((u_ref, m_ref)):
        part = slice(index * EDGE, (index + 1) * EDGE)
        south_going, north_going = ref[rows - EDGE : rows, :], ref[0:EDGE, :]
        sa_ref[part, :] = pick(row_even, south_going, north_going)
        sb_ref[part, :] = pick(row_even, north_going, south_going)
    total = jnp.sum(jnp.sum(wts[...], axis=0, keepdims=True), axis=1, keepdims=True)
    sa_ref[2 * EDGE :, :] = jnp.broadcast_to(total, (EDGE, sa_ref.shape[1]))


def start_mid_kernel(
    rows, cols, u_ref, m_ref, a_ref, b_ref, s_ref, ue_ref, me_ref, ca_ref, cb_ref, sum_ref
):
    sum_ref[...] = s_ref[2 * EDGE :, 0:128] + a_ref[2 * EDGE :, 0:128]
    row_even = lax.axis_index("rows") % 2 == 0
    col_even = lax.axis_index("cols") % 2 == 0
    for index, (src, dst) in enumerate(((u_ref, ue_ref), (m_ref, me_ref))):
        dst[...] = jnp.zeros(dst.shape, F32)
        dst[PAD : PAD + rows, 0:cols] = src[...]
        part = slice(index * EDGE, (index + 1) * EDGE)
        north = pick(row_even, b_ref[part, :], a_ref[part, :])
        south = pick(row_even, a_ref[part, :], b_ref[part, :])
        dst[PAD - EDGE : PAD, 0:cols] = north
        dst[PAD + rows : PAD + rows + EDGE, 0:cols] = south
        west_going = flipped(dst[:, 0:128])[0:EDGE]
        east_going = flipped(dst[:, cols - 128 : cols])[128 - EDGE : 128]
        ca_ref[part, :] = pick(col_even, east_going, west_going)
        cb_ref[part, :] = pick(col_even, west_going, east_going)


def side_tile(left, right, width):
    return jnp.concatenate([right, jnp.zeros((128 - 2 * EDGE, width), F32), left], axis=0)


def hjb_sweep(rows, cols, ua, ub, m, between):
    wide = cols + 128
    tiles = wide // 128
    n_rows, n_cols = lax.axis_size("rows"), lax.axis_size("cols")
    sub = lax.broadcasted_iota(I32, (8, 128), 0)
    lane = lax.broadcasted_iota(I32, (8, 128), 1)
    top, bottom, first, last = sub == 0, sub == 7, lane == 0, lane == 127
    row_first = lax.axis_index("rows") * rows
    col = jnp.where(lane < 64, cols + lane, lane - 128) + lax.axis_index("cols") * cols
    side_ok = (col >= 0) & (col < cols * n_cols)
    src, dst = ua, ub

    def strip(i):
        return [src[i : i + 8, t * 128 : (t + 1) * 128] for t in range(tiles)]

    for step in range(HJB_STEPS):
        if step == HJB_STEPS // 2:
            between()
        start, stop = PAD - 8, PAD + rows + 8
        here = strip(start)
        fell = [pltpu.roll(x, 1, 0) for x in here]
        rose = [pltpu.roll(x, 7, 0) for x in here]
        fell_before = fell
        for i in range(start, stop, 8):
            if i + 8 < stop:
                after = strip(i + 8)
                rose_after = [pltpu.roll(x, 7, 0) for x in after]
                fell_after = [pltpu.roll(x, 1, 0) for x in after]
            else:
                after, rose_after, fell_after = here, rose, fell
            row_ok = None
            if i < PAD or i >= PAD + rows:
                row = sub + (row_first + (i - PAD))
                row_ok = (row >= 0) & (row < rows * n_rows)
            went = [pltpu.roll(x, 1, 1) for x in here]
            came = [pltpu.roll(x, 127, 1) for x in here]
            for t in range(tiles):
                value = here[t]
                up = jnp.where(top, fell_before[t], fell[t])
                down = jnp.where(bottom, rose_after[t], rose[t])
                left = jnp.where(first, went[t - 1], went[t])
                right = jnp.where(last, came[(t + 1) % tiles], came[t])
                slope_x = jnp.maximum(value - jnp.minimum(up, down), 0.0)
                slope_y = jnp.maximum(value - jnp.minimum(left, right), 0.0)
                around = (up + down) + (left + right) + m[i : i + 8, t * 128 : (t + 1) * 128]
                new = 0.5 * value + 0.125 * (around - (slope_x * slope_x + slope_y * slope_y))
                ok = row_ok
                if t == tiles - 1:
                    ok = side_ok if ok is None else ok & side_ok
                dst[i : i + 8, t * 128 : (t + 1) * 128] = (
                    new if ok is None else jnp.where(ok, new, 0.0)
                )
            here, fell_before, fell, rose = after, fell, fell_after, rose_after
        src, dst = dst, src
    return src


def split(value):
    high = value.astype(BF16)
    return high, (value - high.astype(F32)).astype(BF16)


def lane_pick(value, index):
    dims = lax.GatherDimensionNumbers(
        offset_dims=(),
        collapsed_slice_dims=(1,),
        start_index_map=(1,),
        operand_batching_dims=(0,),
        start_indices_batching_dims=(0,),
    )
    return lax.gather(
        value, index[..., None], dims, (1, 1), mode=lax.GatherScatterMode.PROMISE_IN_BOUNDS
    )


def table_height(rows):
    return rows + 16


def fill_tables(rows, cols, u, tabs, halo):
    high_rows = table_height(rows)
    lane = lax.broadcasted_iota(I32, (8, 128), 1)
    lower = lane < 64
    for i in range(0, high_rows, 16):
        for parity in range(2):
            index = (2 * lane + parity) & 127
            for t in range(cols // 256):
                halves = []
                for j in range(2):
                    at = PAD + i + 8 * j
                    one = u[at : at + 8, 2 * t * 128 : (2 * t + 1) * 128]
                    two = u[at : at + 8, (2 * t + 1) * 128 : (2 * t + 2) * 128]
                    halves.append(
                        jnp.where(lower, lane_pick(one, index), lane_pick(two, index))
                    )
                high, low = split(jnp.concatenate(halves, axis=0))
                tabs[parity][i : i + 16, t * 128 : (t + 1) * 128] = high
                tabs[parity][high_rows + i : high_rows + i + 16, t * 128 : (t + 1) * 128] = low
        halo[i : i + 16, :] = jnp.broadcast_to(
            u[PAD + i : PAD + i + 16, cols : cols + 1], (16, 128)
        )


def fill_slots(rows, blocks, cap, first, dest, slot_row, corner_row, counter):
    n_cols = lax.axis_size("cols")
    my_row, my_col = lax.axis_index("rows"), lax.axis_index("cols")
    n_rows = lax.axis_size("rows")
    kinds = 4 if first else 2
    part_rows = 3 * kinds * cap + EDGE
    spare_row = n_cols * part_rows
    for i in range(3 * n_cols):
        counter[i] = 0
    for b in range(blocks):
        tile = dest[b]
        band, column = tile // n_cols, tile % n_cols
        section = jnp.where(band == my_row, 0, jnp.where(band == (my_row ^ 1), 1, 2))
        distance = column ^ my_col
        rank = counter[distance * 3 + section]
        counter[distance * 3 + section] = rank + 1
        slot_row[b] = distance * part_rows + section * (kinds * cap) + rank
        if not first:
            goes = (band < n_rows - 1) & (column < n_cols - 1)
            row = ((column + 1) ^ my_col) * part_rows + 3 * kinds * cap + section
            corner_row[b] = jnp.where(goes, row, spare_row)


def sample_moves(
    rows, cols, blocks, cap, first, tabs, halo, starts, offs, wts, ends, buf, slot_row, corner_row
):
    buf[...] = jnp.zeros(buf.shape, F32)
    high_rows = table_height(rows)
    sub16 = lax.broadcasted_iota(I32, (16, 256), 0)
    sub8 = lax.broadcasted_iota(I32, (8, 256), 0)
    one16, zero16 = jnp.ones((16, 256), BF16), jnp.zeros((16, 256), BF16)

    def step(j, carry):
        def pair(ref):
            return jnp.concatenate([ref[pl.ds(2 * j, 1), :], ref[pl.ds(2 * j + 1, 1), :]], axis=1)

        row, col = row_col(pair(starts), cols)
        lanes = pl.ds(pl.multiple_of(j * 256, 256), 256)
        off_x = offs[0:1, lanes]
        off_y = offs[1:2, lanes]
        odd = (col & 1) == 1
        line = []
        for tab, place in ((tabs[0], (col + 1) >> 1), (tabs[1], col >> 1)):
            at = (jnp.broadcast_to(place, (16, 256)) - sub16).astype(jnp.int16)
            hot = [jnp.where(at == 16 * i, one16, zero16) for i in range(cols // 32)]
            line.append(
                jnp.dot(tab[...], jnp.concatenate(hot, axis=0), preferred_element_type=F32)
            )
        frac_x = 0.5 + 0.45 * jnp.tanh(off_x)
        frac_y = 0.5 + 0.45 * jnp.tanh(off_y)
        blend = jnp.where(odd, 1.0 - frac_y, frac_y)
        edge = jnp.broadcast_to(col == cols - 1, (8, 256))
        row_at = jnp.broadcast_to(row, (8, 256)) - sub8
        near, far = jnp.broadcast_to(1.0 - frac_x, (8, 256)), jnp.broadcast_to(frac_x, (8, 256))
        sum_x, sum_y = jnp.zeros((8, 256), F32), jnp.zeros((8, 256), F32)
        for i in range(0, rows + 8, 8):
            even, odds = [
                both[i : i + 8] + both[high_rows + i : high_rows + i + 8] for both in line
            ]
            beyond = jnp.concatenate([halo[i : i + 8, :]] * 2, axis=1)
            even = jnp.where(edge, beyond, even)
            step_y = odds - even
            mixed = even + blend * step_y
            here, below = row_at == i, row_at == i - 1
            sum_x = sum_x + jnp.where(below, mixed, jnp.where(here, -mixed, 0.0))
            sum_y = sum_y + step_y * jnp.where(here, near, jnp.where(below, far, 0.0))
        grad_x = jnp.sum(sum_x, axis=0, keepdims=True)
        grad_y = jnp.sum(sum_y, axis=0, keepdims=True)
        grad_y = jnp.where(odd, -grad_y, grad_y)
        moved_x = 0.5 + 0.45 * jnp.tanh(off_x - grad_x)
        moved_y = 0.5 + 0.45 * jnp.tanh(off_y - grad_y)
        out = [moved_x, moved_y]
        if first:
            out += [pair(wts), (pair(ends) + 1).astype(F32)]
        else:
            corner = jnp.where(pair(ends) == rows * cols - 1, pair(wts) * moved_x * moved_y, 0.0)
        for half in range(2):
            if not first:
                buf[pl.ds(corner_row[2 * j + half], 1), :] += corner[:, half * 128 : (half + 1) * 128]
            base = slot_row[2 * j + half]
            for q, value in enumerate(out):
                buf[pl.ds(base + q * cap, 1), :] = value[:, half * 128 : (half + 1) * 128]
        return carry

    lax.fori_loop(0, blocks // 2, step, 0, unroll=UNROLL)


def first_kernel(
    rows, cols, blocks, cap, n_cols, *refs
):
    (ue_in, me_in, ra_ref, rb_ref, w_ref, starts, offs, wts, ends, dest_hbm) = refs[:10]
    outs = refs[10 : 10 + n_cols]
    ue_ref, me_ref = refs[10 + n_cols : 12 + n_cols]
    ua, ub, tab_even, tab_odd, halo, buf, slot_row, corner_row, counter, dest, sem = refs[12 + n_cols :]
    fetch = pltpu.make_async_copy(dest_hbm, dest, sem)
    fetch.start()
    col_even = lax.axis_index("cols") % 2 == 0
    tall = ue_in.shape[0]
    width = ra_ref.shape[1]
    for index, (src, dst) in enumerate(((ue_in, ue_ref), (me_in, me_ref))):
        part = slice(index * EDGE, (index + 1) * EDGE)
        west = pick(col_even, rb_ref[part, :], ra_ref[part, :])
        east = pick(col_even, ra_ref[part, :], rb_ref[part, :])
        dst[:, 0:cols] = src[:, 0:cols]
        dst[:, cols : cols + 128] = unflipped(side_tile(west, east, width), tall)
    ua[...] = ue_ref[...]
    ub[...] = jnp.zeros(ub.shape, F32)

    def place_blocks():
        fetch.wait()
        fill_slots(rows, blocks, cap, True, dest, slot_row, corner_row, counter)

    u = hjb_sweep(rows, cols, ua, ub, me_ref, place_blocks)
    tabs = (tab_even, tab_odd)
    fill_tables(rows, cols, u, tabs, halo)
    sample_moves(
        rows, cols, blocks, cap, True, tabs, halo, starts, offs, wts, ends, buf, slot_row, corner_row
    )
    part_rows = 12 * cap + EDGE
    for k in range(n_cols):
        out = outs[(n_cols - k) % n_cols]
        out[0 : part_rows - EDGE, :] = buf[k * part_rows : (k + 1) * part_rows - EDGE, :]
        out[part_rows - EDGE :, :] = w_ref[...]


def again_kernel(rows, cols, blocks, cap, n_cols, *refs):
    (ue_ref, m_in, d_ref, ra_ref, rb_ref, total_in, more_in) = refs[:7]
    (starts, offs, wts, ends, dest_hbm) = refs[7:12]
    outs = refs[12 : 12 + n_cols]
    value_hbm, density_ref, total_ref = refs[12 + n_cols : 15 + n_cols]
    (ua, ub, m, tab_even, tab_odd, halo, buf, slot_row, corner_row, counter, dest, sem, value_sem) = (
        refs[15 + n_cols :]
    )
    total_ref[...] = total_in[...] + more_in[...]
    fetch = pltpu.make_async_copy(dest_hbm, dest, sem)
    fetch.start()
    col_even = lax.axis_index("cols") % 2 == 0
    n_rows = lax.axis_size("rows")
    tall = ue_ref.shape[0]
    width = ra_ref.shape[1]
    half_scale = 0.5 * ((rows * cols * n_rows * n_cols) / total_ref[0:1, 0:1])
    west = pick(col_even, rb_ref[...], ra_ref[...])
    east = pick(col_even, ra_ref[...], rb_ref[...])
    side = unflipped(side_tile(west[0:EDGE], east[0:EDGE], width), tall)
    pushed = unflipped(
        jnp.concatenate([west[EDGE : 2 * EDGE], jnp.zeros((128 - EDGE, width), F32)], axis=0), tall
    )
    m[:, 0:128] = 0.5 * m_in[:, 0:128] + half_scale * (d_ref[:, 0:128] + pushed)
    m[:, 128:cols] = 0.5 * m_in[:, 128:cols] + half_scale * d_ref[:, 128:cols]
    m[:, cols : cols + 128] = 0.5 * m_in[:, cols : cols + 128] + half_scale * (
        d_ref[:, cols : cols + 128] + side
    )
    density_ref[...] = m[PAD : PAD + rows, 0:cols]
    ua[...] = ue_ref[...]
    ub[...] = jnp.zeros(ub.shape, F32)

    def place_blocks():
        fetch.wait()
        fill_slots(rows, blocks, cap, False, dest, slot_row, corner_row, counter)

    u = hjb_sweep(rows, cols, ua, ub, m, place_blocks)
    leave = pltpu.make_async_copy(u.at[PAD : PAD + rows, 0:cols], value_hbm, value_sem)
    leave.start()
    tabs = (tab_even, tab_odd)
    fill_tables(rows, cols, u, tabs, halo)
    sample_moves(
        rows, cols, blocks, cap, False, tabs, halo, starts, offs, wts, ends, buf, slot_row, corner_row
    )
    part_rows = 6 * cap + EDGE
    for k in range(n_cols):
        outs[(n_cols - k) % n_cols][...] = buf[k * part_rows : (k + 1) * part_rows, :]
    leave.wait()


def deposit_blocks(rows, cols, cap, chunks, moves, masses, scratch, slots):
    acc, beside = scratch
    counts = []
    for q in range(chunks):
        cells = masses[(2 * q + 1) * cap : (2 * q + 2) * cap, :]
        counts.append(jnp.sum(jnp.where(cells > 0.5, 1.0, 0.0)).astype(I32) // 128)
    base = jnp.int32(0)
    for q in range(chunks):
        for rank in range(cap):
            slots[base + rank] = 2 * q * cap + rank
        base = base + counts[q]
    for rank in range(2 * GROUP):
        slots[base + rank] = 2 * chunks * cap
    high_rows = table_height(rows)
    sub16 = lax.broadcasted_iota(I32, (16, 128), 0)
    sub8 = lax.broadcasted_iota(I32, (8, 128), 0)
    one16, zero16 = jnp.ones((16, 128), BF16), jnp.zeros((16, 128), BF16)

    def relative(line, sub):
        return jnp.broadcast_to(line, sub.shape) - sub

    def build(first_slot):
        edges, left, right = [], ([], []), ([], [])
        for t in range(GROUP):
            at = slots[first_slot + t]
            move_x = moves[pl.ds(at, 1), :]
            move_y = moves[pl.ds(at + cap, 1), :]
            mass = masses[pl.ds(at, 1), :]
            row, col = row_col(masses[pl.ds(at + cap, 1), :].astype(I32) - 1, cols)
            odd = (col & 1) == 1
            stay, go = mass * (1.0 - move_x), mass * move_x
            row_at = relative(row, sub16).astype(jnp.int16)
            values = []
            for parity in range(2):
                share = jnp.where(odd == (parity == 1), 1.0 - move_y, move_y)
                first, second = stay * share, go * share
                if parity == 0:
                    edge_row = jnp.where(col == cols - 1, row, -2)
                    edges.append((relative(edge_row, sub8), first, second))
                for one, two in zip(split(first), split(second)):
                    values.append(
                        [jnp.broadcast_to(x.astype(F32), (16, 128)).astype(BF16) for x in (one, two)]
                    )
            tiles = [[], [], [], []]
            for i in range(high_rows // 16):
                here, below = row_at == 16 * i, row_at == 16 * i - 1
                for index, (one, two) in enumerate(values):
                    tiles[index].append(jnp.where(here, one, jnp.where(below, two, zero16)))
            for parity in range(2):
                left[parity].append(
                    jnp.concatenate(tiles[2 * parity] + tiles[2 * parity + 1], axis=0)
                )
            for parity, place in ((0, (col + 1) >> 1), (1, col >> 1)):
                place_at = relative(place, sub16).astype(jnp.int16)
                hot = [jnp.where(place_at == 16 * i, one16, zero16) for i in range(cols // 32)]
                right[parity].append(jnp.concatenate(hot, axis=0))
        for i in range(rows // 8 + 1):
            total = beside[8 * i : 8 * i + 8, :]
            for row_at, first, second in edges:
                total = total + jnp.where(
                    row_at == 8 * i, first, jnp.where(row_at == 8 * i - 1, second, 0.0)
                )
            beside[8 * i : 8 * i + 8, :] = total
        for parity in range(2):
            acc[parity] += lax.dot_general(
                jnp.concatenate(left[parity], axis=1),
                jnp.concatenate(right[parity], axis=1),
                (((1,), (1,)), ((), ())),
                preferred_element_type=F32,
            )

    def step(g, carry):
        for part in range(2):
            build((2 * g + part) * GROUP)
        return carry

    lax.fori_loop(0, (base + 2 * GROUP - 1) // (2 * GROUP), step, 0)


def finish_grid(rows, cols, acc, beside, grid):
    high_rows = table_height(rows)
    wide = cols + 128
    lane = lax.broadcasted_iota(I32, (8, wide), 1)
    lane1 = lax.broadcasted_iota(I32, (8, 128), 1)
    odd_lane = (lane1 & 1) == 1
    half = lane1 >> 1

    def weave(i, even, odd):
        for t in range(cols // 128):
            index = half + 64 * (t % 2)
            at = slice((t // 2) * 128, (t // 2 + 1) * 128)
            grid[i : i + 8, t * 128 : (t + 1) * 128] = jnp.where(
                odd_lane, lane_pick(odd[:, at], index), lane_pick(even[:, at], index)
            )
        right = jnp.sum(beside[i : i + 8, :], axis=1, keepdims=True)
        grid[i : i + 8, cols:wide] = jnp.where(lane1 == 0, right, 0.0)

    for i in range(0, rows + 8, 8):
        weave(
            i,
            *[acc[p, i : i + 8, :] + acc[p, high_rows + i : high_rows + i + 8, :] for p in range(2)],
        )

    @pl.when(lax.axis_index("rows") == lax.axis_size("rows") - 1)
    def _():
        tail = grid[rows - 8 : rows, :]
        sub8 = lax.broadcasted_iota(I32, (8, wide), 0)
        spill_row = jnp.broadcast_to(grid[rows : rows + 1, :], (8, wide))
        grid[rows - 8 : rows, :] = tail + jnp.where(sub8 == 7, spill_row, 0.0)
        grid[rows : rows + 8, :] = jnp.zeros((8, wide), F32)

    @pl.when(lax.axis_index("cols") == lax.axis_size("cols") - 1)
    def _():
        for i in range(0, rows + 8, 8):
            line = grid[i : i + 8, :]
            moved = jnp.where(lane == cols - 1, pltpu.roll(line, wide - 1, 1), 0.0)
            grid[i : i + 8, :] = jnp.where(lane < cols, line + moved, 0.0)


def own_deposit_kernel(rows, cols, cap, n_cols, first, *refs):
    pieces, refs = refs[:n_cols], refs[n_cols:]
    if first:
        acc_out, beside_out, masses, moves, *scratch, slots = refs
    else:
        masses, acc_out, beside_out, moves, *scratch, slots = refs
    size = 2 * cap
    for k in range(n_cols):
        moves[k * size : (k + 1) * size, :] = pieces[k][0:size, :]
        if first:
            masses[k * size : (k + 1) * size, :] = pieces[k][size : 2 * size, :]
    for ref in (moves, masses) if first else (moves,):
        ref[n_cols * size :, :] = jnp.zeros((size, 128), F32)
    acc_out[...] = jnp.zeros(acc_out.shape, F32)
    beside_out[...] = jnp.zeros(beside_out.shape, F32)
    deposit_blocks(
        rows, cols, cap, n_cols, moves, masses, (acc_out, beside_out, *scratch), slots
    )


def other_deposit(rows, cols, cap, n_cols, first, came, acc_in, beside_in, masses, grid, scratch):
    moves, acc, beside, *rest, slots = scratch
    size = 2 * cap
    step = 2 * size if first else size
    for index, ref in enumerate(came):
        for k in range(n_cols):
            at = (index * n_cols + k) * size
            moves[at : at + size, :] = ref[k * step : k * step + size, :]
            if first:
                masses[at : at + size, :] = ref[k * step + size : (k + 1) * step, :]
    for ref in (moves, masses) if first else (moves,):
        ref[2 * n_cols * size :, :] = jnp.zeros((size, 128), F32)
    acc[...] = acc_in[...]
    beside[...] = beside_in[...]
    deposit_blocks(
        rows, cols, cap, 2 * n_cols, moves, masses, (acc, beside, *rest), slots
    )
    finish_grid(rows, cols, acc, beside, grid)


def first_deposit_kernel(rows, cols, cap, n_cols, *refs):
    ra_ref, rb_ref, acc_in, beside_in = refs[:4]
    grid, sa_ref, sb_ref, masses = refs[4:8]
    other_deposit(
        rows, cols, cap, n_cols, True, (ra_ref, rb_ref), acc_in, beside_in, masses, grid, refs[8:]
    )
    row_even = lax.axis_index("rows") % 2 == 0
    south_going = grid[rows - 7 : rows + 1, :]
    north_going = grid[0:8, :]
    sa_ref[...] = pick(row_even, south_going, north_going)
    sb_ref[...] = pick(row_even, north_going, south_going)


def last_deposit_kernel(rows, cols, cap, n_cols, *refs):
    ra_ref, rb_ref, acc_in, beside_in, masses, corner_ref = refs[:6]
    grid, row_ref, col_ref = refs[6:9]
    other_deposit(
        rows, cols, cap, n_cols, False, (ra_ref, rb_ref), acc_in, beside_in, masses, grid, refs[9:]
    )
    tail = 2 * cap * n_cols
    corner = corner_ref[0:1, :] + ra_ref[tail + 1 : tail + 2, :] + rb_ref[tail + 2 : tail + 3, :]
    corner = jnp.sum(corner, axis=1, keepdims=True)
    place = lax.broadcasted_iota(I32, (8, 128), 0) + lax.broadcasted_iota(I32, (8, 128), 1)
    row_ref[...] = grid[rows : rows + 8, 0:cols]
    row_ref[:, 0:128] = row_ref[:, 0:128] + jnp.where(place == 0, corner, 0.0)
    col_ref[...] = flipped(grid[0:rows, cols : cols + 128])[0:8]


def edge_mid_kernel(rows, cols, g_ref, a_ref, b_ref, d_ref, ca_ref, cb_ref):
    row_even = lax.axis_index("rows") % 2 == 0
    col_even = lax.axis_index("cols") % 2 == 0
    wide = cols + 128
    north = pick(row_even, b_ref[...], a_ref[...])
    south = pick(row_even, a_ref[...], b_ref[...])
    d_ref[0:PAD, :] = jnp.zeros((PAD, wide), F32)
    d_ref[PAD : PAD + rows, :] = g_ref[0:rows, :]
    d_ref[PAD + rows : PAD + rows + 8, :] = south + g_ref[rows : rows + 8, :]
    d_ref[PAD + rows + 8 :, :] = jnp.zeros((d_ref.shape[0] - PAD - rows - 8, wide), F32)
    d_ref[PAD - 7 : PAD + 1, :] = d_ref[PAD - 7 : PAD + 1, :] + north
    west_going = flipped(d_ref[:, 0:128])[0:EDGE]
    east_going = flipped(d_ref[:, cols - 128 : cols])[128 - EDGE : 128]
    spilled = flipped(d_ref[:, cols : cols + 128])[0:EDGE]
    ca_ref[0:EDGE, :] = pick(col_even, east_going, west_going)
    cb_ref[0:EDGE, :] = pick(col_even, west_going, east_going)
    ca_ref[EDGE:, :] = pick(col_even, spilled, 0.0)
    cb_ref[EDGE:, :] = pick(col_even, 0.0, spilled)


def final_kernel(rows, cols, g_ref, m_ref, row_in, col_in, total_ref, out_ref):
    n_rows, n_cols = lax.axis_size("rows"), lax.axis_size("cols")
    half_scale = 0.5 * ((rows * cols * n_rows * n_cols) / total_ref[0:1, 0:1])
    out_ref[...] = 0.5 * m_ref[...] + half_scale * g_ref[0:rows, 0:cols]
    out_ref[0:8, :] = out_ref[0:8, :] + half_scale * row_in[...]
    beside = jnp.concatenate([col_in[...], jnp.zeros((120, col_in.shape[1]), F32)], axis=0)
    out_ref[:, 0:128] = out_ref[:, 0:128] + half_scale * unflipped(beside, rows)


def exchange_columns(outs):
    came = [xor_permute(part, "cols", len(outs) - i) for i, part in enumerate(outs) if i > 0]
    return [outs[0]] + came


def exchange_rows(pieces, kinds, cap, extra=None):
    step = kinds * cap
    first = [piece[step : 2 * step] for piece in pieces]
    second = [piece[2 * step : 3 * step] for piece in pieces]
    if extra is not None:
        first, second = first + [extra], second + [extra]
    return swap_both(jnp.concatenate(first), jnp.concatenate(second), "rows")


def body(terminal_value, density_start, start_cells, offsets, weights, dest_tiles, end_cells):
    rows, cols = terminal_value.shape
    n_rows, n_cols = lax.axis_size("rows"), lax.axis_size("cols")
    blocks = dest_tiles.shape[0]
    cap = blocks // 4
    chunks = 3 * n_cols
    wide, tall = cols + 128, rows + 2 * PAD
    flat = -(-tall // 128) * 128
    starts = start_cells.reshape(blocks, 128)
    wts = weights.reshape(blocks, 128)
    ends = end_cells.reshape(blocks, 128)
    arrays = (terminal_value, density_start, wts, starts, offsets, ends)
    *arrays, sa, sb = vmem_call(
        functools.partial(start_kernel, rows, len(arrays)),
        (
            *[shape(*x.shape, dtype=x.dtype) for x in arrays],
            shape(3 * EDGE, cols),
            shape(2 * EDGE, cols),
        ),
        len(arrays),
        [pltpu.SemaphoreType.DMA((len(arrays),))],
        hbm_in=range(len(arrays)),
    )(*arrays)
    terminal_value, density_start, wts, starts, offsets, ends = arrays
    ra, rb = swap_both(sa, sb, "rows")
    ue, me, ca, cb, total = vmem_call(
        functools.partial(start_mid_kernel, rows, cols),
        (
            shape(tall, wide),
            shape(tall, wide),
            shape(2 * EDGE, flat),
            shape(2 * EDGE, flat),
            shape(EDGE, 128),
        ),
        5,
    )(terminal_value, density_start, ra, rb, sa)
    ca, cb = swap_both(ca, cb, "cols")
    sweep_scratch = [
        pltpu.VMEM((tall, wide), F32),
        pltpu.VMEM((tall, wide), F32),
    ]

    def sample_scratch(part_rows):
        return [
            pltpu.VMEM((2 * table_height(rows), cols // 2), BF16),
            pltpu.VMEM((2 * table_height(rows), cols // 2), BF16),
            pltpu.VMEM((table_height(rows), 128), F32),
            pltpu.VMEM((n_cols * part_rows + EDGE, 128), F32),
            pltpu.SMEM((blocks,), I32),
            pltpu.SMEM((blocks,), I32),
            pltpu.SMEM((chunks,), I32),
            pltpu.SMEM((blocks,), I32),
            pltpu.SemaphoreType.DMA(()),
        ]

    high_rows = table_height(rows)
    acc_shape = (2, 2 * high_rows, cols // 2)
    beside_shape = (rows + 8, 128)

    def part_rows_of(chunk_count):
        return 2 * cap * (chunk_count + 1)

    own_scratch = [
        pltpu.VMEM((part_rows_of(n_cols), 128), F32),
        pltpu.SMEM((n_cols * cap + 2 * GROUP,), I32),
    ]
    other_scratch = [
        pltpu.VMEM((part_rows_of(2 * n_cols), 128), F32),
        pltpu.VMEM(acc_shape, F32),
        pltpu.VMEM(beside_shape, F32),
        pltpu.SMEM((2 * n_cols * cap + 2 * GROUP,), I32),
    ]
    carried = (shape(*acc_shape), shape(*beside_shape))
    part_rows = 12 * cap + EDGE
    *outs, ue, me = vmem_call(
        functools.partial(first_kernel, rows, cols, blocks, cap, n_cols),
        tuple([shape(part_rows, 128)] * n_cols + [shape(tall, wide)] * 2),
        10,
        sweep_scratch + sample_scratch(part_rows),
        hbm_in=(9,),
    )(ue, me, ca, cb, total, starts, offsets, wts, ends, dest_tiles)
    pieces = exchange_columns(outs)
    total = sum(piece[part_rows - EDGE :] for piece in pieces)
    ra, rb = exchange_rows(pieces, 4, cap)
    bits = [1 << i for i in range(1, n_rows.bit_length() - 1)]
    more = xor_permute(total, "rows", bits[0])
    acc, beside, own_masses = vmem_call(
        functools.partial(own_deposit_kernel, rows, cols, cap, n_cols, True),
        (*carried, shape(part_rows_of(n_cols), 128)),
        n_cols,
        own_scratch,
    )(*pieces)
    grid, ea, eb, masses = vmem_call(
        functools.partial(first_deposit_kernel, rows, cols, cap, n_cols),
        (
            shape(rows + 8, wide),
            shape(8, wide),
            shape(8, wide),
            shape(part_rows_of(2 * n_cols), 128),
        ),
        4,
        other_scratch,
    )(ra, rb, acc, beside)
    ea, eb, more = lax.optimization_barrier((ea, eb, more))
    ea, eb = swap_both(ea, eb, "rows")
    for bit in bits[1:]:
        total = total + more
        more = xor_permute(total, "rows", bit)
    deposit, ca, cb = vmem_call(
        functools.partial(edge_mid_kernel, rows, cols),
        (shape(tall, wide), shape(2 * EDGE, flat), shape(2 * EDGE, flat)),
        3,
    )(grid, ea, eb)
    ca, cb = swap_both(ca, cb, "cols")
    part_rows = 6 * cap + EDGE
    *outs, value, density, total = vmem_call(
        functools.partial(again_kernel, rows, cols, blocks, cap, n_cols),
        tuple([shape(part_rows, 128)] * n_cols + [shape(rows, cols)] * 2 + [shape(EDGE, 128)]),
        12,
        sweep_scratch
        + [pltpu.VMEM((tall, wide), F32)]
        + sample_scratch(part_rows)
        + [pltpu.SemaphoreType.DMA(())],
        hbm_in=(11,),
        hbm_out=(n_cols,),
    )(ue, me, deposit, ca, cb, total, more, starts, offsets, wts, ends, dest_tiles)
    pieces = exchange_columns(outs)
    corner = sum(piece[part_rows - EDGE :] for piece in pieces)
    ra, rb = exchange_rows(pieces, 2, cap, corner)
    acc, beside = vmem_call(
        functools.partial(own_deposit_kernel, rows, cols, cap, n_cols, False),
        carried,
        n_cols + 1,
        own_scratch,
    )(*pieces, own_masses)
    grid, below, beside = vmem_call(
        functools.partial(last_deposit_kernel, rows, cols, cap, n_cols),
        (shape(rows + 8, wide), shape(8, cols), shape(8, rows)),
        6,
        other_scratch,
    )(ra, rb, acc, beside, masses, corner)
    below = lax.ppermute(below, "rows", [(i, i + 1) for i in range(n_rows - 1)])
    beside = lax.ppermute(beside, "cols", [(i, i + 1) for i in range(n_cols - 1)])
    (density,) = vmem_call(
        functools.partial(final_kernel, rows, cols), (shape(rows, cols),), 5, keep=(0,)
    )(grid, density, below, beside, total)
    return (value, density)


def solution(mesh):
    in_specs = (
        P("rows", "cols"),
        P("rows", "cols"),
        P(("rows", "cols")),
        P(None, ("rows", "cols")),
        P(("rows", "cols")),
        P(("rows", "cols")),
        P(("rows", "cols")),
    )
    out_specs = (P("rows", "cols"), P("rows", "cols"))
    return jax.shard_map(body, mesh=mesh, in_specs=in_specs, out_specs=out_specs, check_vma=False)
```

```python
import functools
import jax
import jax.numpy as jnp
from jax import lax
from jax.experimental import pallas as pl
from jax.experimental.pallas import tpu as pltpu
from jax.sharding import PartitionSpec as P

HJB_STEPS = 4
F32, BF16, I32 = jnp.float32, jnp.bfloat16, jnp.int32

PAD = 16
EDGE = 8
GROUP = 4
UNROLL = 4
VMEM_LIMIT = 24 * 1024 * 1024


def swap_pairs(count):
    first = [(i, i ^ 1) for i in range(count)]
    second = [(i, ((i + 1) ^ 1) - 1) for i in range(1, count - 1)]
    return first, second


def swap_both(first, second, axis):
    pairs_a, pairs_b = swap_pairs(lax.axis_size(axis))
    return lax.ppermute(first, axis, pairs_a), lax.ppermute(second, axis, pairs_b)


def xor_permute(value, axis, bit):
    return lax.ppermute(value, axis, [(i, i ^ bit) for i in range(lax.axis_size(axis))])


def vmem_call(kernel, out_shape, n_in, scratch=(), hbm_in=(), hbm_out=(), keep=()):
    def spec(in_hbm):
        return pl.BlockSpec(memory_space=pltpu.HBM if in_hbm else pltpu.VMEM)

    results = [
        leaf if i in keep or i in hbm_out else pltpu.VMEM(leaf.shape, leaf.dtype)
        for i, leaf in enumerate(out_shape)
    ]
    call = pl.pallas_call(
        kernel,
        out_shape=results,
        in_specs=[spec(i in hbm_in) for i in range(n_in)],
        out_specs=[spec(i in hbm_out) for i in range(len(results))],
        scratch_shapes=list(scratch),
        compiler_params=pltpu.CompilerParams(vmem_limit_bytes=VMEM_LIMIT),
    )

    def run(*operands):
        return call(
            *[
                pltpu.with_memory_space_constraint(x, pltpu.HBM if i in hbm_in else pltpu.VMEM)
                for i, x in enumerate(operands)
            ]
        )

    return run


def shape(*dims, dtype=F32):
    return jax.ShapeDtypeStruct(dims, dtype)


def flipped(block):
    rows = block.shape[0]
    width = -(-rows // 128) * 128
    if width > rows:
        block = jnp.concatenate([block, jnp.zeros((width - rows, 128), F32)], axis=0)
    parts = [block[i : i + 128].T for i in range(0, width, 128)]
    return jnp.concatenate(parts, axis=1)


def unflipped(block, rows):
    parts = [block[:, i : i + 128].T for i in range(0, block.shape[1], 128)]
    return jnp.concatenate(parts, axis=0)[:rows]


def row_col(cell, cols):
    if cols & (cols - 1) == 0:
        return cell >> (cols.bit_length() - 1), cell & (cols - 1)
    return cell // cols, cell % cols


def pick(flag, one, other):
    return jnp.where(flag, one, other)


def start_kernel(rows, count, *refs):
    sources, copies = refs[:count], refs[count : 2 * count]
    sa_ref, sb_ref, sems = refs[2 * count :]
    moves = [
        pltpu.make_async_copy(src, dst, sems.at[i])
        for i, (src, dst) in enumerate(zip(sources, copies))
    ]
    for move in moves:
        move.start()
    for move in moves:
        move.wait()
    u_ref, m_ref, wts = copies[:3]
    row_even = lax.axis_index("rows") % 2 == 0
    for index, ref in enumerate((u_ref, m_ref)):
        part = slice(index * EDGE, (index + 1) * EDGE)
        south_going, north_going = ref[rows - EDGE : rows, :], ref[0:EDGE, :]
        sa_ref[part, :] = pick(row_even, south_going, north_going)
        sb_ref[part, :] = pick(row_even, north_going, south_going)
    total = jnp.sum(jnp.sum(wts[...], axis=0, keepdims=True), axis=1, keepdims=True)
    sa_ref[2 * EDGE :, :] = jnp.broadcast_to(total, (EDGE, sa_ref.shape[1]))


def start_mid_kernel(
    rows, cols, u_ref, m_ref, a_ref, b_ref, s_ref, ue_ref, me_ref, ca_ref, cb_ref, sum_ref
):
    sum_ref[...] = s_ref[2 * EDGE :, 0:128] + a_ref[2 * EDGE :, 0:128]
    row_even = lax.axis_index("rows") % 2 == 0
    col_even = lax.axis_index("cols") % 2 == 0
    for index, (src, dst) in enumerate(((u_ref, ue_ref), (m_ref, me_ref))):
        dst[...] = jnp.zeros(dst.shape, F32)
        dst[PAD : PAD + rows, 0:cols] = src[...]
        part = slice(index * EDGE, (index + 1) * EDGE)
        north = pick(row_even, b_ref[part, :], a_ref[part, :])
        south = pick(row_even, a_ref[part, :], b_ref[part, :])
        dst[PAD - EDGE : PAD, 0:cols] = north
        dst[PAD + rows : PAD + rows + EDGE, 0:cols] = south
        west_going = flipped(dst[:, 0:128])[0:EDGE]
        east_going = flipped(dst[:, cols - 128 : cols])[128 - EDGE : 128]
        ca_ref[part, :] = pick(col_even, east_going, west_going)
        cb_ref[part, :] = pick(col_even, west_going, east_going)


def side_tile(left, right, width):
    return jnp.concatenate([right, jnp.zeros((128 - 2 * EDGE, width), F32), left], axis=0)


def hjb_sweep(rows, cols, ua, ub, m, between):
    wide = cols + 128
    tiles = wide // 128
    n_rows, n_cols = lax.axis_size("rows"), lax.axis_size("cols")
    sub = lax.broadcasted_iota(I32, (8, 128), 0)
    lane = lax.broadcasted_iota(I32, (8, 128), 1)
    first, last = lane == 0, lane == 127
    row_first = lax.axis_index("rows") * rows
    col = jnp.where(lane < 64, cols + lane, lane - 128) + lax.axis_index("cols") * cols
    side_ok = (col >= 0) & (col < cols * n_cols)
    src, dst = ua, ub

    for step in range(HJB_STEPS):
        if step == HJB_STEPS // 2:
            between()
        for i in range(PAD - 8, PAD + rows + 8, 8):
            row_ok = None
            if i < PAD or i >= PAD + rows:
                row = sub + (row_first + (i - PAD))
                row_ok = (row >= 0) & (row < rows * n_rows)
            here = [src[t, i : i + 8, :] for t in range(tiles)]
            went = [pltpu.roll(x, 1, 1) for x in here]
            came = [pltpu.roll(x, 127, 1) for x in here]
            for t in range(tiles):
                value = here[t]
                up, down = src[t, i - 1 : i + 7, :], src[t, i + 1 : i + 9, :]
                left = jnp.where(first, went[t - 1], went[t])
                right = jnp.where(last, came[(t + 1) % tiles], came[t])
                slope_x = jnp.maximum(value - jnp.minimum(up, down), 0.0)
                slope_y = jnp.maximum(value - jnp.minimum(left, right), 0.0)
                around = (up + down) + (left + right) + m[i : i + 8, t * 128 : (t + 1) * 128]
                new = 0.5 * value + 0.125 * (around - (slope_x * slope_x + slope_y * slope_y))
                ok = row_ok
                if t == tiles - 1:
                    ok = side_ok if ok is None else ok & side_ok
                dst[t, i : i + 8, :] = new if ok is None else jnp.where(ok, new, 0.0)
        src, dst = dst, src
    return src


def split(value):
    high = value.astype(BF16)
    return high, (value - high.astype(F32)).astype(BF16)


def lane_pick(value, index):
    dims = lax.GatherDimensionNumbers(
        offset_dims=(),
        collapsed_slice_dims=(1,),
        start_index_map=(1,),
        operand_batching_dims=(0,),
        start_indices_batching_dims=(0,),
    )
    return lax.gather(
        value, index[..., None], dims, (1, 1), mode=lax.GatherScatterMode.PROMISE_IN_BOUNDS
    )


def table_height(rows):
    return rows + 16


def fill_tables(rows, cols, u, tabs, halo):
    high_rows = table_height(rows)
    lane = lax.broadcasted_iota(I32, (8, 128), 1)
    lower = lane < 64
    for i in range(0, high_rows, 16):
        for parity in range(2):
            index = (2 * lane + parity) & 127
            for t in range(cols // 256):
                halves = []
                for j in range(2):
                    at = PAD + i + 8 * j
                    one, two = u[2 * t, at : at + 8, :], u[2 * t + 1, at : at + 8, :]
                    halves.append(
                        jnp.where(lower, lane_pick(one, index), lane_pick(two, index))
                    )
                high, low = split(jnp.concatenate(halves, axis=0))
                tabs[parity][i : i + 16, t * 128 : (t + 1) * 128] = high
                tabs[parity][high_rows + i : high_rows + i + 16, t * 128 : (t + 1) * 128] = low
        halo[i : i + 16, :] = jnp.broadcast_to(
            u[cols // 128, PAD + i : PAD + i + 16, 0:1], (16, 128)
        )


def fill_slots(blocks, cap, first, dest, slot_row, corner_row, counter):
    n_cols = lax.axis_size("cols")
    my_row, my_col = lax.axis_index("rows"), lax.axis_index("cols")
    n_rows = lax.axis_size("rows")
    kinds = 4 if first else 2
    part_rows = 3 * kinds * cap + EDGE
    spare_row = n_cols * part_rows
    for i in range(3 * n_cols):
        counter[i] = 0
    for b in range(blocks):
        tile = dest[b]
        band, column = tile // n_cols, tile % n_cols
        section = jnp.where(band == my_row, 0, jnp.where(band == (my_row ^ 1), 1, 2))
        distance = column ^ my_col
        rank = counter[distance * 3 + section]
        counter[distance * 3 + section] = rank + 1
        slot_row[b] = distance * part_rows + section * (kinds * cap) + rank
        if not first:
            goes = (band < n_rows - 1) & (column < n_cols - 1)
            row = ((column + 1) ^ my_col) * part_rows + 3 * kinds * cap + section
            corner_row[b] = jnp.where(goes, row, spare_row)


def sample_moves(
    rows, cols, blocks, cap, first, tabs, halo, starts, offs, wts, ends, buf, slot_row, corner_row
):
    buf[...] = jnp.zeros(buf.shape, F32)
    high_rows = table_height(rows)
    sub16 = lax.broadcasted_iota(I32, (16, 256), 0)
    sub8 = lax.broadcasted_iota(I32, (8, 256), 0)
    one16, zero16 = jnp.ones((16, 256), BF16), jnp.zeros((16, 256), BF16)

    def step(j, carry):
        def pair(ref):
            return jnp.concatenate([ref[pl.ds(2 * j, 1), :], ref[pl.ds(2 * j + 1, 1), :]], axis=1)

        row, col = row_col(pair(starts), cols)
        lanes = pl.ds(pl.multiple_of(j * 256, 256), 256)
        off_x = offs[0:1, lanes]
        off_y = offs[1:2, lanes]
        odd = (col & 1) == 1
        line = []
        for tab, place in ((tabs[0], (col + 1) >> 1), (tabs[1], col >> 1)):
            at = (jnp.broadcast_to(place, (16, 256)) - sub16).astype(jnp.int16)
            hot = [jnp.where(at == 16 * i, one16, zero16) for i in range(cols // 32)]
            line.append(
                jnp.dot(tab[...], jnp.concatenate(hot, axis=0), preferred_element_type=F32)
            )
        frac_x = 0.5 + 0.45 * jnp.tanh(off_x)
        frac_y = 0.5 + 0.45 * jnp.tanh(off_y)
        blend = jnp.where(odd, 1.0 - frac_y, frac_y)
        edge = jnp.broadcast_to(col == cols - 1, (8, 256))
        row_at = jnp.broadcast_to(row, (8, 256)) - sub8
        near, far = jnp.broadcast_to(1.0 - frac_x, (8, 256)), jnp.broadcast_to(frac_x, (8, 256))
        sum_x, sum_y = jnp.zeros((8, 256), F32), jnp.zeros((8, 256), F32)
        for i in range(0, rows + 8, 8):
            even, odds = [
                both[i : i + 8] + both[high_rows + i : high_rows + i + 8] for both in line
            ]
            beyond = jnp.concatenate([halo[i : i + 8, :]] * 2, axis=1)
            even = jnp.where(edge, beyond, even)
            step_y = odds - even
            mixed = even + blend * step_y
            here, below = row_at == i, row_at == i - 1
            sum_x = sum_x + jnp.where(below, mixed, jnp.where(here, -mixed, 0.0))
            sum_y = sum_y + step_y * jnp.where(here, near, jnp.where(below, far, 0.0))
        grad_x = jnp.sum(sum_x, axis=0, keepdims=True)
        grad_y = jnp.sum(sum_y, axis=0, keepdims=True)
        grad_y = jnp.where(odd, -grad_y, grad_y)
        moved_x = 0.5 + 0.45 * jnp.tanh(off_x - grad_x)
        moved_y = 0.5 + 0.45 * jnp.tanh(off_y - grad_y)
        out = [moved_x, moved_y]
        if first:
            out += [pair(wts), (pair(ends) + 1).astype(F32)]
        else:
            corner = jnp.where(pair(ends) == rows * cols - 1, pair(wts) * moved_x * moved_y, 0.0)
        for half in range(2):
            if not first:
                buf[pl.ds(corner_row[2 * j + half], 1), :] += corner[:, half * 128 : (half + 1) * 128]
            base = slot_row[2 * j + half]
            for q, value in enumerate(out):
                buf[pl.ds(base + q * cap, 1), :] = value[:, half * 128 : (half + 1) * 128]
        return carry

    lax.fori_loop(0, blocks // 2, step, 0, unroll=UNROLL)


def first_kernel(
    rows, cols, blocks, cap, n_cols, *refs
):
    (ue_in, me_in, ra_ref, rb_ref, w_ref, starts, offs, wts, ends, dest_hbm) = refs[:10]
    outs = refs[10 : 10 + n_cols]
    ue_ref, me_ref = refs[10 + n_cols : 12 + n_cols]
    ua, ub, tab_even, tab_odd, halo, buf, slot_row, corner_row, counter, dest, sem = refs[12 + n_cols :]
    fetch = pltpu.make_async_copy(dest_hbm, dest, sem)
    fetch.start()
    col_even = lax.axis_index("cols") % 2 == 0
    tall = ue_in.shape[0]
    width = ra_ref.shape[1]
    for index, (src, dst) in enumerate(((ue_in, ue_ref), (me_in, me_ref))):
        part = slice(index * EDGE, (index + 1) * EDGE)
        west = pick(col_even, rb_ref[part, :], ra_ref[part, :])
        east = pick(col_even, ra_ref[part, :], rb_ref[part, :])
        dst[:, 0:cols] = src[:, 0:cols]
        dst[:, cols : cols + 128] = unflipped(side_tile(west, east, width), tall)
    for t in range(cols // 128 + 1):
        ua[t] = ue_ref[:, t * 128 : (t + 1) * 128]
    ub[...] = jnp.zeros(ub.shape, F32)

    def place_blocks():
        fetch.wait()
        fill_slots(blocks, cap, True, dest, slot_row, corner_row, counter)

    u = hjb_sweep(rows, cols, ua, ub, me_ref, place_blocks)
    tabs = (tab_even, tab_odd)
    fill_tables(rows, cols, u, tabs, halo)
    sample_moves(
        rows, cols, blocks, cap, True, tabs, halo, starts, offs, wts, ends, buf, slot_row, corner_row
    )
    part_rows = 12 * cap + EDGE
    for k in range(n_cols):
        out = outs[(n_cols - k) % n_cols]
        out[0 : part_rows - EDGE, :] = buf[k * part_rows : (k + 1) * part_rows - EDGE, :]
        out[part_rows - EDGE :, :] = w_ref[...]


def again_kernel(rows, cols, blocks, cap, n_cols, *refs):
    (ue_ref, m_in, d_ref, ra_ref, rb_ref, total_in, more_in) = refs[:7]
    (starts, offs, wts, ends, dest_hbm) = refs[7:12]
    outs = refs[12 : 12 + n_cols]
    value_hbm, density_ref, total_ref = refs[12 + n_cols : 15 + n_cols]
    (ua, ub, m, tab_even, tab_odd, halo, buf, slot_row, corner_row, counter, dest, sem, value_sems) = (
        refs[15 + n_cols :]
    )
    total_ref[...] = total_in[...] + more_in[...]
    fetch = pltpu.make_async_copy(dest_hbm, dest, sem)
    fetch.start()
    col_even = lax.axis_index("cols") % 2 == 0
    n_rows = lax.axis_size("rows")
    tall = ue_ref.shape[0]
    width = ra_ref.shape[1]
    half_scale = 0.5 * ((rows * cols * n_rows * n_cols) / total_ref[0:1, 0:1])
    west = pick(col_even, rb_ref[...], ra_ref[...])
    east = pick(col_even, ra_ref[...], rb_ref[...])
    side = unflipped(side_tile(west[0:EDGE], east[0:EDGE], width), tall)
    pushed = unflipped(
        jnp.concatenate([west[EDGE : 2 * EDGE], jnp.zeros((128 - EDGE, width), F32)], axis=0), tall
    )
    m[:, 0:128] = 0.5 * m_in[:, 0:128] + half_scale * (d_ref[:, 0:128] + pushed)
    m[:, 128:cols] = 0.5 * m_in[:, 128:cols] + half_scale * d_ref[:, 128:cols]
    m[:, cols : cols + 128] = 0.5 * m_in[:, cols : cols + 128] + half_scale * (
        d_ref[:, cols : cols + 128] + side
    )
    density_ref[...] = m[PAD : PAD + rows, 0:cols]
    for t in range(cols // 128 + 1):
        ua[t] = ue_ref[:, t * 128 : (t + 1) * 128]
    ub[...] = jnp.zeros(ub.shape, F32)

    def place_blocks():
        fetch.wait()
        fill_slots(blocks, cap, False, dest, slot_row, corner_row, counter)

    u = hjb_sweep(rows, cols, ua, ub, m, place_blocks)
    leaving = [
        pltpu.make_async_copy(
            u.at[t, PAD : PAD + rows, :],
            value_hbm.at[:, t * 128 : (t + 1) * 128],
            value_sems.at[t],
        )
        for t in range(cols // 128)
    ]
    for leave in leaving:
        leave.start()
    tabs = (tab_even, tab_odd)
    fill_tables(rows, cols, u, tabs, halo)
    sample_moves(
        rows, cols, blocks, cap, False, tabs, halo, starts, offs, wts, ends, buf, slot_row, corner_row
    )
    part_rows = 6 * cap + EDGE
    for k in range(n_cols):
        outs[(n_cols - k) % n_cols][...] = buf[k * part_rows : (k + 1) * part_rows, :]
    for leave in leaving:
        leave.wait()


def deposit_blocks(rows, cols, cap, chunks, moves, masses, scratch, slots):
    acc, beside = scratch
    counts = []
    for q in range(chunks):
        cells = masses[(2 * q + 1) * cap : (2 * q + 2) * cap, :]
        counts.append(jnp.sum(jnp.where(cells > 0.5, 1.0, 0.0)).astype(I32) // 128)
    base = jnp.int32(0)
    for q in range(chunks):
        for rank in range(cap):
            slots[base + rank] = 2 * q * cap + rank
        base = base + counts[q]
    for rank in range(2 * GROUP):
        slots[base + rank] = 2 * chunks * cap
    high_rows = table_height(rows)
    sub16 = lax.broadcasted_iota(I32, (16, 128), 0)
    sub8 = lax.broadcasted_iota(I32, (8, 128), 0)
    one16, zero16 = jnp.ones((16, 128), BF16), jnp.zeros((16, 128), BF16)

    def relative(line, sub):
        return jnp.broadcast_to(line, sub.shape) - sub

    def build(first_slot):
        edges, left, right = [], ([], []), ([], [])
        for t in range(GROUP):
            at = slots[first_slot + t]
            move_x = moves[pl.ds(at, 1), :]
            move_y = moves[pl.ds(at + cap, 1), :]
            mass = masses[pl.ds(at, 1), :]
            row, col = row_col(masses[pl.ds(at + cap, 1), :].astype(I32) - 1, cols)
            odd = (col & 1) == 1
            stay, go = mass * (1.0 - move_x), mass * move_x
            row_at = relative(row, sub16).astype(jnp.int16)
            values = []
            for parity in range(2):
                share = jnp.where(odd == (parity == 1), 1.0 - move_y, move_y)
                first, second = stay * share, go * share
                if parity == 0:
                    edge_row = jnp.where(col == cols - 1, row, -2)
                    edges.append((relative(edge_row, sub8), first, second))
                for one, two in zip(split(first), split(second)):
                    values.append(
                        [jnp.broadcast_to(x.astype(F32), (16, 128)).astype(BF16) for x in (one, two)]
                    )
            tiles = [[], [], [], []]
            for i in range(high_rows // 16):
                here, below = row_at == 16 * i, row_at == 16 * i - 1
                for index, (one, two) in enumerate(values):
                    tiles[index].append(jnp.where(here, one, jnp.where(below, two, zero16)))
            for parity in range(2):
                left[parity].append(
                    jnp.concatenate(tiles[2 * parity] + tiles[2 * parity + 1], axis=0)
                )
            for parity, place in ((0, (col + 1) >> 1), (1, col >> 1)):
                place_at = relative(place, sub16).astype(jnp.int16)
                hot = [jnp.where(place_at == 16 * i, one16, zero16) for i in range(cols // 32)]
                right[parity].append(jnp.concatenate(hot, axis=0))
        for i in range(rows // 8 + 1):
            total = beside[8 * i : 8 * i + 8, :]
            for row_at, first, second in edges:
                total = total + jnp.where(
                    row_at == 8 * i, first, jnp.where(row_at == 8 * i - 1, second, 0.0)
                )
            beside[8 * i : 8 * i + 8, :] = total
        for parity in range(2):
            acc[parity] += lax.dot_general(
                jnp.concatenate(left[parity], axis=1),
                jnp.concatenate(right[parity], axis=1),
                (((1,), (1,)), ((), ())),
                preferred_element_type=F32,
            )

    def step(g, carry):
        for part in range(2):
            build((2 * g + part) * GROUP)
        return carry

    lax.fori_loop(0, (base + 2 * GROUP - 1) // (2 * GROUP), step, 0)


def finish_grid(rows, cols, acc, beside, grid):
    high_rows = table_height(rows)
    wide = cols + 128
    lane = lax.broadcasted_iota(I32, (8, wide), 1)
    lane1 = lax.broadcasted_iota(I32, (8, 128), 1)
    odd_lane = (lane1 & 1) == 1
    half = lane1 >> 1

    def weave(i, even, odd):
        for t in range(cols // 128):
            index = half + 64 * (t % 2)
            at = slice((t // 2) * 128, (t // 2 + 1) * 128)
            grid[i : i + 8, t * 128 : (t + 1) * 128] = jnp.where(
                odd_lane, lane_pick(odd[:, at], index), lane_pick(even[:, at], index)
            )
        right = jnp.sum(beside[i : i + 8, :], axis=1, keepdims=True)
        grid[i : i + 8, cols:wide] = jnp.where(lane1 == 0, right, 0.0)

    for i in range(0, rows + 8, 8):
        weave(
            i,
            *[acc[p, i : i + 8, :] + acc[p, high_rows + i : high_rows + i + 8, :] for p in range(2)],
        )

    @pl.when(lax.axis_index("rows") == lax.axis_size("rows") - 1)
    def _():
        tail = grid[rows - 8 : rows, :]
        sub8 = lax.broadcasted_iota(I32, (8, wide), 0)
        spill_row = jnp.broadcast_to(grid[rows : rows + 1, :], (8, wide))
        grid[rows - 8 : rows, :] = tail + jnp.where(sub8 == 7, spill_row, 0.0)
        grid[rows : rows + 8, :] = jnp.zeros((8, wide), F32)

    @pl.when(lax.axis_index("cols") == lax.axis_size("cols") - 1)
    def _():
        for i in range(0, rows + 8, 8):
            line = grid[i : i + 8, :]
            moved = jnp.where(lane == cols - 1, pltpu.roll(line, wide - 1, 1), 0.0)
            grid[i : i + 8, :] = jnp.where(lane < cols, line + moved, 0.0)


def own_deposit_kernel(rows, cols, cap, n_cols, first, *refs):
    pieces, refs = refs[:n_cols], refs[n_cols:]
    if first:
        acc_out, beside_out, masses, moves, *scratch, slots = refs
    else:
        masses, acc_out, beside_out, moves, *scratch, slots = refs
    size = 2 * cap
    for k in range(n_cols):
        moves[k * size : (k + 1) * size, :] = pieces[k][0:size, :]
        if first:
            masses[k * size : (k + 1) * size, :] = pieces[k][size : 2 * size, :]
    for ref in (moves, masses) if first else (moves,):
        ref[n_cols * size :, :] = jnp.zeros((size, 128), F32)
    acc_out[...] = jnp.zeros(acc_out.shape, F32)
    beside_out[...] = jnp.zeros(beside_out.shape, F32)
    deposit_blocks(
        rows, cols, cap, n_cols, moves, masses, (acc_out, beside_out, *scratch), slots
    )


def other_deposit(rows, cols, cap, n_cols, first, came, acc_in, beside_in, masses, grid, scratch):
    moves, acc, beside, *rest, slots = scratch
    size = 2 * cap
    step = 2 * size if first else size
    for index, ref in enumerate(came):
        for k in range(n_cols):
            at = (index * n_cols + k) * size
            moves[at : at + size, :] = ref[k * step : k * step + size, :]
            if first:
                masses[at : at + size, :] = ref[k * step + size : (k + 1) * step, :]
    for ref in (moves, masses) if first else (moves,):
        ref[2 * n_cols * size :, :] = jnp.zeros((size, 128), F32)
    acc[...] = acc_in[...]
    beside[...] = beside_in[...]
    deposit_blocks(
        rows, cols, cap, 2 * n_cols, moves, masses, (acc, beside, *rest), slots
    )
    finish_grid(rows, cols, acc, beside, grid)


def first_deposit_kernel(rows, cols, cap, n_cols, *refs):
    ra_ref, rb_ref, acc_in, beside_in = refs[:4]
    grid, sa_ref, sb_ref, masses = refs[4:8]
    other_deposit(
        rows, cols, cap, n_cols, True, (ra_ref, rb_ref), acc_in, beside_in, masses, grid, refs[8:]
    )
    row_even = lax.axis_index("rows") % 2 == 0
    south_going = grid[rows - 7 : rows + 1, :]
    north_going = grid[0:8, :]
    sa_ref[...] = pick(row_even, south_going, north_going)
    sb_ref[...] = pick(row_even, north_going, south_going)


def last_deposit_kernel(rows, cols, cap, n_cols, *refs):
    ra_ref, rb_ref, acc_in, beside_in, masses, corner_ref = refs[:6]
    grid, row_ref, col_ref = refs[6:9]
    other_deposit(
        rows, cols, cap, n_cols, False, (ra_ref, rb_ref), acc_in, beside_in, masses, grid, refs[9:]
    )
    tail = 2 * cap * n_cols
    corner = corner_ref[0:1, :] + ra_ref[tail + 1 : tail + 2, :] + rb_ref[tail + 2 : tail + 3, :]
    corner = jnp.sum(corner, axis=1, keepdims=True)
    place = lax.broadcasted_iota(I32, (8, 128), 0) + lax.broadcasted_iota(I32, (8, 128), 1)
    row_ref[...] = grid[rows : rows + 8, 0:cols]
    row_ref[:, 0:128] = row_ref[:, 0:128] + jnp.where(place == 0, corner, 0.0)
    col_ref[...] = flipped(grid[0:rows, cols : cols + 128])[0:8]


def edge_mid_kernel(rows, cols, g_ref, a_ref, b_ref, d_ref, ca_ref, cb_ref):
    row_even = lax.axis_index("rows") % 2 == 0
    col_even = lax.axis_index("cols") % 2 == 0
    wide = cols + 128
    north = pick(row_even, b_ref[...], a_ref[...])
    south = pick(row_even, a_ref[...], b_ref[...])
    d_ref[0:PAD, :] = jnp.zeros((PAD, wide), F32)
    d_ref[PAD : PAD + rows, :] = g_ref[0:rows, :]
    d_ref[PAD + rows : PAD + rows + 8, :] = south + g_ref[rows : rows + 8, :]
    d_ref[PAD + rows + 8 :, :] = jnp.zeros((d_ref.shape[0] - PAD - rows - 8, wide), F32)
    d_ref[PAD - 7 : PAD + 1, :] = d_ref[PAD - 7 : PAD + 1, :] + north
    west_going = flipped(d_ref[:, 0:128])[0:EDGE]
    east_going = flipped(d_ref[:, cols - 128 : cols])[128 - EDGE : 128]
    spilled = flipped(d_ref[:, cols : cols + 128])[0:EDGE]
    ca_ref[0:EDGE, :] = pick(col_even, east_going, west_going)
    cb_ref[0:EDGE, :] = pick(col_even, west_going, east_going)
    ca_ref[EDGE:, :] = pick(col_even, spilled, 0.0)
    cb_ref[EDGE:, :] = pick(col_even, 0.0, spilled)


def final_kernel(rows, cols, g_ref, m_ref, row_in, col_in, total_ref, out_ref):
    n_rows, n_cols = lax.axis_size("rows"), lax.axis_size("cols")
    half_scale = 0.5 * ((rows * cols * n_rows * n_cols) / total_ref[0:1, 0:1])
    out_ref[...] = 0.5 * m_ref[...] + half_scale * g_ref[0:rows, 0:cols]
    out_ref[0:8, :] = out_ref[0:8, :] + half_scale * row_in[...]
    beside = jnp.concatenate([col_in[...], jnp.zeros((120, col_in.shape[1]), F32)], axis=0)
    out_ref[:, 0:128] = out_ref[:, 0:128] + half_scale * unflipped(beside, rows)


def exchange_columns(outs):
    came = [xor_permute(part, "cols", len(outs) - i) for i, part in enumerate(outs) if i > 0]
    return [outs[0]] + came


def exchange_rows(pieces, kinds, cap, extra=None):
    step = kinds * cap
    first = [piece[step : 2 * step] for piece in pieces]
    second = [piece[2 * step : 3 * step] for piece in pieces]
    if extra is not None:
        first, second = first + [extra], second + [extra]
    return swap_both(jnp.concatenate(first), jnp.concatenate(second), "rows")


def body(terminal_value, density_start, start_cells, offsets, weights, dest_tiles, end_cells):
    rows, cols = terminal_value.shape
    n_rows, n_cols = lax.axis_size("rows"), lax.axis_size("cols")
    blocks = dest_tiles.shape[0]
    cap = blocks // 4
    chunks = 3 * n_cols
    wide, tall = cols + 128, rows + 2 * PAD
    flat = -(-tall // 128) * 128
    starts = start_cells.reshape(blocks, 128)
    wts = weights.reshape(blocks, 128)
    ends = end_cells.reshape(blocks, 128)
    arrays = (terminal_value, density_start, wts, starts, offsets, ends)
    *arrays, sa, sb = vmem_call(
        functools.partial(start_kernel, rows, len(arrays)),
        (
            *[shape(*x.shape, dtype=x.dtype) for x in arrays],
            shape(3 * EDGE, cols),
            shape(2 * EDGE, cols),
        ),
        len(arrays),
        [pltpu.SemaphoreType.DMA((len(arrays),))],
        hbm_in=range(len(arrays)),
    )(*arrays)
    terminal_value, density_start, wts, starts, offsets, ends = arrays
    ra, rb = swap_both(sa, sb, "rows")
    ue, me, ca, cb, total = vmem_call(
        functools.partial(start_mid_kernel, rows, cols),
        (
            shape(tall, wide),
            shape(tall, wide),
            shape(2 * EDGE, flat),
            shape(2 * EDGE, flat),
            shape(EDGE, 128),
        ),
        5,
    )(terminal_value, density_start, ra, rb, sa)
    ca, cb = swap_both(ca, cb, "cols")
    sweep_scratch = [pltpu.VMEM((wide // 128, tall, 128), F32)] * 2

    def sample_scratch(part_rows):
        return [
            pltpu.VMEM((2 * table_height(rows), cols // 2), BF16),
            pltpu.VMEM((2 * table_height(rows), cols // 2), BF16),
            pltpu.VMEM((table_height(rows), 128), F32),
            pltpu.VMEM((n_cols * part_rows + EDGE, 128), F32),
            pltpu.SMEM((blocks,), I32),
            pltpu.SMEM((blocks,), I32),
            pltpu.SMEM((chunks,), I32),
            pltpu.SMEM((blocks,), I32),
            pltpu.SemaphoreType.DMA(()),
        ]

    high_rows = table_height(rows)
    acc_shape = (2, 2 * high_rows, cols // 2)
    beside_shape = (rows + 8, 128)

    def part_rows_of(chunk_count):
        return 2 * cap * (chunk_count + 1)

    own_scratch = [
        pltpu.VMEM((part_rows_of(n_cols), 128), F32),
        pltpu.SMEM((n_cols * cap + 2 * GROUP,), I32),
    ]
    other_scratch = [
        pltpu.VMEM((part_rows_of(2 * n_cols), 128), F32),
        pltpu.VMEM(acc_shape, F32),
        pltpu.VMEM(beside_shape, F32),
        pltpu.SMEM((2 * n_cols * cap + 2 * GROUP,), I32),
    ]
    carried = (shape(*acc_shape), shape(*beside_shape))
    part_rows = 12 * cap + EDGE
    *outs, ue, me = vmem_call(
        functools.partial(first_kernel, rows, cols, blocks, cap, n_cols),
        tuple([shape(part_rows, 128)] * n_cols + [shape(tall, wide)] * 2),
        10,
        sweep_scratch + sample_scratch(part_rows),
        hbm_in=(9,),
    )(ue, me, ca, cb, total, starts, offsets, wts, ends, dest_tiles)
    pieces = exchange_columns(outs)
    total = sum(piece[part_rows - EDGE :] for piece in pieces)
    ra, rb = exchange_rows(pieces, 4, cap)
    bits = [1 << i for i in range(1, n_rows.bit_length() - 1)]
    more = xor_permute(total, "rows", bits[0])
    acc, beside, own_masses = vmem_call(
        functools.partial(own_deposit_kernel, rows, cols, cap, n_cols, True),
        (*carried, shape(part_rows_of(n_cols), 128)),
        n_cols,
        own_scratch,
    )(*pieces)
    grid, ea, eb, masses = vmem_call(
        functools.partial(first_deposit_kernel, rows, cols, cap, n_cols),
        (
            shape(rows + 8, wide),
            shape(8, wide),
            shape(8, wide),
            shape(part_rows_of(2 * n_cols), 128),
        ),
        4,
        other_scratch,
    )(ra, rb, acc, beside)
    ea, eb, more = lax.optimization_barrier((ea, eb, more))
    ea, eb = swap_both(ea, eb, "rows")
    for bit in bits[1:]:
        total = total + more
        more = xor_permute(total, "rows", bit)
    deposit, ca, cb = vmem_call(
        functools.partial(edge_mid_kernel, rows, cols),
        (shape(tall, wide), shape(2 * EDGE, flat), shape(2 * EDGE, flat)),
        3,
    )(grid, ea, eb)
    ca, cb = swap_both(ca, cb, "cols")
    part_rows = 6 * cap + EDGE
    *outs, value, density, total = vmem_call(
        functools.partial(again_kernel, rows, cols, blocks, cap, n_cols),
        tuple([shape(part_rows, 128)] * n_cols + [shape(rows, cols)] * 2 + [shape(EDGE, 128)]),
        12,
        sweep_scratch
        + [pltpu.VMEM((tall, wide), F32)]
        + sample_scratch(part_rows)
        + [pltpu.SemaphoreType.DMA((cols // 128,))],
        hbm_in=(11,),
        hbm_out=(n_cols,),
    )(ue, me, deposit, ca, cb, total, more, starts, offsets, wts, ends, dest_tiles)
    pieces = exchange_columns(outs)
    corner = sum(piece[part_rows - EDGE :] for piece in pieces)
    ra, rb = exchange_rows(pieces, 2, cap, corner)
    acc, beside = vmem_call(
        functools.partial(own_deposit_kernel, rows, cols, cap, n_cols, False),
        carried,
        n_cols + 1,
        own_scratch,
    )(*pieces, own_masses)
    grid, below, beside = vmem_call(
        functools.partial(last_deposit_kernel, rows, cols, cap, n_cols),
        (shape(rows + 8, wide), shape(8, cols), shape(8, rows)),
        6,
        other_scratch,
    )(ra, rb, acc, beside, masses, corner)
    below = lax.ppermute(below, "rows", [(i, i + 1) for i in range(n_rows - 1)])
    beside = lax.ppermute(beside, "cols", [(i, i + 1) for i in range(n_cols - 1)])
    (density,) = vmem_call(
        functools.partial(final_kernel, rows, cols), (shape(rows, cols),), 5, keep=(0,)
    )(grid, density, below, beside, total)
    return (value, density)


def solution(mesh):
    in_specs = (
        P("rows", "cols"),
        P("rows", "cols"),
        P(("rows", "cols")),
        P(None, ("rows", "cols")),
        P(("rows", "cols")),
        P(("rows", "cols")),
        P(("rows", "cols")),
    )
    out_specs = (P("rows", "cols"), P("rows", "cols"))
    return jax.shard_map(body, mesh=mesh, in_specs=in_specs, out_specs=out_specs, check_vma=False)
```

```python
import functools
import jax
import jax.numpy as jnp
from jax import lax
from jax.experimental import pallas as pl
from jax.experimental.pallas import tpu as pltpu
from jax.sharding import PartitionSpec as P

HJB_STEPS = 4
F32, BF16, I32 = jnp.float32, jnp.bfloat16, jnp.int32

PAD = 16
EDGE = 8
GROUP = 4
VMEM_LIMIT = 24 * 1024 * 1024


def swap_pairs(count):
    first = [(i, i ^ 1) for i in range(count)]
    second = [(i, ((i + 1) ^ 1) - 1) for i in range(1, count - 1)]
    return first, second


def swap_both(first, second, axis):
    pairs_a, pairs_b = swap_pairs(lax.axis_size(axis))
    return lax.ppermute(first, axis, pairs_a), lax.ppermute(second, axis, pairs_b)


def xor_permute(value, axis, bit):
    return lax.ppermute(value, axis, [(i, i ^ bit) for i in range(lax.axis_size(axis))])


def vmem_call(kernel, out_shape, n_in, scratch=(), hbm_in=(), hbm_out=(), keep=()):
    def spec(in_hbm):
        return pl.BlockSpec(memory_space=pltpu.HBM if in_hbm else pltpu.VMEM)

    results = [
        leaf if i in keep or i in hbm_out else pltpu.VMEM(leaf.shape, leaf.dtype)
        for i, leaf in enumerate(out_shape)
    ]
    call = pl.pallas_call(
        kernel,
        out_shape=results,
        in_specs=[spec(i in hbm_in) for i in range(n_in)],
        out_specs=[spec(i in hbm_out) for i in range(len(results))],
        scratch_shapes=list(scratch),
        compiler_params=pltpu.CompilerParams(vmem_limit_bytes=VMEM_LIMIT),
    )

    def run(*operands):
        return call(
            *[
                pltpu.with_memory_space_constraint(x, pltpu.HBM if i in hbm_in else pltpu.VMEM)
                for i, x in enumerate(operands)
            ]
        )

    return run


def shape(*dims, dtype=F32):
    return jax.ShapeDtypeStruct(dims, dtype)


def flipped(block):
    rows = block.shape[0]
    width = -(-rows // 128) * 128
    if width > rows:
        block = jnp.concatenate([block, jnp.zeros((width - rows, 128), F32)], axis=0)
    parts = [block[i : i + 128].T for i in range(0, width, 128)]
    return jnp.concatenate(parts, axis=1)


def unflipped(block, rows):
    parts = [block[:, i : i + 128].T for i in range(0, block.shape[1], 128)]
    return jnp.concatenate(parts, axis=0)[:rows]


def row_col(cell, cols):
    if cols & (cols - 1) == 0:
        return cell >> (cols.bit_length() - 1), cell & (cols - 1)
    return cell // cols, cell % cols


def pick(flag, one, other):
    return jnp.where(flag, one, other)


def start_kernel(rows, count, *refs):
    sources, copies = refs[:count], refs[count : 2 * count]
    sa_ref, sb_ref, sems = refs[2 * count :]
    moves = [
        pltpu.make_async_copy(src, dst, sems.at[i])
        for i, (src, dst) in enumerate(zip(sources, copies))
    ]
    for move in moves:
        move.start()
    for move in moves:
        move.wait()
    u_ref, m_ref, wts = copies[:3]
    row_even = lax.axis_index("rows") % 2 == 0
    for index, ref in enumerate((u_ref, m_ref)):
        part = slice(index * EDGE, (index + 1) * EDGE)
        south_going, north_going = ref[rows - EDGE : rows, :], ref[0:EDGE, :]
        sa_ref[part, :] = pick(row_even, south_going, north_going)
        sb_ref[part, :] = pick(row_even, north_going, south_going)
    total = jnp.sum(jnp.sum(wts[...], axis=0, keepdims=True), axis=1, keepdims=True)
    sa_ref[2 * EDGE :, :] = jnp.broadcast_to(total, (EDGE, sa_ref.shape[1]))


def start_mid_kernel(
    rows, cols, u_ref, m_ref, a_ref, b_ref, s_ref, ue_ref, me_ref, ca_ref, cb_ref, sum_ref
):
    sum_ref[...] = s_ref[2 * EDGE :, 0:128] + a_ref[2 * EDGE :, 0:128]
    row_even = lax.axis_index("rows") % 2 == 0
    col_even = lax.axis_index("cols") % 2 == 0
    for index, (src, dst) in enumerate(((u_ref, ue_ref), (m_ref, me_ref))):
        dst[...] = jnp.zeros(dst.shape, F32)
        dst[PAD : PAD + rows, 0:cols] = src[...]
        part = slice(index * EDGE, (index + 1) * EDGE)
        north = pick(row_even, b_ref[part, :], a_ref[part, :])
        south = pick(row_even, a_ref[part, :], b_ref[part, :])
        dst[PAD - EDGE : PAD, 0:cols] = north
        dst[PAD + rows : PAD + rows + EDGE, 0:cols] = south
        west_going = flipped(dst[:, 0:128])[0:EDGE]
        east_going = flipped(dst[:, cols - 128 : cols])[128 - EDGE : 128]
        ca_ref[part, :] = pick(col_even, east_going, west_going)
        cb_ref[part, :] = pick(col_even, west_going, east_going)


def side_tile(left, right, width):
    return jnp.concatenate([right, jnp.zeros((128 - 2 * EDGE, width), F32), left], axis=0)


def hjb_sweep(rows, cols, ua, ub, m, between):
    wide = cols + 128
    tiles = wide // 128
    n_rows, n_cols = lax.axis_size("rows"), lax.axis_size("cols")
    sub = lax.broadcasted_iota(I32, (8, 128), 0)
    lane = lax.broadcasted_iota(I32, (8, 128), 1)
    first, last = lane == 0, lane == 127
    row_first = lax.axis_index("rows") * rows
    col = jnp.where(lane < 64, cols + lane, lane - 128) + lax.axis_index("cols") * cols
    side_ok = (col >= 0) & (col < cols * n_cols)
    src, dst = ua, ub

    for step in range(HJB_STEPS):
        if step == HJB_STEPS // 2:
            between()
        for i in range(PAD - 8, PAD + rows + 8, 8):
            row_ok = None
            if i < PAD or i >= PAD + rows:
                row = sub + (row_first + (i - PAD))
                row_ok = (row >= 0) & (row < rows * n_rows)
            here = [src[t, i : i + 8, :] for t in range(tiles)]
            went = [pltpu.roll(x, 1, 1) for x in here]
            came = [pltpu.roll(x, 127, 1) for x in here]
            for t in range(tiles):
                value = here[t]
                up, down = src[t, i - 1 : i + 7, :], src[t, i + 1 : i + 9, :]
                left = jnp.where(first, went[t - 1], went[t])
                right = jnp.where(last, came[(t + 1) % tiles], came[t])
                slope_x = jnp.maximum(value - jnp.minimum(up, down), 0.0)
                slope_y = jnp.maximum(value - jnp.minimum(left, right), 0.0)
                around = (up + down) + (left + right) + m[i : i + 8, t * 128 : (t + 1) * 128]
                new = 0.5 * value + 0.125 * (around - (slope_x * slope_x + slope_y * slope_y))
                ok = row_ok
                if t == tiles - 1:
                    ok = side_ok if ok is None else ok & side_ok
                dst[t, i : i + 8, :] = new if ok is None else jnp.where(ok, new, 0.0)
        src, dst = dst, src
    return src


def split(value):
    high = value.astype(BF16)
    return high, (value - high.astype(F32)).astype(BF16)


def lane_pick(value, index):
    dims = lax.GatherDimensionNumbers(
        offset_dims=(),
        collapsed_slice_dims=(1,),
        start_index_map=(1,),
        operand_batching_dims=(0,),
        start_indices_batching_dims=(0,),
    )
    return lax.gather(
        value, index[..., None], dims, (1, 1), mode=lax.GatherScatterMode.PROMISE_IN_BOUNDS
    )


def table_height(rows):
    return rows + 16


def fill_tables(rows, cols, u, tabs, halo):
    high_rows = table_height(rows)
    lane = lax.broadcasted_iota(I32, (8, 128), 1)
    lower = lane < 64
    for i in range(0, high_rows, 16):
        for parity in range(2):
            index = (2 * lane + parity) & 127
            for t in range(cols // 256):
                halves = []
                for j in range(2):
                    at = PAD + i + 8 * j
                    one, two = u[2 * t, at : at + 8, :], u[2 * t + 1, at : at + 8, :]
                    halves.append(
                        jnp.where(lower, lane_pick(one, index), lane_pick(two, index))
                    )
                high, low = split(jnp.concatenate(halves, axis=0))
                tabs[parity][i : i + 16, t * 128 : (t + 1) * 128] = high
                tabs[parity][high_rows + i : high_rows + i + 16, t * 128 : (t + 1) * 128] = low
        halo[i : i + 16, :] = jnp.broadcast_to(
            u[cols // 128, PAD + i : PAD + i + 16, 0:1], (16, 128)
        )


def fill_slots(blocks, cap, first, dest, slot_row, corner_row, counter):
    n_cols = lax.axis_size("cols")
    my_row, my_col = lax.axis_index("rows"), lax.axis_index("cols")
    n_rows = lax.axis_size("rows")
    kinds = 4 if first else 2
    part_rows = 3 * kinds * cap + EDGE
    spare_row = n_cols * part_rows
    for i in range(3 * n_cols):
        counter[i] = 0
    for b in range(blocks):
        tile = dest[b]
        band, column = tile // n_cols, tile % n_cols
        section = jnp.where(band == my_row, 0, jnp.where(band == (my_row ^ 1), 1, 2))
        distance = column ^ my_col
        rank = counter[distance * 3 + section]
        counter[distance * 3 + section] = rank + 1
        slot_row[b] = distance * part_rows + section * (kinds * cap) + rank
        if not first:
            goes = (band < n_rows - 1) & (column < n_cols - 1)
            row = ((column + 1) ^ my_col) * part_rows + 3 * kinds * cap + section
            corner_row[b] = jnp.where(goes, row, spare_row)


def sample_moves(
    rows, cols, blocks, cap, first, tabs, halo, starts, offs, wts, ends, buf, slot_row, corner_row
):
    buf[...] = jnp.zeros(buf.shape, F32)
    high_rows = table_height(rows)
    sub16 = lax.broadcasted_iota(I32, (16, 256), 0)
    sub8 = lax.broadcasted_iota(I32, (8, 256), 0)
    one16, zero16 = jnp.ones((16, 256), BF16), jnp.zeros((16, 256), BF16)

    def step(j, carry):
        def pair(ref):
            return jnp.concatenate([ref[pl.ds(2 * j, 1), :], ref[pl.ds(2 * j + 1, 1), :]], axis=1)

        row, col = row_col(pair(starts), cols)
        lanes = pl.ds(pl.multiple_of(j * 256, 256), 256)
        off_x = offs[0:1, lanes]
        off_y = offs[1:2, lanes]
        odd = (col & 1) == 1
        line = []
        for tab, place in ((tabs[0], (col + 1) >> 1), (tabs[1], col >> 1)):
            at = (jnp.broadcast_to(place, (16, 256)) - sub16).astype(jnp.int16)
            hot = [jnp.where(at == 16 * i, one16, zero16) for i in range(cols // 32)]
            line.append(
                jnp.dot(tab[...], jnp.concatenate(hot, axis=0), preferred_element_type=F32)
            )
        frac_x = 0.5 + 0.45 * jnp.tanh(off_x)
        frac_y = 0.5 + 0.45 * jnp.tanh(off_y)
        blend = jnp.where(odd, 1.0 - frac_y, frac_y)
        edge = jnp.broadcast_to(col == cols - 1, (8, 256))
        row_at = jnp.broadcast_to(row, (8, 256)) - sub8
        near, far = jnp.broadcast_to(1.0 - frac_x, (8, 256)), jnp.broadcast_to(frac_x, (8, 256))
        sum_x, sum_y = jnp.zeros((8, 256), F32), jnp.zeros((8, 256), F32)
        for i in range(0, rows + 8, 8):
            even, odds = [
                both[i : i + 8] + both[high_rows + i : high_rows + i + 8] for both in line
            ]
            beyond = jnp.concatenate([halo[i : i + 8, :]] * 2, axis=1)
            even = jnp.where(edge, beyond, even)
            step_y = odds - even
            mixed = even + blend * step_y
            here, below = row_at == i, row_at == i - 1
            sum_x = sum_x + jnp.where(below, mixed, jnp.where(here, -mixed, 0.0))
            sum_y = sum_y + step_y * jnp.where(here, near, jnp.where(below, far, 0.0))
        grad_x = jnp.sum(sum_x, axis=0, keepdims=True)
        grad_y = jnp.sum(sum_y, axis=0, keepdims=True)
        grad_y = jnp.where(odd, -grad_y, grad_y)
        moved_x = 0.5 + 0.45 * jnp.tanh(off_x - grad_x)
        moved_y = 0.5 + 0.45 * jnp.tanh(off_y - grad_y)
        out = [moved_x, moved_y]
        if first:
            out += [pair(wts), (pair(ends) + 1).astype(F32)]
        else:
            corner = jnp.where(pair(ends) == rows * cols - 1, pair(wts) * moved_x * moved_y, 0.0)
        for half in range(2):
            if not first:
                buf[pl.ds(corner_row[2 * j + half], 1), :] += corner[:, half * 128 : (half + 1) * 128]
            base = slot_row[2 * j + half]
            for q, value in enumerate(out):
                buf[pl.ds(base + q * cap, 1), :] = value[:, half * 128 : (half + 1) * 128]
        return carry

    lax.fori_loop(0, blocks // 2, step, 0, unroll=True if first else 4)


def first_kernel(
    rows, cols, blocks, cap, n_cols, *refs
):
    (ue_in, me_in, ra_ref, rb_ref, w_ref, starts, offs, wts, ends, dest_hbm) = refs[:10]
    outs = refs[10 : 10 + n_cols]
    ue_ref, me_ref = refs[10 + n_cols : 12 + n_cols]
    ua, ub, tab_even, tab_odd, halo, buf, slot_row, corner_row, counter, dest, sem = refs[12 + n_cols :]
    fetch = pltpu.make_async_copy(dest_hbm, dest, sem)
    fetch.start()
    col_even = lax.axis_index("cols") % 2 == 0
    tall = ue_in.shape[0]
    width = ra_ref.shape[1]
    for index, (src, dst) in enumerate(((ue_in, ue_ref), (me_in, me_ref))):
        part = slice(index * EDGE, (index + 1) * EDGE)
        west = pick(col_even, rb_ref[part, :], ra_ref[part, :])
        east = pick(col_even, ra_ref[part, :], rb_ref[part, :])
        dst[:, 0:cols] = src[:, 0:cols]
        dst[:, cols : cols + 128] = unflipped(side_tile(west, east, width), tall)
    for t in range(cols // 128 + 1):
        ua[t] = ue_ref[:, t * 128 : (t + 1) * 128]
    ub[...] = jnp.zeros(ub.shape, F32)

    def place_blocks():
        fetch.wait()
        fill_slots(blocks, cap, True, dest, slot_row, corner_row, counter)

    u = hjb_sweep(rows, cols, ua, ub, me_ref, place_blocks)
    tabs = (tab_even, tab_odd)
    fill_tables(rows, cols, u, tabs, halo)
    sample_moves(
        rows, cols, blocks, cap, True, tabs, halo, starts, offs, wts, ends, buf, slot_row, corner_row
    )
    part_rows = 12 * cap + EDGE
    for k in range(n_cols):
        out = outs[(n_cols - k) % n_cols]
        out[0 : part_rows - EDGE, :] = buf[k * part_rows : (k + 1) * part_rows - EDGE, :]
        out[part_rows - EDGE :, :] = w_ref[...]


def again_kernel(rows, cols, blocks, cap, n_cols, *refs):
    (ue_ref, m_in, d_ref, ra_ref, rb_ref, total_in, more_in) = refs[:7]
    (starts, offs, wts, ends, dest_hbm) = refs[7:12]
    outs = refs[12 : 12 + n_cols]
    value_hbm, density_ref, total_ref = refs[12 + n_cols : 15 + n_cols]
    (ua, ub, m, tab_even, tab_odd, halo, buf, slot_row, corner_row, counter, dest, sem, value_sems) = (
        refs[15 + n_cols :]
    )
    total_ref[...] = total_in[...] + more_in[...]
    fetch = pltpu.make_async_copy(dest_hbm, dest, sem)
    fetch.start()
    col_even = lax.axis_index("cols") % 2 == 0
    n_rows = lax.axis_size("rows")
    tall = ue_ref.shape[0]
    width = ra_ref.shape[1]
    half_scale = 0.5 * ((rows * cols * n_rows * n_cols) / total_ref[0:1, 0:1])
    west = pick(col_even, rb_ref[...], ra_ref[...])
    east = pick(col_even, ra_ref[...], rb_ref[...])
    side = unflipped(side_tile(west[0:EDGE], east[0:EDGE], width), tall)
    pushed = unflipped(
        jnp.concatenate([west[EDGE : 2 * EDGE], jnp.zeros((128 - EDGE, width), F32)], axis=0), tall
    )
    m[:, 0:128] = 0.5 * m_in[:, 0:128] + half_scale * (d_ref[:, 0:128] + pushed)
    m[:, 128:cols] = 0.5 * m_in[:, 128:cols] + half_scale * d_ref[:, 128:cols]
    m[:, cols : cols + 128] = 0.5 * m_in[:, cols : cols + 128] + half_scale * (
        d_ref[:, cols : cols + 128] + side
    )
    density_ref[...] = m[PAD : PAD + rows, 0:cols]
    for t in range(cols // 128 + 1):
        ua[t] = ue_ref[:, t * 128 : (t + 1) * 128]
    ub[...] = jnp.zeros(ub.shape, F32)

    def place_blocks():
        fetch.wait()
        fill_slots(blocks, cap, False, dest, slot_row, corner_row, counter)

    u = hjb_sweep(rows, cols, ua, ub, m, place_blocks)
    leaving = [
        pltpu.make_async_copy(
            u.at[t, PAD : PAD + rows, :],
            value_hbm.at[:, t * 128 : (t + 1) * 128],
            value_sems.at[t],
        )
        for t in range(cols // 128)
    ]
    for leave in leaving:
        leave.start()
    tabs = (tab_even, tab_odd)
    fill_tables(rows, cols, u, tabs, halo)
    sample_moves(
        rows, cols, blocks, cap, False, tabs, halo, starts, offs, wts, ends, buf, slot_row, corner_row
    )
    part_rows = 6 * cap + EDGE
    for k in range(n_cols):
        outs[(n_cols - k) % n_cols][...] = buf[k * part_rows : (k + 1) * part_rows, :]
    for leave in leaving:
        leave.wait()


def deposit_blocks(rows, cols, cap, chunks, moves, masses, scratch, slots):
    acc, beside = scratch
    counts = []
    for q in range(chunks):
        cells = masses[(2 * q + 1) * cap : (2 * q + 2) * cap, :]
        counts.append(jnp.sum(jnp.where(cells > 0.5, 1.0, 0.0)).astype(I32) // 128)
    base = jnp.int32(0)
    for q in range(chunks):
        for rank in range(cap):
            slots[base + rank] = 2 * q * cap + rank
        base = base + counts[q]
    for rank in range(2 * GROUP):
        slots[base + rank] = 2 * chunks * cap
    high_rows = table_height(rows)
    sub16 = lax.broadcasted_iota(I32, (16, 128), 0)
    sub8 = lax.broadcasted_iota(I32, (8, 128), 0)
    one16, zero16 = jnp.ones((16, 128), BF16), jnp.zeros((16, 128), BF16)

    def relative(line, sub):
        return jnp.broadcast_to(line, sub.shape) - sub

    def build(first_slot):
        edges, left, right = [], ([], []), ([], [])
        for t in range(GROUP):
            at = slots[first_slot + t]
            move_x = moves[pl.ds(at, 1), :]
            move_y = moves[pl.ds(at + cap, 1), :]
            mass = masses[pl.ds(at, 1), :]
            row, col = row_col(masses[pl.ds(at + cap, 1), :].astype(I32) - 1, cols)
            odd = (col & 1) == 1
            stay, go = mass * (1.0 - move_x), mass * move_x
            row_at = relative(row, sub16).astype(jnp.int16)
            values = []
            for parity in range(2):
                share = jnp.where(odd == (parity == 1), 1.0 - move_y, move_y)
                first, second = stay * share, go * share
                if parity == 0:
                    edge_row = jnp.where(col == cols - 1, row, -2)
                    edges.append((relative(edge_row, sub8), first, second))
                for one, two in zip(split(first), split(second)):
                    values.append(
                        [jnp.broadcast_to(x.astype(F32), (16, 128)).astype(BF16) for x in (one, two)]
                    )
            tiles = [[], [], [], []]
            for i in range(high_rows // 16):
                here, below = row_at == 16 * i, row_at == 16 * i - 1
                for index, (one, two) in enumerate(values):
                    tiles[index].append(jnp.where(here, one, jnp.where(below, two, zero16)))
            for parity in range(2):
                left[parity].append(
                    jnp.concatenate(tiles[2 * parity] + tiles[2 * parity + 1], axis=0)
                )
            for parity, place in ((0, (col + 1) >> 1), (1, col >> 1)):
                place_at = relative(place, sub16).astype(jnp.int16)
                hot = [jnp.where(place_at == 16 * i, one16, zero16) for i in range(cols // 32)]
                right[parity].append(jnp.concatenate(hot, axis=0))
        for i in range(rows // 8 + 1):
            total = beside[8 * i : 8 * i + 8, :]
            for row_at, first, second in edges:
                total = total + jnp.where(
                    row_at == 8 * i, first, jnp.where(row_at == 8 * i - 1, second, 0.0)
                )
            beside[8 * i : 8 * i + 8, :] = total
        for parity in range(2):
            acc[parity] += lax.dot_general(
                jnp.concatenate(left[parity], axis=1),
                jnp.concatenate(right[parity], axis=1),
                (((1,), (1,)), ((), ())),
                preferred_element_type=F32,
            )

    def step(g, carry):
        for part in range(2):
            build((2 * g + part) * GROUP)
        return carry

    def double_step(g, carry):
        return step(2 * g + 1, step(2 * g, carry))

    steps = (base + 2 * GROUP - 1) // (2 * GROUP)
    lax.fori_loop(0, steps // 2, double_step, 0)
    lax.fori_loop(steps - steps % 2, steps, step, 0)


def finish_grid(rows, cols, acc, beside, grid):
    high_rows = table_height(rows)
    wide = cols + 128
    lane = lax.broadcasted_iota(I32, (8, wide), 1)
    lane1 = lax.broadcasted_iota(I32, (8, 128), 1)
    odd_lane = (lane1 & 1) == 1
    half = lane1 >> 1

    def weave(i, even, odd):
        for t in range(cols // 128):
            index = half + 64 * (t % 2)
            at = slice((t // 2) * 128, (t // 2 + 1) * 128)
            grid[i : i + 8, t * 128 : (t + 1) * 128] = jnp.where(
                odd_lane, lane_pick(odd[:, at], index), lane_pick(even[:, at], index)
            )
        right = jnp.sum(beside[i : i + 8, :], axis=1, keepdims=True)
        grid[i : i + 8, cols:wide] = jnp.where(lane1 == 0, right, 0.0)

    for i in range(0, rows + 8, 8):
        weave(
            i,
            *[acc[p, i : i + 8, :] + acc[p, high_rows + i : high_rows + i + 8, :] for p in range(2)],
        )

    @pl.when(lax.axis_index("rows") == lax.axis_size("rows") - 1)
    def _():
        tail = grid[rows - 8 : rows, :]
        sub8 = lax.broadcasted_iota(I32, (8, wide), 0)
        spill_row = jnp.broadcast_to(grid[rows : rows + 1, :], (8, wide))
        grid[rows - 8 : rows, :] = tail + jnp.where(sub8 == 7, spill_row, 0.0)
        grid[rows : rows + 8, :] = jnp.zeros((8, wide), F32)

    @pl.when(lax.axis_index("cols") == lax.axis_size("cols") - 1)
    def _():
        for i in range(0, rows + 8, 8):
            line = grid[i : i + 8, :]
            moved = jnp.where(lane == cols - 1, pltpu.roll(line, wide - 1, 1), 0.0)
            grid[i : i + 8, :] = jnp.where(lane < cols, line + moved, 0.0)


def own_deposit_kernel(rows, cols, cap, n_cols, first, *refs):
    pieces, refs = refs[:n_cols], refs[n_cols:]
    if first:
        acc_out, beside_out, masses, moves, *scratch, slots = refs
    else:
        masses, acc_out, beside_out, moves, *scratch, slots = refs
    size = 2 * cap
    for k in range(n_cols):
        moves[k * size : (k + 1) * size, :] = pieces[k][0:size, :]
        if first:
            masses[k * size : (k + 1) * size, :] = pieces[k][size : 2 * size, :]
    for ref in (moves, masses) if first else (moves,):
        ref[n_cols * size :, :] = jnp.zeros((size, 128), F32)
    acc_out[...] = jnp.zeros(acc_out.shape, F32)
    beside_out[...] = jnp.zeros(beside_out.shape, F32)
    deposit_blocks(
        rows, cols, cap, n_cols, moves, masses, (acc_out, beside_out, *scratch), slots
    )


def other_deposit(rows, cols, cap, n_cols, first, came, acc_in, beside_in, masses, grid, scratch):
    moves, acc, beside, *rest, slots = scratch
    size = 2 * cap
    step = 2 * size if first else size
    for index, ref in enumerate(came):
        for k in range(n_cols):
            at = (index * n_cols + k) * size
            moves[at : at + size, :] = ref[k * step : k * step + size, :]
            if first:
                masses[at : at + size, :] = ref[k * step + size : (k + 1) * step, :]
    for ref in (moves, masses) if first else (moves,):
        ref[2 * n_cols * size :, :] = jnp.zeros((size, 128), F32)
    acc[...] = acc_in[...]
    beside[...] = beside_in[...]
    deposit_blocks(
        rows, cols, cap, 2 * n_cols, moves, masses, (acc, beside, *rest), slots
    )
    finish_grid(rows, cols, acc, beside, grid)


def first_deposit_kernel(rows, cols, cap, n_cols, *refs):
    ra_ref, rb_ref, acc_in, beside_in = refs[:4]
    grid, sa_ref, sb_ref, masses = refs[4:8]
    other_deposit(
        rows, cols, cap, n_cols, True, (ra_ref, rb_ref), acc_in, beside_in, masses, grid, refs[8:]
    )
    row_even = lax.axis_index("rows") % 2 == 0
    south_going = grid[rows - 7 : rows + 1, :]
    north_going = grid[0:8, :]
    sa_ref[...] = pick(row_even, south_going, north_going)
    sb_ref[...] = pick(row_even, north_going, south_going)


def last_deposit_kernel(rows, cols, cap, n_cols, *refs):
    ra_ref, rb_ref, acc_in, beside_in, masses, corner_ref = refs[:6]
    grid, row_ref, col_ref = refs[6:9]
    other_deposit(
        rows, cols, cap, n_cols, False, (ra_ref, rb_ref), acc_in, beside_in, masses, grid, refs[9:]
    )
    tail = 2 * cap * n_cols
    corner = corner_ref[0:1, :] + ra_ref[tail + 1 : tail + 2, :] + rb_ref[tail + 2 : tail + 3, :]
    corner = jnp.sum(corner, axis=1, keepdims=True)
    place = lax.broadcasted_iota(I32, (8, 128), 0) + lax.broadcasted_iota(I32, (8, 128), 1)
    row_ref[...] = grid[rows : rows + 8, 0:cols]
    row_ref[:, 0:128] = row_ref[:, 0:128] + jnp.where(place == 0, corner, 0.0)
    col_ref[...] = flipped(grid[0:rows, cols : cols + 128])[0:8]


def edge_mid_kernel(rows, cols, g_ref, a_ref, b_ref, d_ref, ca_ref, cb_ref):
    row_even = lax.axis_index("rows") % 2 == 0
    col_even = lax.axis_index("cols") % 2 == 0
    wide = cols + 128
    north = pick(row_even, b_ref[...], a_ref[...])
    south = pick(row_even, a_ref[...], b_ref[...])
    d_ref[0:PAD, :] = jnp.zeros((PAD, wide), F32)
    d_ref[PAD : PAD + rows, :] = g_ref[0:rows, :]
    d_ref[PAD + rows : PAD + rows + 8, :] = south + g_ref[rows : rows + 8, :]
    d_ref[PAD + rows + 8 :, :] = jnp.zeros((d_ref.shape[0] - PAD - rows - 8, wide), F32)
    d_ref[PAD - 7 : PAD + 1, :] = d_ref[PAD - 7 : PAD + 1, :] + north
    west_going = flipped(d_ref[:, 0:128])[0:EDGE]
    east_going = flipped(d_ref[:, cols - 128 : cols])[128 - EDGE : 128]
    spilled = flipped(d_ref[:, cols : cols + 128])[0:EDGE]
    ca_ref[0:EDGE, :] = pick(col_even, east_going, west_going)
    cb_ref[0:EDGE, :] = pick(col_even, west_going, east_going)
    ca_ref[EDGE:, :] = pick(col_even, spilled, 0.0)
    cb_ref[EDGE:, :] = pick(col_even, 0.0, spilled)


def final_kernel(rows, cols, g_ref, m_ref, row_in, col_in, total_ref, out_ref):
    n_rows, n_cols = lax.axis_size("rows"), lax.axis_size("cols")
    half_scale = 0.5 * ((rows * cols * n_rows * n_cols) / total_ref[0:1, 0:1])
    out_ref[...] = 0.5 * m_ref[...] + half_scale * g_ref[0:rows, 0:cols]
    out_ref[0:8, :] = out_ref[0:8, :] + half_scale * row_in[...]
    beside = jnp.concatenate([col_in[...], jnp.zeros((120, col_in.shape[1]), F32)], axis=0)
    out_ref[:, 0:128] = out_ref[:, 0:128] + half_scale * unflipped(beside, rows)


def exchange_columns(outs):
    came = [xor_permute(part, "cols", len(outs) - i) for i, part in enumerate(outs) if i > 0]
    return [outs[0]] + came


def exchange_rows(pieces, kinds, cap, extra=None):
    step = kinds * cap
    first = [piece[step : 2 * step] for piece in pieces]
    second = [piece[2 * step : 3 * step] for piece in pieces]
    if extra is not None:
        first, second = first + [extra], second + [extra]
    return swap_both(jnp.concatenate(first), jnp.concatenate(second), "rows")


def body(terminal_value, density_start, start_cells, offsets, weights, dest_tiles, end_cells):
    rows, cols = terminal_value.shape
    n_rows, n_cols = lax.axis_size("rows"), lax.axis_size("cols")
    blocks = dest_tiles.shape[0]
    cap = blocks // 4
    chunks = 3 * n_cols
    wide, tall = cols + 128, rows + 2 * PAD
    flat = -(-tall // 128) * 128
    starts = start_cells.reshape(blocks, 128)
    wts = weights.reshape(blocks, 128)
    ends = end_cells.reshape(blocks, 128)
    arrays = (terminal_value, density_start, wts, starts, offsets, ends)
    *arrays, sa, sb = vmem_call(
        functools.partial(start_kernel, rows, len(arrays)),
        (
            *[shape(*x.shape, dtype=x.dtype) for x in arrays],
            shape(3 * EDGE, cols),
            shape(2 * EDGE, cols),
        ),
        len(arrays),
        [pltpu.SemaphoreType.DMA((len(arrays),))],
        hbm_in=range(len(arrays)),
    )(*arrays)
    terminal_value, density_start, wts, starts, offsets, ends = arrays
    ra, rb = swap_both(sa, sb, "rows")
    ue, me, ca, cb, total = vmem_call(
        functools.partial(start_mid_kernel, rows, cols),
        (
            shape(tall, wide),
            shape(tall, wide),
            shape(2 * EDGE, flat),
            shape(2 * EDGE, flat),
            shape(EDGE, 128),
        ),
        5,
    )(terminal_value, density_start, ra, rb, sa)
    ca, cb = swap_both(ca, cb, "cols")
    sweep_scratch = [pltpu.VMEM((wide // 128, tall, 128), F32)] * 2

    def sample_scratch(part_rows):
        return [
            pltpu.VMEM((2 * table_height(rows), cols // 2), BF16),
            pltpu.VMEM((2 * table_height(rows), cols // 2), BF16),
            pltpu.VMEM((table_height(rows), 128), F32),
            pltpu.VMEM((n_cols * part_rows + EDGE, 128), F32),
            pltpu.SMEM((blocks,), I32),
            pltpu.SMEM((blocks,), I32),
            pltpu.SMEM((chunks,), I32),
            pltpu.SMEM((blocks,), I32),
            pltpu.SemaphoreType.DMA(()),
        ]

    high_rows = table_height(rows)
    acc_shape = (2, 2 * high_rows, cols // 2)
    beside_shape = (rows + 8, 128)

    def part_rows_of(chunk_count):
        return 2 * cap * (chunk_count + 1)

    own_scratch = [
        pltpu.VMEM((part_rows_of(n_cols), 128), F32),
        pltpu.SMEM((n_cols * cap + 2 * GROUP,), I32),
    ]
    other_scratch = [
        pltpu.VMEM((part_rows_of(2 * n_cols), 128), F32),
        pltpu.VMEM(acc_shape, F32),
        pltpu.VMEM(beside_shape, F32),
        pltpu.SMEM((2 * n_cols * cap + 2 * GROUP,), I32),
    ]
    carried = (shape(*acc_shape), shape(*beside_shape))
    part_rows = 12 * cap + EDGE
    *outs, ue, me = vmem_call(
        functools.partial(first_kernel, rows, cols, blocks, cap, n_cols),
        tuple([shape(part_rows, 128)] * n_cols + [shape(tall, wide)] * 2),
        10,
        sweep_scratch + sample_scratch(part_rows),
        hbm_in=(9,),
    )(ue, me, ca, cb, total, starts, offsets, wts, ends, dest_tiles)
    pieces = exchange_columns(outs)
    total = sum(piece[part_rows - EDGE :] for piece in pieces)
    ra, rb = exchange_rows(pieces, 4, cap)
    bits = [1 << i for i in range(1, n_rows.bit_length() - 1)]
    more = xor_permute(total, "rows", bits[0])
    acc, beside, own_masses = vmem_call(
        functools.partial(own_deposit_kernel, rows, cols, cap, n_cols, True),
        (*carried, shape(part_rows_of(n_cols), 128)),
        n_cols,
        own_scratch,
    )(*pieces)
    grid, ea, eb, masses = vmem_call(
        functools.partial(first_deposit_kernel, rows, cols, cap, n_cols),
        (
            shape(rows + 8, wide),
            shape(8, wide),
            shape(8, wide),
            shape(part_rows_of(2 * n_cols), 128),
        ),
        4,
        other_scratch,
    )(ra, rb, acc, beside)
    ea, eb, more = lax.optimization_barrier((ea, eb, more))
    ea, eb = swap_both(ea, eb, "rows")
    for bit in bits[1:]:
        total = total + more
        more = xor_permute(total, "rows", bit)
    deposit, ca, cb = vmem_call(
        functools.partial(edge_mid_kernel, rows, cols),
        (shape(tall, wide), shape(2 * EDGE, flat), shape(2 * EDGE, flat)),
        3,
    )(grid, ea, eb)
    ca, cb = swap_both(ca, cb, "cols")
    part_rows = 6 * cap + EDGE
    *outs, value, density, total = vmem_call(
        functools.partial(again_kernel, rows, cols, blocks, cap, n_cols),
        tuple([shape(part_rows, 128)] * n_cols + [shape(rows, cols)] * 2 + [shape(EDGE, 128)]),
        12,
        sweep_scratch
        + [pltpu.VMEM((tall, wide), F32)]
        + sample_scratch(part_rows)
        + [pltpu.SemaphoreType.DMA((cols // 128,))],
        hbm_in=(11,),
        hbm_out=(n_cols,),
    )(ue, me, deposit, ca, cb, total, more, starts, offsets, wts, ends, dest_tiles)
    pieces = exchange_columns(outs)
    corner = sum(piece[part_rows - EDGE :] for piece in pieces)
    ra, rb = exchange_rows(pieces, 2, cap, corner)
    acc, beside = vmem_call(
        functools.partial(own_deposit_kernel, rows, cols, cap, n_cols, False),
        carried,
        n_cols + 1,
        own_scratch,
    )(*pieces, own_masses)
    grid, below, beside = vmem_call(
        functools.partial(last_deposit_kernel, rows, cols, cap, n_cols),
        (shape(rows + 8, wide), shape(8, cols), shape(8, rows)),
        6,
        other_scratch,
    )(ra, rb, acc, beside, masses, corner)
    below = lax.ppermute(below, "rows", [(i, i + 1) for i in range(n_rows - 1)])
    beside = lax.ppermute(beside, "cols", [(i, i + 1) for i in range(n_cols - 1)])
    (density,) = vmem_call(
        functools.partial(final_kernel, rows, cols), (shape(rows, cols),), 5, keep=(0,)
    )(grid, density, below, beside, total)
    return (value, density)


def solution(mesh):
    in_specs = (
        P("rows", "cols"),
        P("rows", "cols"),
        P(("rows", "cols")),
        P(None, ("rows", "cols")),
        P(("rows", "cols")),
        P(("rows", "cols")),
        P(("rows", "cols")),
    )
    out_specs = (P("rows", "cols"), P("rows", "cols"))
    return jax.shard_map(body, mesh=mesh, in_specs=in_specs, out_specs=out_specs, check_vma=False)
```
